128 devices in a mesh: section: 2 (over core), seq: 4 (over x), dp: 16 (over z, y).
Axes of the slice: x: 4, y: 4, z: 4, core: 2. Of those that a mesh axis runs over, the one named last changes fastest.
Arguments:
- section_input: bfloat16 [2, 16, 512, 4096], P('section', 'dp', 'seq'), may hold values from -6 to 6
- saved_qkv: bfloat16 [2, 16, 512, 3, 2048], P('section', 'dp', None, None, 'seq'), may hold values from -14 to 14
- modulation: float32 [2, 16, 2, 4096], P('section', 'dp'), may hold values from -4 to 4
- w_qkv: bfloat16 [2, 4096, 3, 2048], P('section', 'dp', None, 'seq'), may hold values from -0.09375 to 0.09375
- w_out: bfloat16 [2, 2048, 4096], P('section', 'seq'), may hold values from -0.125 to 0.125
- lengths: int32 [16], P('dp'), may hold values from 1 to 512, 5120 in all
- student_out: bfloat16 [16, 512, 4096], P('dp', 'seq'), may hold values from -6 to 6
- teacher_target: bfloat16 [16, 512, 4096], P('dp', 'seq'), may hold values from -6 to 6
Outputs:
- grad_input: bfloat16 [2, 16, 512, 4096], P('section', 'dp', 'seq')
- grad_out: bfloat16 [2, 2048, 4096], P('section', 'seq', 'dp')
The draws below stay inside these ranges and needn't reach their ends.
Inputs may be any that keep to these rules, and one draw needn't show every extreme that they name: `lengths`: at least one micro-batch is 512 tokens long.
All inputs are finite; a program needn't handle non-finite values. No bound on the sum of `lengths` on one device may be relied on, other than what follows from the above.
Results may differ from the reference program's by a relative error of at most 0.014.
Values may be sent and summed in bfloat16 or wider, within the bound.
A program may use at most 192 MiB of HBM per device.

```python
import math
import jax
import jax.numpy as jnp
import numpy as np
from jax import lax

D = 4096
HEAD_DIM = 128
HW = 2048
CAP = 512
SECTIONS = 2
BATCH = 16


def draw_saved_qkv(key, part):
    key_main = jax.random.fold_in(key, 11)
    full_shape = (SECTIONS, BATCH, CAP, 3, HW)
    values = jnp.clip(jax.random.normal(key_main, full_shape, jnp.float32), -5.0, 5.0)
    return values.astype(jnp.bfloat16)


def block_levels(stream_key, shape, cuts, least, largest):
    gain = 1.0
    for axis_at, blocks in cuts:
        heights = jax.random.uniform(jax.random.fold_in(jax.random.fold_in(stream_key, 6), axis_at), (blocks,), jnp.float32, least / len(cuts), largest / len(cuts))
        gain = gain * jnp.repeat(jnp.exp(heights), shape[axis_at] // blocks).reshape((-1,) + (1,) * (len(shape) - 1 - axis_at))
    return gain


def profile(count, total, bound, skew):
    weights = [(1 << 20) // math.isqrt(standing ** skew) + 1 for standing in range(2, count + 1)]
    surplus, given = total - bound - (count - 1), [1] * (count - 1)
    while surplus > 0:
        movable = [i for i in range(count - 1) if given[i] < bound]
        whole, budget = sum([weights[i] for i in movable]), surplus
        for i in movable:
            addition = min(bound - given[i], max(1, budget * weights[i] // whole), surplus)
            given[i] = given[i] + addition
            surplus = surplus - addition
    return np.array([bound] + given)


def ragged_sizes(rng, number_of, total, reach, slope):
    if number_of == 2:
        one = jax.random.randint(rng, (), max(1, total - reach), min(reach, total - 1) + 1)
        return jnp.stack([one, total - one])
    sizes = jnp.asarray(profile(number_of, total, reach, slope), jnp.int32)
    pairs = (number_of - 1) // 2
    giver, sink = sizes[1:1 + 2 * pairs:2], sizes[2:2 + 2 * pairs:2]
    room = jnp.minimum(giver - 1, reach - sink)
    shifted = jax.random.randint(jax.random.fold_in(rng, 1), (pairs,), 0, 1 << 20) % (room + 1)
    sizes = sizes.at[1:1 + 2 * pairs:2].set(giver - shifted).at[2:2 + 2 * pairs:2].set(sink + shifted)
    return sizes[jax.random.permutation(jax.random.fold_in(rng, 2), number_of)]


def centred(stream_key, dims, width, most, split=(), kind=jnp.bfloat16):
    factor_of = block_levels(stream_key, dims, split, -0.22, 0.18) if split else 1.0
    drawn = jax.random.normal(stream_key, dims, jnp.float32) * width * factor_of
    return jnp.minimum(jnp.maximum(drawn, -most), most).astype(kind)


def setup_inputs(seed: int = 0) -> dict:
    key_of = jax.random.split(jax.random.key(seed), 9)
    return {
        "section_input": centred(key_of[0], (SECTIONS, BATCH, CAP, D), 1.0, 6.0, ((0, 2), (1, 16), (2, 4))),
        "saved_qkv": draw_saved_qkv(jax.random.fold_in(key_of[8], 71), 0),
        "modulation": centred(key_of[2], (SECTIONS, BATCH, 2, D), 0.7, 4.0, ((0, 2), (1, 16)), jnp.float32),
        "w_qkv": centred(key_of[3], (SECTIONS, D, 3, HW), D ** -0.5, 0.09375, ((0, 2), (1, 16), (3, 4))),
        "w_out": centred(key_of[4], (SECTIONS, HW, D), HW ** -0.5, 0.125, ((0, 2), (1, 4))),
        "lengths": ragged_sizes(key_of[5], BATCH, BATCH * CAP * 5 // 8, CAP, 1).astype(jnp.int32),
        "student_out": centred(key_of[6], (BATCH, CAP, D), 1.0, 6.0, ((0, 16), (1, 4))),
        "teacher_target": centred(key_of[7], (BATCH, CAP, D), 1.0, 6.0, ((0, 16), (1, 4))),
    }


def widen(tensor):
    return lax.optimization_barrier(tensor).astype(jnp.float32)

def layer_norm_parts(tokens):
    values = tokens.astype(jnp.float32)
    center = values - lax.optimization_barrier(jnp.mean(values, axis=-1, keepdims=True))
    variance = lax.optimization_barrier(jnp.mean(center * center, axis=-1, keepdims=True))
    inverse = lax.rsqrt(variance + 1e-06)
    return (center * inverse, inverse)

def attend_backward(saved_rows, d_attn, live_keys, head_size):
    row_total = saved_rows.shape[0]
    feature_width = saved_rows.shape[2]
    head_count = feature_width // head_size
    queries = saved_rows[:, 0].reshape(row_total, head_count, head_size).astype(jnp.float32)
    key_rows = saved_rows[:, 1].reshape(row_total, head_count, head_size).astype(jnp.float32)
    value_rows = saved_rows[:, 2].reshape(row_total, head_count, head_size).astype(jnp.float32)
    factor = 1.0 / math.sqrt(head_size)
    scores = jnp.einsum('qhd,khd->hqk', queries, key_rows) * factor
    scores = jnp.where(live_keys[None, None, :], scores, -1e+30)
    peak_score = lax.optimization_barrier(jnp.max(scores, axis=-1, keepdims=True))
    weights = jnp.exp(scores - peak_score)
    weights = weights / lax.optimization_barrier(jnp.sum(weights, axis=-1, keepdims=True))
    rounded = widen(weights.astype(jnp.bfloat16))
    attn_mixed = jnp.einsum('hqk,khd->qhd', rounded, value_rows).astype(jnp.bfloat16)
    upstream = d_attn.reshape(row_total, head_count, head_size).astype(jnp.float32)
    d_weights = jnp.einsum('qhd,khd->hqk', upstream, value_rows)
    delta_rows = jnp.einsum('qhd,qhd->hq', upstream, widen(attn_mixed))
    d_scores = widen((weights * (d_weights - delta_rows[:, :, None]) * factor).astype(jnp.bfloat16))
    grad_q = jnp.einsum('hqk,khd->qhd', d_scores, key_rows).astype(jnp.bfloat16)
    grad_k = jnp.einsum('hqk,qhd->khd', d_scores, queries).astype(jnp.bfloat16)
    grad_v = jnp.einsum('hqk,qhd->khd', rounded, upstream).astype(jnp.bfloat16)
    stacked = jnp.stack([grad_q, grad_k, grad_v], axis=1).reshape(row_total, 3, feature_width)
    return (attn_mixed.reshape(row_total, feature_width), stacked)

def reference(section_input, saved_qkv, modulation, w_qkv, w_out, lengths, student_out, teacher_target):
    section_total = section_input.shape[0]
    batch_total = section_input.shape[1]
    capacity = section_input.shape[2]
    model_width = section_input.shape[3]
    attn_width = saved_qkv.shape[4]
    key_positions = jnp.arange(capacity, dtype=jnp.int32)
    grad_rows = [[None] * batch_total for section_pos in range(section_total)]
    out_grads = [jnp.zeros((attn_width, model_width), jnp.float32) for section_pos in range(section_total)]
    for batch_row in range(batch_total):
        live_keys = key_positions < lengths[batch_row]
        gap = student_out[batch_row].astype(jnp.float32) - teacher_target[batch_row].astype(jnp.float32)
        d_output = jnp.where(live_keys[:, None], gap, 0.0).astype(jnp.bfloat16)
        for section_pos in reversed(range(section_total)):
            normed, inverse = layer_norm_parts(section_input[section_pos, batch_row])
            scale_term = modulation[section_pos, batch_row, 0]
            gate_term = modulation[section_pos, batch_row, 1]
            d_branch = (gate_term * d_output.astype(jnp.float32)).astype(jnp.bfloat16)
            d_attn = jnp.dot(d_branch, w_out[section_pos].T, preferred_element_type=jnp.float32).astype(jnp.bfloat16)
            attn_mixed, d_saved = attend_backward(saved_qkv[section_pos, batch_row], d_attn, live_keys, HEAD_DIM)
            flat_grads = d_saved.reshape(capacity, 3 * attn_width)
            weight_flat = w_qkv[section_pos].reshape(model_width, 3 * attn_width)
            d_mod = jnp.dot(flat_grads, weight_flat.T, preferred_element_type=jnp.float32)
            d_norm = d_mod * (1.0 + scale_term)
            d_layer = inverse * (d_norm - lax.optimization_barrier(jnp.mean(d_norm, axis=-1, keepdims=True)) - normed * lax.optimization_barrier(jnp.mean(d_norm * normed, axis=-1, keepdims=True)))
            d_input = (d_output.astype(jnp.float32) + d_layer).astype(jnp.bfloat16)
            out_grads[section_pos] = out_grads[section_pos] + jnp.dot(attn_mixed.T, d_branch, preferred_element_type=jnp.float32)
            grad_rows[section_pos][batch_row] = d_input
            d_output = d_input
    grad_input = jnp.stack([jnp.stack(grad_rows[section_pos], axis=0) for section_pos in range(section_total)], axis=0)
    grad_out = jnp.stack(out_grads, axis=0).astype(jnp.bfloat16)
    return (grad_input, grad_out)
```

```python
import math

import jax
import jax.numpy as jnp
from jax import lax
from jax.sharding import PartitionSpec as P

HEAD_DIM = 128


def widen(tensor):
    return lax.optimization_barrier(tensor).astype(jnp.float32)


def layer_norm_parts(tokens):
    values = tokens.astype(jnp.float32)
    center = values - jnp.mean(values, axis=-1, keepdims=True)
    variance = jnp.mean(center * center, axis=-1, keepdims=True)
    inverse = lax.rsqrt(variance + 1e-06)
    return (center * inverse, inverse)


def attend_forward(saved_rows, live_keys, head_size):
    row_total = saved_rows.shape[0]
    feature_width = saved_rows.shape[2]
    head_count = feature_width // head_size
    queries = saved_rows[:, 0].reshape(row_total, head_count, head_size).astype(jnp.float32)
    key_rows = saved_rows[:, 1].reshape(row_total, head_count, head_size).astype(jnp.float32)
    value_rows = saved_rows[:, 2].reshape(row_total, head_count, head_size).astype(jnp.float32)
    factor = 1.0 / math.sqrt(head_size)
    scores = jnp.einsum("qhd,khd->hqk", queries, key_rows) * factor
    scores = jnp.where(live_keys[None, None, :], scores, -1e30)
    peak_score = jnp.max(scores, axis=-1, keepdims=True)
    weights = jnp.exp(scores - peak_score)
    weights = weights / jnp.sum(weights, axis=-1, keepdims=True)
    rounded = widen(weights.astype(jnp.bfloat16))
    attn_mixed = jnp.einsum("hqk,khd->qhd", rounded, value_rows).astype(jnp.bfloat16)
    return weights, rounded, attn_mixed


def attend_backward(saved_rows, fwd, d_attn, head_size):
    weights, rounded, attn_mixed = fwd
    row_total = saved_rows.shape[0]
    feature_width = saved_rows.shape[2]
    head_count = feature_width // head_size
    queries = saved_rows[:, 0].reshape(row_total, head_count, head_size).astype(jnp.float32)
    key_rows = saved_rows[:, 1].reshape(row_total, head_count, head_size).astype(jnp.float32)
    value_rows = saved_rows[:, 2].reshape(row_total, head_count, head_size).astype(jnp.float32)
    factor = 1.0 / math.sqrt(head_size)
    upstream = d_attn.reshape(row_total, head_count, head_size).astype(jnp.float32)
    d_weights = jnp.einsum("qhd,khd->hqk", upstream, value_rows)
    delta_rows = jnp.einsum("qhd,qhd->hq", upstream, widen(attn_mixed))
    d_scores = widen((weights * (d_weights - delta_rows[:, :, None]) * factor).astype(jnp.bfloat16))
    grad_q = jnp.einsum("hqk,khd->qhd", d_scores, key_rows).astype(jnp.bfloat16)
    grad_k = jnp.einsum("hqk,qhd->khd", d_scores, queries).astype(jnp.bfloat16)
    grad_v = jnp.einsum("hqk,qhd->khd", rounded, upstream).astype(jnp.bfloat16)
    stacked = jnp.stack([grad_q, grad_k, grad_v], axis=1).reshape(row_total, 3 * feature_width)
    return stacked


def body(section_input, saved_qkv, modulation, w_qkv, w_out, lengths, student_out, teacher_target):
    section_total = lax.axis_size("section")
    section_pos = lax.axis_index("section")
    seq_pos = lax.axis_index("seq")
    inputs = section_input[0, 0]
    saved_rows = saved_qkv[0, 0]
    mods = modulation[0, 0]
    weight_out = w_out[0]
    shard_rows, model_width = inputs.shape
    capacity = saved_rows.shape[0]
    local_width = saved_rows.shape[2]
    live_length = lengths[0]

    weight_flat = lax.all_gather(w_qkv[0], "dp", axis=0, tiled=True).reshape(
        model_width, 3 * local_width
    )
    normed, inverse = layer_norm_parts(inputs)
    positions = seq_pos * shard_rows + jnp.arange(shard_rows, dtype=jnp.int32)
    row_live = positions < live_length
    gap = student_out[0].astype(jnp.float32) - teacher_target[0].astype(jnp.float32)
    loss_grad = jnp.where(row_live[:, None], gap, 0.0).astype(jnp.bfloat16)
    live_keys = jnp.arange(capacity, dtype=jnp.int32) < live_length
    fwd = attend_forward(saved_rows, live_keys, HEAD_DIM)
    attn_mixed = fwd[2].reshape(capacity, local_width)
    scale_term = mods[0]
    gate_term = mods[1]

    def section_work(d_output):
        d_branch = (gate_term * d_output.astype(jnp.float32)).astype(jnp.bfloat16)
        branch_full = lax.all_gather(d_branch, "seq", axis=0, tiled=True)
        out_local = jnp.dot(attn_mixed.T, branch_full, preferred_element_type=jnp.float32)
        d_attn = jnp.dot(branch_full, weight_out.T, preferred_element_type=jnp.float32).astype(
            jnp.bfloat16
        )
        flat_grads = attend_backward(saved_rows, fwd, d_attn, HEAD_DIM)
        d_mod_part = jnp.dot(flat_grads, weight_flat.T, preferred_element_type=jnp.float32)
        d_mod = lax.psum_scatter(
            d_mod_part.astype(jnp.bfloat16), "seq", scatter_dimension=0, tiled=True
        ).astype(jnp.float32)
        d_norm = d_mod * (1.0 + scale_term)
        d_layer = inverse * (
            d_norm
            - jnp.mean(d_norm, axis=-1, keepdims=True)
            - normed * jnp.mean(d_norm * normed, axis=-1, keepdims=True)
        )
        d_input = (d_output.astype(jnp.float32) + d_layer).astype(jnp.bfloat16)
        return d_input, out_local

    incoming = loss_grad
    grad_input = None
    out_local = None
    for stage in reversed(range(section_total)):
        d_input, stage_out = section_work(incoming)
        here = section_pos == stage
        grad_input = d_input if grad_input is None else jnp.where(here, d_input, grad_input)
        out_local = stage_out if out_local is None else jnp.where(here, stage_out, out_local)
        if stage > 0:
            incoming = lax.ppermute(d_input, "section", [(stage, stage - 1)])
    out_slice = lax.psum_scatter(out_local, "dp", scatter_dimension=1, tiled=True)
    return (grad_input[None, None], out_slice.astype(jnp.bfloat16)[None])


def solution(mesh):
    in_specs = (
        P("section", "dp", "seq", None),
        P("section", "dp", None, None, "seq"),
        P("section", "dp", None, None),
        P("section", "dp", None, "seq"),
        P("section", "seq", None),
        P("dp"),
        P("dp", "seq", None),
        P("dp", "seq", None),
    )
    out_specs = (P("section", "dp", "seq", None), P("section", "seq", "dp"))
    return jax.shard_map(body, mesh=mesh, in_specs=in_specs, out_specs=out_specs, check_vma=False)
```

```python
import math

import jax
import jax.numpy as jnp
from jax import lax
from jax.sharding import PartitionSpec as P

HEAD_DIM = 128


def widen(tensor):
    return lax.optimization_barrier(tensor).astype(jnp.float32)


def layer_norm_parts(tokens):
    values = tokens.astype(jnp.float32)
    center = values - jnp.mean(values, axis=-1, keepdims=True)
    variance = jnp.mean(center * center, axis=-1, keepdims=True)
    inverse = lax.rsqrt(variance + 1e-06)
    return (center * inverse, inverse)


def attend_forward(saved_rows, live_keys, head_size):
    row_total = saved_rows.shape[0]
    feature_width = saved_rows.shape[2]
    head_count = feature_width // head_size
    queries = saved_rows[:, 0].reshape(row_total, head_count, head_size).astype(jnp.float32)
    key_rows = saved_rows[:, 1].reshape(row_total, head_count, head_size).astype(jnp.float32)
    value_rows = saved_rows[:, 2].reshape(row_total, head_count, head_size).astype(jnp.float32)
    factor = 1.0 / math.sqrt(head_size)
    scores = jnp.einsum("qhd,khd->hqk", queries, key_rows) * factor
    scores = jnp.where(live_keys[None, None, :], scores, -1e30)
    peak_score = jnp.max(scores, axis=-1, keepdims=True)
    weights = jnp.exp(scores - peak_score)
    weights = weights / jnp.sum(weights, axis=-1, keepdims=True)
    rounded = widen(weights.astype(jnp.bfloat16))
    attn_mixed = jnp.einsum("hqk,khd->qhd", rounded, value_rows).astype(jnp.bfloat16)
    return weights, rounded, attn_mixed


def attend_backward(saved_rows, fwd, d_attn, head_size):
    weights, rounded, attn_mixed = fwd
    row_total = saved_rows.shape[0]
    feature_width = saved_rows.shape[2]
    head_count = feature_width // head_size
    queries = saved_rows[:, 0].reshape(row_total, head_count, head_size).astype(jnp.float32)
    key_rows = saved_rows[:, 1].reshape(row_total, head_count, head_size).astype(jnp.float32)
    value_rows = saved_rows[:, 2].reshape(row_total, head_count, head_size).astype(jnp.float32)
    factor = 1.0 / math.sqrt(head_size)
    upstream = d_attn.reshape(row_total, head_count, head_size).astype(jnp.float32)
    d_weights = jnp.einsum("qhd,khd->hqk", upstream, value_rows)
    delta_rows = jnp.einsum("qhd,qhd->hq", upstream, widen(attn_mixed))
    d_scores = widen((weights * (d_weights - delta_rows[:, :, None]) * factor).astype(jnp.bfloat16))
    grad_q = jnp.einsum("hqk,khd->qhd", d_scores, key_rows).astype(jnp.bfloat16)
    grad_k = jnp.einsum("hqk,qhd->khd", d_scores, queries).astype(jnp.bfloat16)
    grad_v = jnp.einsum("hqk,qhd->khd", rounded, upstream).astype(jnp.bfloat16)
    stacked = jnp.stack([grad_q, grad_k, grad_v], axis=1).reshape(row_total, 3 * feature_width)
    return stacked


RING = ("section", "seq")


def shift_pairs(stage, count, step):
    base = stage * count
    return [(base + pos, base + (pos + step) % count) for pos in range(count)]


def gather_ring(shard, stage, count):
    half = shard.shape[0] // 2
    from_left = lax.ppermute(shard, RING, shift_pairs(stage, count, 1))
    from_right = lax.ppermute(shard, RING, shift_pairs(stage, count, -1))
    far_top = lax.ppermute(from_left[:half], RING, shift_pairs(stage, count, 1))
    far_bottom = lax.ppermute(from_right[half:], RING, shift_pairs(stage, count, -1))
    far = jnp.concatenate([far_top, far_bottom], axis=0)
    return jnp.concatenate([shard, from_right, far, from_left], axis=0)


def reduce_ring(partial, stage, count):
    rows = partial.shape[0] // count
    half = rows // 2
    blocks = [partial[k * rows : (k + 1) * rows] for k in range(count)]
    low = lambda value: value.astype(jnp.bfloat16)
    first_right = lax.ppermute(low(blocks[2][:half]), RING, shift_pairs(stage, count, 1))
    first_left = lax.ppermute(low(blocks[2][half:]), RING, shift_pairs(stage, count, -1))
    to_right = jnp.concatenate(
        [first_right.astype(jnp.float32) + blocks[1][:half], blocks[1][half:]], axis=0
    )
    to_left = jnp.concatenate(
        [blocks[3][:half], first_left.astype(jnp.float32) + blocks[3][half:]], axis=0
    )
    got_left = lax.ppermute(low(to_right), RING, shift_pairs(stage, count, 1))
    got_right = lax.ppermute(low(to_left), RING, shift_pairs(stage, count, -1))
    return blocks[0] + got_left.astype(jnp.float32) + got_right.astype(jnp.float32)


def body(section_input, saved_qkv, modulation, w_qkv, w_out, lengths, student_out, teacher_target):
    section_total = lax.axis_size("section")
    section_pos = lax.axis_index("section")
    seq_total = lax.axis_size("seq")
    seq_pos = lax.axis_index("seq")
    inputs = section_input[0, 0]
    saved_rows = saved_qkv[0, 0]
    mods = modulation[0, 0]
    weight_out = w_out[0]
    shard_rows, model_width = inputs.shape
    capacity = saved_rows.shape[0]
    local_width = saved_rows.shape[2]
    live_length = lengths[0]

    weight_flat = lax.all_gather(w_qkv[0], "dp", axis=0, tiled=True).reshape(
        model_width, 3 * local_width
    )
    normed, inverse = layer_norm_parts(inputs)
    positions = seq_pos * shard_rows + jnp.arange(shard_rows, dtype=jnp.int32)
    row_live = positions < live_length
    gap = student_out[0].astype(jnp.float32) - teacher_target[0].astype(jnp.float32)
    loss_grad = jnp.where(row_live[:, None], gap, 0.0).astype(jnp.bfloat16)
    order = (seq_pos + jnp.arange(seq_total, dtype=jnp.int32)) % seq_total
    token_order = (order[:, None] * shard_rows + jnp.arange(shard_rows, dtype=jnp.int32)).reshape(-1)
    saved_off = jnp.take(saved_rows, token_order, axis=0)
    live_keys = token_order < live_length
    fwd = attend_forward(saved_off, live_keys, HEAD_DIM)
    attn_mixed = fwd[2].reshape(capacity, local_width)
    scale_term = mods[0]
    gate_term = mods[1]

    def section_work(d_output, stage):
        d_branch = (gate_term * d_output.astype(jnp.float32)).astype(jnp.bfloat16)
        branch_full = gather_ring(d_branch, stage, seq_total)
        out_local = jnp.dot(attn_mixed.T, branch_full, preferred_element_type=jnp.float32)
        d_attn = jnp.dot(branch_full, weight_out.T, preferred_element_type=jnp.float32).astype(
            jnp.bfloat16
        )
        flat_grads = attend_backward(saved_off, fwd, d_attn, HEAD_DIM)
        d_mod_part = jnp.dot(flat_grads, weight_flat.T, preferred_element_type=jnp.float32)
        d_mod = reduce_ring(d_mod_part, stage, seq_total)
        d_norm = d_mod * (1.0 + scale_term)
        d_layer = inverse * (
            d_norm
            - jnp.mean(d_norm, axis=-1, keepdims=True)
            - normed * jnp.mean(d_norm * normed, axis=-1, keepdims=True)
        )
        d_input = (d_output.astype(jnp.float32) + d_layer).astype(jnp.bfloat16)
        return d_input, out_local

    incoming = loss_grad
    grad_input = None
    out_local = None
    for stage in reversed(range(section_total)):
        d_input, stage_out = section_work(incoming, stage)
        here = section_pos == stage
        grad_input = d_input if grad_input is None else jnp.where(here, d_input, grad_input)
        out_local = stage_out if out_local is None else jnp.where(here, stage_out, out_local)
        if stage > 0:
            incoming = lax.ppermute(d_input, "section", [(stage, stage - 1)])
    out_slice = lax.psum_scatter(out_local, "dp", scatter_dimension=1, tiled=True)
    return (grad_input[None, None], out_slice.astype(jnp.bfloat16)[None])


def solution(mesh):
    in_specs = (
        P("section", "dp", "seq", None),
        P("section", "dp", None, None, "seq"),
        P("section", "dp", None, None),
        P("section", "dp", None, "seq"),
        P("section", "seq", None),
        P("dp"),
        P("dp", "seq", None),
        P("dp", "seq", None),
    )
    out_specs = (P("section", "dp", "seq", None), P("section", "seq", "dp"))
    return jax.shard_map(body, mesh=mesh, in_specs=in_specs, out_specs=out_specs, check_vma=False)
```

```python
import math

import jax
import jax.numpy as jnp
from jax import lax
from jax.sharding import PartitionSpec as P

HEAD_DIM = 128


def widen(tensor):
    return lax.optimization_barrier(tensor).astype(jnp.float32)


def layer_norm_parts(tokens):
    values = tokens.astype(jnp.float32)
    center = values - jnp.mean(values, axis=-1, keepdims=True)
    variance = jnp.mean(center * center, axis=-1, keepdims=True)
    inverse = lax.rsqrt(variance + 1e-06)
    return (center * inverse, inverse)


def attend_forward(saved_rows, live_keys, head_size):
    row_total = saved_rows.shape[0]
    feature_width = saved_rows.shape[2]
    head_count = feature_width // head_size
    queries = saved_rows[:, 0].reshape(row_total, head_count, head_size).astype(jnp.float32)
    key_rows = saved_rows[:, 1].reshape(row_total, head_count, head_size).astype(jnp.float32)
    value_rows = saved_rows[:, 2].reshape(row_total, head_count, head_size).astype(jnp.float32)
    factor = 1.0 / math.sqrt(head_size)
    scores = jnp.einsum("qhd,khd->hqk", queries, key_rows) * factor
    scores = jnp.where(live_keys[None, None, :], scores, -1e30)
    peak_score = jnp.max(scores, axis=-1, keepdims=True)
    weights = jnp.exp(scores - peak_score)
    weights = weights / jnp.sum(weights, axis=-1, keepdims=True)
    rounded = widen(weights.astype(jnp.bfloat16))
    attn_mixed = jnp.einsum("hqk,khd->qhd", rounded, value_rows).astype(jnp.bfloat16)
    return weights, rounded, attn_mixed


def attend_backward(saved_rows, fwd, d_attn, head_size):
    weights, rounded, attn_mixed = fwd
    row_total = saved_rows.shape[0]
    feature_width = saved_rows.shape[2]
    head_count = feature_width // head_size
    queries = saved_rows[:, 0].reshape(row_total, head_count, head_size).astype(jnp.float32)
    key_rows = saved_rows[:, 1].reshape(row_total, head_count, head_size).astype(jnp.float32)
    value_rows = saved_rows[:, 2].reshape(row_total, head_count, head_size).astype(jnp.float32)
    factor = 1.0 / math.sqrt(head_size)
    upstream = d_attn.reshape(row_total, head_count, head_size).astype(jnp.float32)
    d_weights = jnp.einsum("qhd,khd->hqk", upstream, value_rows)
    delta_rows = jnp.einsum("qhd,qhd->hq", upstream, widen(attn_mixed))
    d_scores = widen((weights * (d_weights - delta_rows[:, :, None]) * factor).astype(jnp.bfloat16))
    grad_q = jnp.einsum("hqk,khd->qhd", d_scores, key_rows).astype(jnp.bfloat16)
    grad_k = jnp.einsum("hqk,qhd->khd", d_scores, queries).astype(jnp.bfloat16)
    grad_v = jnp.einsum("hqk,qhd->khd", rounded, upstream).astype(jnp.bfloat16)
    stacked = jnp.stack([grad_q, grad_k, grad_v], axis=1).reshape(row_total, 3 * feature_width)
    return stacked


RING = ("section", "seq")


def shift_pairs(stage, count, step):
    base = stage * count
    return [(base + pos, base + (pos + step) % count) for pos in range(count)]


def gather_ring(shard, stage, count):
    half = shard.shape[0] // 2
    from_left = lax.ppermute(shard, RING, shift_pairs(stage, count, 1))
    from_right = lax.ppermute(shard, RING, shift_pairs(stage, count, -1))
    far_top = lax.ppermute(from_left[:half], RING, shift_pairs(stage, count, 1))
    far_bottom = lax.ppermute(from_right[half:], RING, shift_pairs(stage, count, -1))
    far = jnp.concatenate([far_top, far_bottom], axis=0)
    return jnp.concatenate([shard, from_right, far, from_left], axis=0)


def reduce_ring(partial, stage, count):
    rows = partial.shape[0] // count
    half = rows // 2
    blocks = [partial[k * rows : (k + 1) * rows] for k in range(count)]
    low = lambda value: value.astype(jnp.bfloat16)
    first_right = lax.ppermute(low(blocks[2][:half]), RING, shift_pairs(stage, count, 1))
    first_left = lax.ppermute(low(blocks[2][half:]), RING, shift_pairs(stage, count, -1))
    to_right = jnp.concatenate(
        [first_right.astype(jnp.float32) + blocks[1][:half], blocks[1][half:]], axis=0
    )
    to_left = jnp.concatenate(
        [blocks[3][:half], first_left.astype(jnp.float32) + blocks[3][half:]], axis=0
    )
    got_left = lax.ppermute(low(to_right), RING, shift_pairs(stage, count, 1))
    got_right = lax.ppermute(low(to_left), RING, shift_pairs(stage, count, -1))
    return blocks[0] + got_left.astype(jnp.float32) + got_right.astype(jnp.float32)


DP_RING = ("section", "dp")


def grid_pairs(stage, rows, cols, step_row, step_col):
    base = stage * rows * cols
    return [
        (base + r * cols + c, base + ((r + step_row) % rows) * cols + (c + step_col) % cols)
        for r in range(rows)
        for c in range(cols)
    ]


def gather_on(shard, axes, pairs_of):
    half = shard.shape[0] // 2
    from_left = lax.ppermute(shard, axes, pairs_of(1))
    from_right = lax.ppermute(shard, axes, pairs_of(-1))
    far_top = lax.ppermute(from_left[:half], axes, pairs_of(1))
    far_bottom = lax.ppermute(from_right[half:], axes, pairs_of(-1))
    far = jnp.concatenate([far_top, far_bottom], axis=0)
    return jnp.concatenate([shard, from_right, far, from_left], axis=0)


def gather_grid(local, stage, rows, cols):
    half = local.shape[0] // 2
    along_z = lambda step: grid_pairs(stage, rows, cols, step, 0)
    along_y = lambda step: grid_pairs(stage, rows, cols, 0, step)
    first = gather_on(gather_on(local[:half], DP_RING, along_z), DP_RING, along_y)
    second = gather_on(gather_on(local[half:], DP_RING, along_y), DP_RING, along_z)
    return jnp.concatenate([first, second], axis=0)


def grid_order(z_pos, y_pos, rows, cols, block):
    half = block // 2
    z_new = jnp.arange(rows, dtype=jnp.int32)[:, None, None, None]
    y_new = jnp.arange(cols, dtype=jnp.int32)[None, :, None, None]
    part = jnp.arange(2, dtype=jnp.int32)[None, None, :, None]
    inner = jnp.arange(half, dtype=jnp.int32)[None, None, None, :]
    kz = (z_new - z_pos) % rows
    ky = (y_new - y_pos) % cols
    first = (ky * rows + kz) * half + inner
    second = rows * cols * half + (kz * cols + ky) * half + inner
    return jnp.where(part == 0, first, second).reshape(-1)


def body(section_input, saved_qkv, modulation, w_qkv, w_out, lengths, student_out, teacher_target):
    section_total = lax.axis_size("section")
    section_pos = lax.axis_index("section")
    seq_total = lax.axis_size("seq")
    seq_pos = lax.axis_index("seq")
    inputs = section_input[0, 0]
    saved_rows = saved_qkv[0, 0]
    mods = modulation[0, 0]
    weight_out = w_out[0]
    shard_rows, model_width = inputs.shape
    capacity = saved_rows.shape[0]
    local_width = saved_rows.shape[2]
    live_length = lengths[0]

    dp_pos = lax.axis_index("dp")
    grid_rows = 4
    grid_cols = lax.axis_size("dp") // grid_rows
    z_pos = dp_pos // grid_cols
    y_pos = dp_pos % grid_cols
    w_local = w_qkv[0]
    block_rows = w_local.shape[0]
    weights_of = {}
    last = section_total - 1
    weights_of[last] = gather_grid(w_local, last, grid_rows, grid_cols)
    for stage in reversed(range(last)):
        token = lax.ppermute(weights_of[stage + 1][:8], "section", [(stage + 1, stage)])
        w_after, _ = lax.optimization_barrier((w_local, token))
        weights_of[stage] = gather_grid(w_after, stage, grid_rows, grid_cols)
    feature_order = grid_order(z_pos, y_pos, grid_rows, grid_cols, block_rows)
    normed, inverse = layer_norm_parts(inputs)
    positions = seq_pos * shard_rows + jnp.arange(shard_rows, dtype=jnp.int32)
    row_live = positions < live_length
    gap = student_out[0].astype(jnp.float32) - teacher_target[0].astype(jnp.float32)
    loss_grad = jnp.where(row_live[:, None], gap, 0.0).astype(jnp.bfloat16)
    order = (seq_pos + jnp.arange(seq_total, dtype=jnp.int32)) % seq_total
    token_order = (order[:, None] * shard_rows + jnp.arange(shard_rows, dtype=jnp.int32)).reshape(-1)
    saved_off = jnp.take(saved_rows, token_order, axis=0)
    live_keys = token_order < live_length
    fwd = attend_forward(saved_off, live_keys, HEAD_DIM)
    attn_mixed = fwd[2].reshape(capacity, local_width)
    scale_term = mods[0]
    gate_term = mods[1]

    def section_work(d_output, stage):
        d_branch = (gate_term * d_output.astype(jnp.float32)).astype(jnp.bfloat16)
        branch_full = gather_ring(d_branch, stage, seq_total)
        out_local = jnp.dot(attn_mixed.T, branch_full, preferred_element_type=jnp.float32)
        d_attn = jnp.dot(branch_full, weight_out.T, preferred_element_type=jnp.float32).astype(
            jnp.bfloat16
        )
        flat_grads = attend_backward(saved_off, fwd, d_attn, HEAD_DIM)
        weight_flat = weights_of[stage].reshape(model_width, 3 * local_width)
        d_mod_part = jnp.dot(flat_grads, weight_flat.T, preferred_element_type=jnp.float32)
        d_mod_off = reduce_ring(d_mod_part, stage, seq_total)
        chunk = block_rows // 2
        d_mod = jnp.take(
            d_mod_off.reshape(shard_rows, model_width // chunk, chunk),
            feature_order.reshape(-1, chunk)[:, 0] // chunk,
            axis=1,
        ).reshape(shard_rows, model_width)
        d_norm = d_mod * (1.0 + scale_term)
        d_layer = inverse * (
            d_norm
            - jnp.mean(d_norm, axis=-1, keepdims=True)
            - normed * jnp.mean(d_norm * normed, axis=-1, keepdims=True)
        )
        d_input = (d_output.astype(jnp.float32) + d_layer).astype(jnp.bfloat16)
        return d_input, out_local

    incoming = loss_grad
    grad_input = None
    out_local = None
    for stage in reversed(range(section_total)):
        d_input, stage_out = section_work(incoming, stage)
        here = section_pos == stage
        grad_input = d_input if grad_input is None else jnp.where(here, d_input, grad_input)
        out_local = stage_out if out_local is None else jnp.where(here, stage_out, out_local)
        if stage > 0:
            incoming = lax.ppermute(d_input, "section", [(stage, stage - 1)])
    out_slice = lax.psum_scatter(out_local, "dp", scatter_dimension=1, tiled=True)
    return (grad_input[None, None], out_slice.astype(jnp.bfloat16)[None])


def solution(mesh):
    in_specs = (
        P("section", "dp", "seq", None),
        P("section", "dp", None, None, "seq"),
        P("section", "dp", None, None),
        P("section", "dp", None, "seq"),
        P("section", "seq", None),
        P("dp"),
        P("dp", "seq", None),
        P("dp", "seq", None),
    )
    out_specs = (P("section", "dp", "seq", None), P("section", "seq", "dp"))
    return jax.shard_map(body, mesh=mesh, in_specs=in_specs, out_specs=out_specs, check_vma=False)
```

```python
import functools
import math

import jax
import jax.numpy as jnp
from jax import lax
from jax.experimental import pallas as pl
from jax.experimental.pallas import tpu as pltpu
from jax.sharding import PartitionSpec as P

HEAD_DIM = 128


def widen(tensor):
    return lax.optimization_barrier(tensor).astype(jnp.float32)


def layer_norm_parts(tokens):
    values = tokens.astype(jnp.float32)
    center = values - jnp.mean(values, axis=-1, keepdims=True)
    variance = jnp.mean(center * center, axis=-1, keepdims=True)
    inverse = lax.rsqrt(variance + 1e-06)
    return (center * inverse, inverse)


def attend_forward(saved_rows, live_keys, head_size):
    row_total = saved_rows.shape[0]
    feature_width = saved_rows.shape[2]
    head_count = feature_width // head_size
    queries = saved_rows[:, 0].reshape(row_total, head_count, head_size).astype(jnp.float32)
    key_rows = saved_rows[:, 1].reshape(row_total, head_count, head_size).astype(jnp.float32)
    value_rows = saved_rows[:, 2].reshape(row_total, head_count, head_size).astype(jnp.float32)
    factor = 1.0 / math.sqrt(head_size)
    scores = jnp.einsum("qhd,khd->hqk", queries, key_rows) * factor
    scores = jnp.where(live_keys[None, None, :], scores, -1e30)
    peak_score = jnp.max(scores, axis=-1, keepdims=True)
    weights = jnp.exp(scores - peak_score)
    weights = weights / jnp.sum(weights, axis=-1, keepdims=True)
    rounded = widen(weights.astype(jnp.bfloat16))
    attn_mixed = jnp.einsum("hqk,khd->qhd", rounded, value_rows).astype(jnp.bfloat16)
    return weights, rounded, attn_mixed


def attend_backward(saved_rows, fwd, d_attn, head_size):
    weights, rounded, attn_mixed = fwd
    row_total = saved_rows.shape[0]
    feature_width = saved_rows.shape[2]
    head_count = feature_width // head_size
    queries = saved_rows[:, 0].reshape(row_total, head_count, head_size).astype(jnp.float32)
    key_rows = saved_rows[:, 1].reshape(row_total, head_count, head_size).astype(jnp.float32)
    value_rows = saved_rows[:, 2].reshape(row_total, head_count, head_size).astype(jnp.float32)
    factor = 1.0 / math.sqrt(head_size)
    upstream = d_attn.reshape(row_total, head_count, head_size).astype(jnp.float32)
    d_weights = jnp.einsum("qhd,khd->hqk", upstream, value_rows)
    delta_rows = jnp.einsum("qhd,qhd->hq", upstream, widen(attn_mixed))
    d_scores = widen((weights * (d_weights - delta_rows[:, :, None]) * factor).astype(jnp.bfloat16))
    grad_q = jnp.einsum("hqk,khd->qhd", d_scores, key_rows).astype(jnp.bfloat16)
    grad_k = jnp.einsum("hqk,qhd->khd", d_scores, queries).astype(jnp.bfloat16)
    grad_v = jnp.einsum("hqk,qhd->khd", rounded, upstream).astype(jnp.bfloat16)
    stacked = jnp.stack([grad_q, grad_k, grad_v], axis=1).reshape(row_total, 3 * feature_width)
    return stacked


RING = ("section", "seq")


def shift_pairs(stage, count, step):
    base = stage * count
    return [(base + pos, base + (pos + step) % count) for pos in range(count)]


def gather_ring(shard, stage, count):
    half = shard.shape[0] // 2
    from_left = lax.ppermute(shard, RING, shift_pairs(stage, count, 1))
    from_right = lax.ppermute(shard, RING, shift_pairs(stage, count, -1))
    far_top = lax.ppermute(from_left[:half], RING, shift_pairs(stage, count, 1))
    far_bottom = lax.ppermute(from_right[half:], RING, shift_pairs(stage, count, -1))
    far = jnp.concatenate([far_top, far_bottom], axis=0)
    return jnp.concatenate([shard, from_right, far, from_left], axis=0)


MESH_ID = pl.DeviceIdType.MESH


def ring_gather_kernel(stage, count, x_ref, o_ref, send_sem, recv_sem, own_sem):
    rows = x_ref.shape[0]
    half = rows // 2
    pos = lax.axis_index("seq")
    dp_pos = lax.axis_index("dp")

    @pl.when(lax.axis_index("section") == stage)
    def _():
        right = lax.rem(pos + 1, count)
        left = lax.rem(pos + count - 1, count)
        barrier = pltpu.get_barrier_semaphore()
        for neighbour in (left, right):
            pl.semaphore_signal(
                barrier, inc=1, device_id=(stage, neighbour, dp_pos), device_id_type=MESH_ID
            )
        pl.semaphore_wait(barrier, 2)
        own = pltpu.make_async_copy(x_ref, o_ref.at[pl.ds(0, rows)], own_sem)
        own.start()

        def remote(src, dst, slot, target):
            return pltpu.make_async_remote_copy(
                src_ref=src,
                dst_ref=dst,
                send_sem=send_sem.at[slot],
                recv_sem=recv_sem.at[slot],
                device_id=(stage, target, dp_pos),
                device_id_type=MESH_ID,
            )

        to_right = remote(x_ref, o_ref.at[pl.ds(3 * rows, rows)], 0, right)
        to_left = remote(x_ref, o_ref.at[pl.ds(rows, rows)], 1, left)
        to_right.start()
        to_left.start()
        to_right.wait()
        to_left.wait()
        relay_right = remote(
            o_ref.at[pl.ds(3 * rows, half)], o_ref.at[pl.ds(2 * rows, half)], 2, right
        )
        relay_left = remote(
            o_ref.at[pl.ds(rows + half, half)], o_ref.at[pl.ds(2 * rows + half, half)], 3, left
        )
        relay_right.start()
        relay_left.start()
        relay_right.wait()
        relay_left.wait()
        own.wait()


def ring_gather(shard, stage, count):
    rows, width = shard.shape
    return pl.pallas_call(
        functools.partial(ring_gather_kernel, stage, count),
        out_shape=jax.ShapeDtypeStruct((count * rows, width), shard.dtype),
        in_specs=[pl.BlockSpec(memory_space=pl.ANY)],
        out_specs=pl.BlockSpec(memory_space=pl.ANY),
        scratch_shapes=[
            pltpu.SemaphoreType.DMA((4,)),
            pltpu.SemaphoreType.DMA((4,)),
            pltpu.SemaphoreType.DMA(()),
        ],
        compiler_params=pltpu.CompilerParams(collective_id=stage, has_side_effects=True),
    )(shard)


def reduce_ring(partial, stage, count):
    rows = partial.shape[0] // count
    half = rows // 2
    blocks = [partial[k * rows : (k + 1) * rows] for k in range(count)]
    low = lambda value: value.astype(jnp.bfloat16)
    first_right = lax.ppermute(low(blocks[2][:half]), RING, shift_pairs(stage, count, 1))
    first_left = lax.ppermute(low(blocks[2][half:]), RING, shift_pairs(stage, count, -1))
    to_right = jnp.concatenate(
        [first_right.astype(jnp.float32) + blocks[1][:half], blocks[1][half:]], axis=0
    )
    to_left = jnp.concatenate(
        [blocks[3][:half], first_left.astype(jnp.float32) + blocks[3][half:]], axis=0
    )
    got_left = lax.ppermute(low(to_right), RING, shift_pairs(stage, count, 1))
    got_right = lax.ppermute(low(to_left), RING, shift_pairs(stage, count, -1))
    return blocks[0] + got_left.astype(jnp.float32) + got_right.astype(jnp.float32)


def body(section_input, saved_qkv, modulation, w_qkv, w_out, lengths, student_out, teacher_target):
    section_total = lax.axis_size("section")
    section_pos = lax.axis_index("section")
    seq_total = lax.axis_size("seq")
    seq_pos = lax.axis_index("seq")
    inputs = section_input[0, 0]
    saved_rows = saved_qkv[0, 0]
    mods = modulation[0, 0]
    weight_out = w_out[0]
    shard_rows, model_width = inputs.shape
    capacity = saved_rows.shape[0]
    local_width = saved_rows.shape[2]
    live_length = lengths[0]

    weight_flat = lax.all_gather(w_qkv[0], "dp", axis=0, tiled=True).reshape(
        model_width, 3 * local_width
    )
    normed, inverse = layer_norm_parts(inputs)
    positions = seq_pos * shard_rows + jnp.arange(shard_rows, dtype=jnp.int32)
    row_live = positions < live_length
    gap = student_out[0].astype(jnp.float32) - teacher_target[0].astype(jnp.float32)
    loss_grad = jnp.where(row_live[:, None], gap, 0.0).astype(jnp.bfloat16)
    order = (seq_pos + jnp.arange(seq_total, dtype=jnp.int32)) % seq_total
    token_order = (order[:, None] * shard_rows + jnp.arange(shard_rows, dtype=jnp.int32)).reshape(-1)
    saved_off = jnp.take(saved_rows, token_order, axis=0)
    live_keys = token_order < live_length
    fwd = attend_forward(saved_off, live_keys, HEAD_DIM)
    attn_mixed = fwd[2].reshape(capacity, local_width)
    scale_term = mods[0]
    gate_term = mods[1]

    def section_work(d_output, stage):
        d_branch = (gate_term * d_output.astype(jnp.float32)).astype(jnp.bfloat16)
        branch_full = ring_gather(d_branch, stage, seq_total)
        out_local = jnp.dot(attn_mixed.T, branch_full, preferred_element_type=jnp.float32)
        d_attn = jnp.dot(branch_full, weight_out.T, preferred_element_type=jnp.float32).astype(
            jnp.bfloat16
        )
        flat_grads = attend_backward(saved_off, fwd, d_attn, HEAD_DIM)
        d_mod_part = jnp.dot(flat_grads, weight_flat.T, preferred_element_type=jnp.float32)
        d_mod = reduce_ring(d_mod_part, stage, seq_total)
        d_norm = d_mod * (1.0 + scale_term)
        d_layer = inverse * (
            d_norm
            - jnp.mean(d_norm, axis=-1, keepdims=True)
            - normed * jnp.mean(d_norm * normed, axis=-1, keepdims=True)
        )
        d_input = (d_output.astype(jnp.float32) + d_layer).astype(jnp.bfloat16)
        return d_input, out_local

    incoming = loss_grad
    grad_input = None
    out_local = None
    for stage in reversed(range(section_total)):
        d_input, stage_out = section_work(incoming, stage)
        here = section_pos == stage
        grad_input = d_input if grad_input is None else jnp.where(here, d_input, grad_input)
        out_local = stage_out if out_local is None else jnp.where(here, stage_out, out_local)
        if stage > 0:
            incoming = lax.ppermute(d_input, "section", [(stage, stage - 1)])
    out_slice = lax.psum_scatter(out_local, "dp", scatter_dimension=1, tiled=True)
    return (grad_input[None, None], out_slice.astype(jnp.bfloat16)[None])


def solution(mesh):
    in_specs = (
        P("section", "dp", "seq", None),
        P("section", "dp", None, None, "seq"),
        P("section", "dp", None, None),
        P("section", "dp", None, "seq"),
        P("section", "seq", None),
        P("dp"),
        P("dp", "seq", None),
        P("dp", "seq", None),
    )
    out_specs = (P("section", "dp", "seq", None), P("section", "seq", "dp"))
    return jax.shard_map(body, mesh=mesh, in_specs=in_specs, out_specs=out_specs, check_vma=False)
```

```python
import functools
import math

import jax
import jax.numpy as jnp
from jax import lax
from jax.experimental import pallas as pl
from jax.experimental.pallas import tpu as pltpu
from jax.sharding import PartitionSpec as P

HEAD_DIM = 128


def widen(tensor):
    return lax.optimization_barrier(tensor).astype(jnp.float32)


def layer_norm_parts(tokens):
    values = tokens.astype(jnp.float32)
    center = values - jnp.mean(values, axis=-1, keepdims=True)
    variance = jnp.mean(center * center, axis=-1, keepdims=True)
    inverse = lax.rsqrt(variance + 1e-06)
    return (center * inverse, inverse)


def attend_forward(saved_rows, live_keys, head_size):
    row_total = saved_rows.shape[0]
    feature_width = saved_rows.shape[2]
    head_count = feature_width // head_size
    queries = saved_rows[:, 0].reshape(row_total, head_count, head_size).astype(jnp.float32)
    key_rows = saved_rows[:, 1].reshape(row_total, head_count, head_size).astype(jnp.float32)
    value_rows = saved_rows[:, 2].reshape(row_total, head_count, head_size).astype(jnp.float32)
    factor = 1.0 / math.sqrt(head_size)
    scores = jnp.einsum("qhd,khd->hqk", queries, key_rows) * factor
    scores = jnp.where(live_keys[None, None, :], scores, -1e30)
    peak_score = jnp.max(scores, axis=-1, keepdims=True)
    weights = jnp.exp(scores - peak_score)
    weights = weights / jnp.sum(weights, axis=-1, keepdims=True)
    rounded = widen(weights.astype(jnp.bfloat16))
    attn_mixed = jnp.einsum("hqk,khd->qhd", rounded, value_rows).astype(jnp.bfloat16)
    return weights, rounded, attn_mixed


def attend_backward(saved_rows, fwd, d_attn, head_size):
    weights, rounded, attn_mixed = fwd
    row_total = saved_rows.shape[0]
    feature_width = saved_rows.shape[2]
    head_count = feature_width // head_size
    queries = saved_rows[:, 0].reshape(row_total, head_count, head_size).astype(jnp.float32)
    key_rows = saved_rows[:, 1].reshape(row_total, head_count, head_size).astype(jnp.float32)
    value_rows = saved_rows[:, 2].reshape(row_total, head_count, head_size).astype(jnp.float32)
    factor = 1.0 / math.sqrt(head_size)
    upstream = d_attn.reshape(row_total, head_count, head_size).astype(jnp.float32)
    d_weights = jnp.einsum("qhd,khd->hqk", upstream, value_rows)
    delta_rows = jnp.einsum("qhd,qhd->hq", upstream, widen(attn_mixed))
    d_scores = widen((weights * (d_weights - delta_rows[:, :, None]) * factor).astype(jnp.bfloat16))
    grad_q = jnp.einsum("hqk,khd->qhd", d_scores, key_rows).astype(jnp.bfloat16)
    grad_k = jnp.einsum("hqk,qhd->khd", d_scores, queries).astype(jnp.bfloat16)
    grad_v = jnp.einsum("hqk,qhd->khd", rounded, upstream).astype(jnp.bfloat16)
    stacked = jnp.stack([grad_q, grad_k, grad_v], axis=1).reshape(row_total, 3 * feature_width)
    return stacked


RING = ("section", "seq")


def shift_pairs(stage, count, step):
    base = stage * count
    return [(base + pos, base + (pos + step) % count) for pos in range(count)]


def gather_ring(shard, stage, count):
    half = shard.shape[0] // 2
    from_left = lax.ppermute(shard, RING, shift_pairs(stage, count, 1))
    from_right = lax.ppermute(shard, RING, shift_pairs(stage, count, -1))
    far_top = lax.ppermute(from_left[:half], RING, shift_pairs(stage, count, 1))
    far_bottom = lax.ppermute(from_right[half:], RING, shift_pairs(stage, count, -1))
    far = jnp.concatenate([far_top, far_bottom], axis=0)
    return jnp.concatenate([shard, from_right, far, from_left], axis=0)


MESH_ID = pl.DeviceIdType.MESH


def ring_gather_kernel(stage, count, x_ref, o_ref, send_sem, recv_sem, own_sem):
    rows = x_ref.shape[0]
    half = rows // 2
    pos = lax.axis_index("seq")
    dp_pos = lax.axis_index("dp")

    @pl.when(lax.axis_index("section") == stage)
    def _():
        right = lax.rem(pos + 1, count)
        left = lax.rem(pos + count - 1, count)
        barrier = pltpu.get_barrier_semaphore()
        for neighbour in (left, right):
            pl.semaphore_signal(
                barrier, inc=1, device_id=(stage, neighbour, dp_pos), device_id_type=MESH_ID
            )
        pl.semaphore_wait(barrier, 2)
        own = pltpu.make_async_copy(x_ref, o_ref.at[pl.ds(0, rows)], own_sem)
        own.start()

        def remote(src, dst, slot, target):
            return pltpu.make_async_remote_copy(
                src_ref=src,
                dst_ref=dst,
                send_sem=send_sem.at[slot],
                recv_sem=recv_sem.at[slot],
                device_id=(stage, target, dp_pos),
                device_id_type=MESH_ID,
            )

        to_right = remote(x_ref, o_ref.at[pl.ds(3 * rows, rows)], 0, right)
        to_left = remote(x_ref, o_ref.at[pl.ds(rows, rows)], 1, left)
        to_right.start()
        to_left.start()
        to_right.wait()
        to_left.wait()
        relay_right = remote(
            o_ref.at[pl.ds(3 * rows, half)], o_ref.at[pl.ds(2 * rows, half)], 2, right
        )
        relay_left = remote(
            o_ref.at[pl.ds(rows + half, half)], o_ref.at[pl.ds(2 * rows + half, half)], 3, left
        )
        relay_right.start()
        relay_left.start()
        relay_right.wait()
        relay_left.wait()
        own.wait()


def ring_gather(shard, stage, count):
    rows, width = shard.shape
    return pl.pallas_call(
        functools.partial(ring_gather_kernel, stage, count),
        out_shape=jax.ShapeDtypeStruct((count * rows, width), shard.dtype),
        in_specs=[pl.BlockSpec(memory_space=pl.ANY)],
        out_specs=pl.BlockSpec(memory_space=pl.ANY),
        scratch_shapes=[
            pltpu.SemaphoreType.DMA((4,)),
            pltpu.SemaphoreType.DMA((4,)),
            pltpu.SemaphoreType.DMA(()),
        ],
        compiler_params=pltpu.CompilerParams(collective_id=stage, has_side_effects=True),
    )(shard)


def reduce_ring(partial, stage, count):
    rows = partial.shape[0] // count
    half = rows // 2
    blocks = [partial[k * rows : (k + 1) * rows] for k in range(count)]
    low = lambda value: value.astype(jnp.bfloat16)
    first_right = lax.ppermute(low(blocks[2][:half]), RING, shift_pairs(stage, count, 1))
    first_left = lax.ppermute(low(blocks[2][half:]), RING, shift_pairs(stage, count, -1))
    to_right = jnp.concatenate(
        [first_right.astype(jnp.float32) + blocks[1][:half], blocks[1][half:]], axis=0
    )
    to_left = jnp.concatenate(
        [blocks[3][:half], first_left.astype(jnp.float32) + blocks[3][half:]], axis=0
    )
    got_left = lax.ppermute(low(to_right), RING, shift_pairs(stage, count, 1))
    got_right = lax.ppermute(low(to_left), RING, shift_pairs(stage, count, -1))
    return blocks[0] + got_left.astype(jnp.float32) + got_right.astype(jnp.float32)


def swap(value):
    return lax.ppermute(value, "section", [(0, 1), (1, 0)])


def seq_pairs(count, step):
    return [(pos, (pos + step) % count) for pos in range(count)]


def reduce_seq(partial, count):
    rows = partial.shape[0] // count
    half = rows // 2
    blocks = [partial[k * rows : (k + 1) * rows] for k in range(count)]
    low = lambda value: value.astype(jnp.bfloat16)
    first_right = lax.ppermute(low(blocks[2][:half]), "seq", seq_pairs(count, 1))
    first_left = lax.ppermute(low(blocks[2][half:]), "seq", seq_pairs(count, -1))
    to_right = jnp.concatenate(
        [first_right.astype(jnp.float32) + blocks[1][:half], blocks[1][half:]], axis=0
    )
    to_left = jnp.concatenate(
        [blocks[3][:half], first_left.astype(jnp.float32) + blocks[3][half:]], axis=0
    )
    got_left = lax.ppermute(low(to_right), "seq", seq_pairs(count, 1))
    got_right = lax.ppermute(low(to_left), "seq", seq_pairs(count, -1))
    return blocks[0] + got_left.astype(jnp.float32) + got_right.astype(jnp.float32)


def body(section_input, saved_qkv, modulation, w_qkv, w_out, lengths, student_out, teacher_target):
    section_total = lax.axis_size("section")
    section_pos = lax.axis_index("section")
    seq_total = lax.axis_size("seq")
    seq_pos = lax.axis_index("seq")
    inputs = section_input[0, 0]
    saved_rows = saved_qkv[0, 0]
    weight_out = w_out[0]
    shard_rows, model_width = inputs.shape
    capacity = saved_rows.shape[0]
    local_width = saved_rows.shape[2]
    live_length = lengths[0]
    w_local = w_qkv[0]
    block_rows = w_local.shape[0]
    half_rows = block_rows // 2
    blocks_total = model_width // block_rows

    other_inputs = swap(inputs)
    other_mods = swap(modulation[0, 0])
    other_w = swap(w_local)
    parts = {}
    for stage in range(section_total):
        own = section_pos == stage
        x_stage = jnp.where(own, inputs, other_inputs)
        mods_stage = jnp.where(own, modulation[0, 0], other_mods)
        parts[stage] = (layer_norm_parts(x_stage), mods_stage)

    weights_of = {}
    for stage in reversed(range(section_total)):
        own = section_pos == stage
        contribution = jnp.where(own, w_local[:half_rows], other_w[half_rows:])
        weights_of[stage] = lax.all_gather(contribution, "dp", axis=0, tiled=True).reshape(
            blocks_total * half_rows, 3 * local_width
        )

    positions = seq_pos * shard_rows + jnp.arange(shard_rows, dtype=jnp.int32)
    row_live = positions < live_length
    gap = student_out[0].astype(jnp.float32) - teacher_target[0].astype(jnp.float32)
    loss_grad = jnp.where(row_live[:, None], gap, 0.0).astype(jnp.bfloat16)
    order = (seq_pos + jnp.arange(seq_total, dtype=jnp.int32)) % seq_total
    token_order = (order[:, None] * shard_rows + jnp.arange(shard_rows, dtype=jnp.int32)).reshape(-1)
    saved_off = jnp.take(saved_rows, token_order, axis=0)
    live_keys = token_order < live_length
    fwd = attend_forward(saved_off, live_keys, HEAD_DIM)
    attn_mixed = fwd[2].reshape(capacity, local_width)

    def pick_half(value, half_index):
        split = value.reshape(value.shape[0], blocks_total, 2, half_rows)
        return lax.dynamic_index_in_dim(split, half_index, 2, False).reshape(value.shape[0], -1)

    def section_work(d_output, stage):
        own = section_pos == stage
        half_index = jnp.where(own, 0, 1)
        (normed, inverse), mods_stage = parts[stage]
        scale_term = mods_stage[0]
        gate_term = mods_stage[1]
        d_branch = (gate_term * d_output.astype(jnp.float32)).astype(jnp.bfloat16)
        branch_full = ring_gather(d_branch, stage, seq_total)
        out_local = jnp.dot(attn_mixed.T, branch_full, preferred_element_type=jnp.float32)
        d_attn = jnp.dot(branch_full, weight_out.T, preferred_element_type=jnp.float32).astype(
            jnp.bfloat16
        )
        own_grads = attend_backward(saved_off, fwd, d_attn, HEAD_DIM)
        handed = lax.ppermute(own_grads, "section", [(stage, 1 - stage)])
        flat_grads = jnp.where(own, own_grads, handed)
        d_mod_part = jnp.dot(flat_grads, weights_of[stage].T, preferred_element_type=jnp.float32)
        d_mod = reduce_seq(d_mod_part, seq_total)
        normed_half = pick_half(normed, half_index)
        d_norm = d_mod * (1.0 + pick_half(scale_term[None], half_index))
        sums = jnp.stack([jnp.sum(d_norm, axis=-1), jnp.sum(d_norm * normed_half, axis=-1)])
        sums = (sums + swap(sums)) / model_width
        d_layer = inverse * (d_norm - sums[0][:, None] - normed_half * sums[1][:, None])
        d_half = (pick_half(d_output, half_index).astype(jnp.float32) + d_layer).astype(
            jnp.bfloat16
        )
        other_half = swap(d_half)
        split = lambda value: value.reshape(shard_rows, blocks_total, 1, half_rows)
        joined = jnp.where(
            own,
            jnp.concatenate([split(d_half), split(other_half)], axis=2),
            jnp.concatenate([split(other_half), split(d_half)], axis=2),
        )
        return joined.reshape(shard_rows, model_width), out_local

    incoming = loss_grad
    grad_input = None
    out_local = None
    for stage in reversed(range(section_total)):
        d_input, stage_out = section_work(incoming, stage)
        here = section_pos == stage
        grad_input = d_input if grad_input is None else jnp.where(here, d_input, grad_input)
        out_local = stage_out if out_local is None else jnp.where(here, stage_out, out_local)
        incoming = d_input
    out_slice = lax.psum_scatter(out_local, "dp", scatter_dimension=1, tiled=True)
    return (grad_input[None, None], out_slice.astype(jnp.bfloat16)[None])


def solution(mesh):
    in_specs = (
        P("section", "dp", "seq", None),
        P("section", "dp", None, None, "seq"),
        P("section", "dp", None, None),
        P("section", "dp", None, "seq"),
        P("section", "seq", None),
        P("dp"),
        P("dp", "seq", None),
        P("dp", "seq", None),
    )
    out_specs = (P("section", "dp", "seq", None), P("section", "seq", "dp"))
    return jax.shard_map(body, mesh=mesh, in_specs=in_specs, out_specs=out_specs, check_vma=False)
```

```python
import functools
import math

import jax
import jax.numpy as jnp
from jax import lax
from jax.experimental import pallas as pl
from jax.experimental.pallas import tpu as pltpu
from jax.sharding import PartitionSpec as P

HEAD_DIM = 128


def widen(tensor):
    return lax.optimization_barrier(tensor).astype(jnp.float32)


def layer_norm_parts(tokens):
    values = tokens.astype(jnp.float32)
    center = values - jnp.mean(values, axis=-1, keepdims=True)
    variance = jnp.mean(center * center, axis=-1, keepdims=True)
    inverse = lax.rsqrt(variance + 1e-06)
    return (center * inverse, inverse)


def attend_forward(saved_rows, live_keys, head_size):
    row_total = saved_rows.shape[0]
    feature_width = saved_rows.shape[2]
    head_count = feature_width // head_size
    queries = saved_rows[:, 0].reshape(row_total, head_count, head_size).astype(jnp.float32)
    key_rows = saved_rows[:, 1].reshape(row_total, head_count, head_size).astype(jnp.float32)
    value_rows = saved_rows[:, 2].reshape(row_total, head_count, head_size).astype(jnp.float32)
    factor = 1.0 / math.sqrt(head_size)
    scores = jnp.einsum("qhd,khd->hqk", queries, key_rows) * factor
    scores = jnp.where(live_keys[None, None, :], scores, -1e30)
    peak_score = jnp.max(scores, axis=-1, keepdims=True)
    weights = jnp.exp(scores - peak_score)
    weights = weights / jnp.sum(weights, axis=-1, keepdims=True)
    rounded = widen(weights.astype(jnp.bfloat16))
    attn_mixed = jnp.einsum("hqk,khd->qhd", rounded, value_rows).astype(jnp.bfloat16)
    return weights, rounded, attn_mixed


def attend_backward(saved_rows, fwd, d_attn, head_size):
    weights, rounded, attn_mixed = fwd
    row_total = saved_rows.shape[0]
    feature_width = saved_rows.shape[2]
    head_count = feature_width // head_size
    queries = saved_rows[:, 0].reshape(row_total, head_count, head_size).astype(jnp.float32)
    key_rows = saved_rows[:, 1].reshape(row_total, head_count, head_size).astype(jnp.float32)
    value_rows = saved_rows[:, 2].reshape(row_total, head_count, head_size).astype(jnp.float32)
    factor = 1.0 / math.sqrt(head_size)
    upstream = d_attn.reshape(row_total, head_count, head_size).astype(jnp.float32)
    d_weights = jnp.einsum("qhd,khd->hqk", upstream, value_rows)
    delta_rows = jnp.einsum("qhd,qhd->hq", upstream, widen(attn_mixed))
    d_scores = widen((weights * (d_weights - delta_rows[:, :, None]) * factor).astype(jnp.bfloat16))
    grad_q = jnp.einsum("hqk,khd->qhd", d_scores, key_rows).astype(jnp.bfloat16)
    grad_k = jnp.einsum("hqk,qhd->khd", d_scores, queries).astype(jnp.bfloat16)
    grad_v = jnp.einsum("hqk,qhd->khd", rounded, upstream).astype(jnp.bfloat16)
    stacked = jnp.stack([grad_q, grad_k, grad_v], axis=1).reshape(row_total, 3 * feature_width)
    return stacked


RING = ("section", "seq")


def shift_pairs(stage, count, step):
    base = stage * count
    return [(base + pos, base + (pos + step) % count) for pos in range(count)]


def gather_ring(shard, stage, count):
    half = shard.shape[0] // 2
    from_left = lax.ppermute(shard, RING, shift_pairs(stage, count, 1))
    from_right = lax.ppermute(shard, RING, shift_pairs(stage, count, -1))
    far_top = lax.ppermute(from_left[:half], RING, shift_pairs(stage, count, 1))
    far_bottom = lax.ppermute(from_right[half:], RING, shift_pairs(stage, count, -1))
    far = jnp.concatenate([far_top, far_bottom], axis=0)
    return jnp.concatenate([shard, from_right, far, from_left], axis=0)


MESH_ID = pl.DeviceIdType.MESH


def ring_gather_kernel(stage, count, x_ref, o_ref, send_sem, recv_sem, own_sem):
    rows = x_ref.shape[0]
    half = rows // 2
    pos = lax.axis_index("seq")
    dp_pos = lax.axis_index("dp")

    @pl.when(lax.axis_index("section") == stage)
    def _():
        right = lax.rem(pos + 1, count)
        left = lax.rem(pos + count - 1, count)
        barrier = pltpu.get_barrier_semaphore()
        for neighbour in (left, right):
            pl.semaphore_signal(
                barrier, inc=1, device_id=(stage, neighbour, dp_pos), device_id_type=MESH_ID
            )
        pl.semaphore_wait(barrier, 2)
        own = pltpu.make_async_copy(x_ref, o_ref.at[pl.ds(0, rows)], own_sem)
        own.start()

        def remote(src, dst, slot, target):
            return pltpu.make_async_remote_copy(
                src_ref=src,
                dst_ref=dst,
                send_sem=send_sem.at[slot],
                recv_sem=recv_sem.at[slot],
                device_id=(stage, target, dp_pos),
                device_id_type=MESH_ID,
            )

        to_right = remote(x_ref, o_ref.at[pl.ds(3 * rows, rows)], 0, right)
        to_left = remote(x_ref, o_ref.at[pl.ds(rows, rows)], 1, left)
        to_right.start()
        to_left.start()
        to_right.wait()
        to_left.wait()
        relay_right = remote(
            o_ref.at[pl.ds(3 * rows, half)], o_ref.at[pl.ds(2 * rows, half)], 2, right
        )
        relay_left = remote(
            o_ref.at[pl.ds(rows + half, half)], o_ref.at[pl.ds(2 * rows + half, half)], 3, left
        )
        relay_right.start()
        relay_left.start()
        relay_right.wait()
        relay_left.wait()
        own.wait()


def ring_gather(shard, stage, count):
    rows, width = shard.shape
    return pl.pallas_call(
        functools.partial(ring_gather_kernel, stage, count),
        out_shape=jax.ShapeDtypeStruct((count * rows, width), shard.dtype),
        in_specs=[pl.BlockSpec(memory_space=pl.ANY)],
        out_specs=pl.BlockSpec(memory_space=pl.ANY),
        scratch_shapes=[
            pltpu.SemaphoreType.DMA((4,)),
            pltpu.SemaphoreType.DMA((4,)),
            pltpu.SemaphoreType.DMA(()),
        ],
        compiler_params=pltpu.CompilerParams(collective_id=stage, has_side_effects=True),
    )(shard)


def reduce_ring(partial, stage, count):
    rows = partial.shape[0] // count
    half = rows // 2
    blocks = [partial[k * rows : (k + 1) * rows] for k in range(count)]
    low = lambda value: value.astype(jnp.bfloat16)
    first_right = lax.ppermute(low(blocks[2][:half]), RING, shift_pairs(stage, count, 1))
    first_left = lax.ppermute(low(blocks[2][half:]), RING, shift_pairs(stage, count, -1))
    to_right = jnp.concatenate(
        [first_right.astype(jnp.float32) + blocks[1][:half], blocks[1][half:]], axis=0
    )
    to_left = jnp.concatenate(
        [blocks[3][:half], first_left.astype(jnp.float32) + blocks[3][half:]], axis=0
    )
    got_left = lax.ppermute(low(to_right), RING, shift_pairs(stage, count, 1))
    got_right = lax.ppermute(low(to_left), RING, shift_pairs(stage, count, -1))
    return blocks[0] + got_left.astype(jnp.float32) + got_right.astype(jnp.float32)


def swap(value):
    return lax.ppermute(value, "section", [(0, 1), (1, 0)])


def seq_pairs(count, step):
    return [(pos, (pos + step) % count) for pos in range(count)]


def reduce_seq(partial, count):
    rows = partial.shape[0] // count
    half = rows // 2
    blocks = [partial[k * rows : (k + 1) * rows] for k in range(count)]
    low = lambda value: value.astype(jnp.bfloat16)
    first_right = lax.ppermute(low(blocks[2][:half]), "seq", seq_pairs(count, 1))
    first_left = lax.ppermute(low(blocks[2][half:]), "seq", seq_pairs(count, -1))
    to_right = jnp.concatenate(
        [first_right.astype(jnp.float32) + blocks[1][:half], blocks[1][half:]], axis=0
    )
    to_left = jnp.concatenate(
        [blocks[3][:half], first_left.astype(jnp.float32) + blocks[3][half:]], axis=0
    )
    got_left = lax.ppermute(low(to_right), "seq", seq_pairs(count, 1))
    got_right = lax.ppermute(low(to_left), "seq", seq_pairs(count, -1))
    return blocks[0] + got_left.astype(jnp.float32) + got_right.astype(jnp.float32)


def body(section_input, saved_qkv, modulation, w_qkv, w_out, lengths, student_out, teacher_target):
    section_total = lax.axis_size("section")
    section_pos = lax.axis_index("section")
    seq_total = lax.axis_size("seq")
    seq_pos = lax.axis_index("seq")
    inputs = section_input[0, 0]
    saved_rows = saved_qkv[0, 0]
    weight_out = w_out[0]
    shard_rows, model_width = inputs.shape
    capacity = saved_rows.shape[0]
    local_width = saved_rows.shape[2]
    live_length = lengths[0]
    w_local = w_qkv[0]
    block_rows = w_local.shape[0]
    half_rows = block_rows // 2
    blocks_total = model_width // block_rows

    other_inputs = swap(inputs)
    other_mods = swap(modulation[0, 0])
    other_w = swap(w_local)
    parts = {}
    for stage in range(section_total):
        own = section_pos == stage
        x_stage = jnp.where(own, inputs, other_inputs)
        mods_stage = jnp.where(own, modulation[0, 0], other_mods)
        parts[stage] = (layer_norm_parts(x_stage), mods_stage)

    weights_of = {}
    for stage in reversed(range(section_total)):
        own = section_pos == stage
        contribution = jnp.where(own, w_local[:half_rows], other_w[half_rows:])
        weights_of[stage] = lax.all_gather(contribution, "dp", axis=0, tiled=True).reshape(
            blocks_total * half_rows, 3 * local_width
        )

    positions = seq_pos * shard_rows + jnp.arange(shard_rows, dtype=jnp.int32)
    row_live = positions < live_length
    gap = student_out[0].astype(jnp.float32) - teacher_target[0].astype(jnp.float32)
    loss_grad = jnp.where(row_live[:, None], gap, 0.0).astype(jnp.bfloat16)
    order = (seq_pos + jnp.arange(seq_total, dtype=jnp.int32)) % seq_total
    token_order = (order[:, None] * shard_rows + jnp.arange(shard_rows, dtype=jnp.int32)).reshape(-1)
    saved_off = jnp.take(saved_rows, token_order, axis=0)
    live_keys = token_order < live_length
    fwd = attend_forward(saved_off, live_keys, HEAD_DIM)
    attn_mixed = fwd[2].reshape(capacity, local_width)

    def pick_half(value, own):
        split = value.reshape(value.shape[0], blocks_total, block_rows)
        chosen = jnp.where(own, split[:, :, :half_rows], split[:, :, half_rows:])
        return chosen.reshape(value.shape[0], blocks_total * half_rows)

    def section_work(d_output, stage):
        own = section_pos == stage
        (normed, inverse), mods_stage = parts[stage]
        scale_term = mods_stage[0]
        gate_term = mods_stage[1]
        d_branch = (gate_term * d_output.astype(jnp.float32)).astype(jnp.bfloat16)
        branch_full = ring_gather(d_branch, stage, seq_total)
        d_attn = jnp.dot(branch_full, weight_out.T, preferred_element_type=jnp.float32).astype(
            jnp.bfloat16
        )
        own_grads = attend_backward(saved_off, fwd, d_attn, HEAD_DIM)
        handed = lax.ppermute(own_grads, "section", [(stage, 1 - stage)])
        flat_grads = jnp.where(own, own_grads, handed)
        d_mod_part = jnp.dot(flat_grads, weights_of[stage].T, preferred_element_type=jnp.float32)
        d_mod = reduce_seq(d_mod_part, seq_total)
        normed_half = pick_half(normed, own)
        d_norm = d_mod * (1.0 + pick_half(scale_term[None], own))
        sums = jnp.stack([jnp.sum(d_norm, axis=-1), jnp.sum(d_norm * normed_half, axis=-1)])
        sums = (sums + swap(sums)) / model_width
        d_layer = inverse * (d_norm - sums[0][:, None] - normed_half * sums[1][:, None])
        d_half = (pick_half(d_output, own).astype(jnp.float32) + d_layer).astype(
            jnp.bfloat16
        )
        other_half = swap(d_half)
        mine = d_half.reshape(shard_rows, blocks_total, half_rows)
        theirs = other_half.reshape(shard_rows, blocks_total, half_rows)
        joined = jnp.concatenate(
            [jnp.where(own, mine, theirs), jnp.where(own, theirs, mine)], axis=2
        )
        return joined.reshape(shard_rows, model_width), branch_full

    incoming = loss_grad
    grad_input = None
    branch_own = None
    for stage in reversed(range(section_total)):
        d_input, branch_full = section_work(incoming, stage)
        here = section_pos == stage
        grad_input = d_input if grad_input is None else jnp.where(here, d_input, grad_input)
        branch_own = branch_full if branch_own is None else jnp.where(here, branch_full, branch_own)
        incoming = d_input
    out_local = jnp.dot(attn_mixed.T, branch_own, preferred_element_type=jnp.float32)
    out_slice = lax.psum_scatter(out_local, "dp", scatter_dimension=1, tiled=True)
    return (grad_input[None, None], out_slice.astype(jnp.bfloat16)[None])


def solution(mesh):
    in_specs = (
        P("section", "dp", "seq", None),
        P("section", "dp", None, None, "seq"),
        P("section", "dp", None, None),
        P("section", "dp", None, "seq"),
        P("section", "seq", None),
        P("dp"),
        P("dp", "seq", None),
        P("dp", "seq", None),
    )
    out_specs = (P("section", "dp", "seq", None), P("section", "seq", "dp"))
    return jax.shard_map(body, mesh=mesh, in_specs=in_specs, out_specs=out_specs, check_vma=False)
```

```python
import functools
import math

import jax
import jax.numpy as jnp
from jax import lax
from jax.experimental import pallas as pl
from jax.experimental.pallas import tpu as pltpu
from jax.sharding import PartitionSpec as P

HEAD_DIM = 128


def widen(tensor):
    return lax.optimization_barrier(tensor).astype(jnp.float32)


def layer_norm_parts(tokens):
    values = tokens.astype(jnp.float32)
    center = values - jnp.mean(values, axis=-1, keepdims=True)
    variance = jnp.mean(center * center, axis=-1, keepdims=True)
    inverse = lax.rsqrt(variance + 1e-06)
    return (center * inverse, inverse)


def attend_forward(saved_rows, live_keys, head_size):
    row_total = saved_rows.shape[0]
    feature_width = saved_rows.shape[2]
    head_count = feature_width // head_size
    queries = saved_rows[:, 0].reshape(row_total, head_count, head_size).astype(jnp.float32)
    key_rows = saved_rows[:, 1].reshape(row_total, head_count, head_size).astype(jnp.float32)
    value_rows = saved_rows[:, 2].reshape(row_total, head_count, head_size).astype(jnp.float32)
    factor = 1.0 / math.sqrt(head_size)
    scores = jnp.einsum("qhd,khd->hqk", queries, key_rows) * factor
    scores = jnp.where(live_keys[None, None, :], scores, -1e30)
    peak_score = jnp.max(scores, axis=-1, keepdims=True)
    weights = jnp.exp(scores - peak_score)
    weights = weights / jnp.sum(weights, axis=-1, keepdims=True)
    rounded = widen(weights.astype(jnp.bfloat16))
    attn_mixed = jnp.einsum("hqk,khd->qhd", rounded, value_rows).astype(jnp.bfloat16)
    return weights, rounded, attn_mixed


def attend_backward(saved_rows, fwd, d_attn, head_size):
    weights, rounded, attn_mixed = fwd
    row_total = saved_rows.shape[0]
    feature_width = saved_rows.shape[2]
    head_count = feature_width // head_size
    queries = saved_rows[:, 0].reshape(row_total, head_count, head_size).astype(jnp.float32)
    key_rows = saved_rows[:, 1].reshape(row_total, head_count, head_size).astype(jnp.float32)
    value_rows = saved_rows[:, 2].reshape(row_total, head_count, head_size).astype(jnp.float32)
    factor = 1.0 / math.sqrt(head_size)
    upstream = d_attn.reshape(row_total, head_count, head_size).astype(jnp.float32)
    d_weights = jnp.einsum("qhd,khd->hqk", upstream, value_rows)
    delta_rows = jnp.einsum("qhd,qhd->hq", upstream, widen(attn_mixed))
    d_scores = widen((weights * (d_weights - delta_rows[:, :, None]) * factor).astype(jnp.bfloat16))
    grad_q = jnp.einsum("hqk,khd->qhd", d_scores, key_rows).astype(jnp.bfloat16)
    grad_k = jnp.einsum("hqk,qhd->khd", d_scores, queries).astype(jnp.bfloat16)
    grad_v = jnp.einsum("hqk,qhd->khd", rounded, upstream).astype(jnp.bfloat16)
    stacked = jnp.stack([grad_q, grad_k, grad_v], axis=1).reshape(row_total, 3 * feature_width)
    return stacked


RING = ("section", "seq")


def shift_pairs(stage, count, step):
    base = stage * count
    return [(base + pos, base + (pos + step) % count) for pos in range(count)]


def gather_ring(shard, stage, count):
    half = shard.shape[0] // 2
    from_left = lax.ppermute(shard, RING, shift_pairs(stage, count, 1))
    from_right = lax.ppermute(shard, RING, shift_pairs(stage, count, -1))
    far_top = lax.ppermute(from_left[:half], RING, shift_pairs(stage, count, 1))
    far_bottom = lax.ppermute(from_right[half:], RING, shift_pairs(stage, count, -1))
    far = jnp.concatenate([far_top, far_bottom], axis=0)
    return jnp.concatenate([shard, from_right, far, from_left], axis=0)


MESH_ID = pl.DeviceIdType.MESH


def ring_gather_kernel(stage, count, x_ref, o_ref, send_sem, recv_sem, own_sem):
    rows = x_ref.shape[0]
    half = rows // 2
    pos = lax.axis_index("seq")
    dp_pos = lax.axis_index("dp")

    @pl.when(lax.axis_index("section") == stage)
    def _():
        right = lax.rem(pos + 1, count)
        left = lax.rem(pos + count - 1, count)
        barrier = pltpu.get_barrier_semaphore()
        for neighbour in (left, right):
            pl.semaphore_signal(
                barrier, inc=1, device_id=(stage, neighbour, dp_pos), device_id_type=MESH_ID
            )
        pl.semaphore_wait(barrier, 2)
        own = pltpu.make_async_copy(x_ref, o_ref.at[pl.ds(0, rows)], own_sem)
        own.start()

        def remote(src, dst, slot, target):
            return pltpu.make_async_remote_copy(
                src_ref=src,
                dst_ref=dst,
                send_sem=send_sem.at[slot],
                recv_sem=recv_sem.at[slot],
                device_id=(stage, target, dp_pos),
                device_id_type=MESH_ID,
            )

        to_right = remote(x_ref, o_ref.at[pl.ds(3 * rows, rows)], 0, right)
        to_left = remote(x_ref, o_ref.at[pl.ds(rows, rows)], 1, left)
        to_right.start()
        to_left.start()
        to_right.wait()
        to_left.wait()
        relay_right = remote(
            o_ref.at[pl.ds(3 * rows, half)], o_ref.at[pl.ds(2 * rows, half)], 2, right
        )
        relay_left = remote(
            o_ref.at[pl.ds(rows + half, half)], o_ref.at[pl.ds(2 * rows + half, half)], 3, left
        )
        relay_right.start()
        relay_left.start()
        relay_right.wait()
        relay_left.wait()
        own.wait()


def ring_gather(shard, stage, count):
    rows, width = shard.shape
    return pl.pallas_call(
        functools.partial(ring_gather_kernel, stage, count),
        out_shape=jax.ShapeDtypeStruct((count * rows, width), shard.dtype),
        in_specs=[pl.BlockSpec(memory_space=pl.ANY)],
        out_specs=pl.BlockSpec(memory_space=pl.ANY),
        scratch_shapes=[
            pltpu.SemaphoreType.DMA((4,)),
            pltpu.SemaphoreType.DMA((4,)),
            pltpu.SemaphoreType.DMA(()),
        ],
        compiler_params=pltpu.CompilerParams(collective_id=stage, has_side_effects=True),
    )(shard)


def reduce_ring(partial, stage, count):
    rows = partial.shape[0] // count
    half = rows // 2
    blocks = [partial[k * rows : (k + 1) * rows] for k in range(count)]
    low = lambda value: value.astype(jnp.bfloat16)
    first_right = lax.ppermute(low(blocks[2][:half]), RING, shift_pairs(stage, count, 1))
    first_left = lax.ppermute(low(blocks[2][half:]), RING, shift_pairs(stage, count, -1))
    to_right = jnp.concatenate(
        [first_right.astype(jnp.float32) + blocks[1][:half], blocks[1][half:]], axis=0
    )
    to_left = jnp.concatenate(
        [blocks[3][:half], first_left.astype(jnp.float32) + blocks[3][half:]], axis=0
    )
    got_left = lax.ppermute(low(to_right), RING, shift_pairs(stage, count, 1))
    got_right = lax.ppermute(low(to_left), RING, shift_pairs(stage, count, -1))
    return blocks[0] + got_left.astype(jnp.float32) + got_right.astype(jnp.float32)


def swap(value):
    return lax.ppermute(value, "section", [(0, 1), (1, 0)])


def seq_pairs(count, step):
    return [(pos, (pos + step) % count) for pos in range(count)]


def reduce_seq(partial, count):
    rows = partial.shape[0] // count
    half = rows // 2
    blocks = [partial[k * rows : (k + 1) * rows] for k in range(count)]
    low = lambda value: value.astype(jnp.bfloat16)
    first_right = lax.ppermute(low(blocks[2][:half]), "seq", seq_pairs(count, 1))
    first_left = lax.ppermute(low(blocks[2][half:]), "seq", seq_pairs(count, -1))
    to_right = jnp.concatenate(
        [first_right.astype(jnp.float32) + blocks[1][:half], blocks[1][half:]], axis=0
    )
    to_left = jnp.concatenate(
        [blocks[3][:half], first_left.astype(jnp.float32) + blocks[3][half:]], axis=0
    )
    got_left = lax.ppermute(low(to_right), "seq", seq_pairs(count, 1))
    got_right = lax.ppermute(low(to_left), "seq", seq_pairs(count, -1))
    return blocks[0] + got_left.astype(jnp.float32) + got_right.astype(jnp.float32)


def body(section_input, saved_qkv, modulation, w_qkv, w_out, lengths, student_out, teacher_target):
    section_total = lax.axis_size("section")
    section_pos = lax.axis_index("section")
    seq_total = lax.axis_size("seq")
    seq_pos = lax.axis_index("seq")
    inputs = section_input[0, 0]
    saved_rows = saved_qkv[0, 0]
    weight_out = w_out[0]
    shard_rows, model_width = inputs.shape
    capacity = saved_rows.shape[0]
    local_width = saved_rows.shape[2]
    live_length = lengths[0]
    w_local = w_qkv[0]
    block_rows = w_local.shape[0]
    half_rows = block_rows // 2
    blocks_total = model_width // block_rows

    other_inputs = swap(inputs)
    other_mods = swap(modulation[0, 0])
    other_w = swap(w_local)
    parts = {}
    for stage in range(section_total):
        own = section_pos == stage
        x_stage = jnp.where(own, inputs, other_inputs)
        mods_stage = jnp.where(own, modulation[0, 0], other_mods)
        parts[stage] = (layer_norm_parts(x_stage), mods_stage)

    weights_of = {}
    for stage in reversed(range(section_total)):
        own = section_pos == stage
        contribution = jnp.where(own, w_local[:half_rows], other_w[half_rows:])
        weights_of[stage] = lax.all_gather(contribution, "dp", axis=0, tiled=True).reshape(
            blocks_total * half_rows, 3 * local_width
        )

    positions = seq_pos * shard_rows + jnp.arange(shard_rows, dtype=jnp.int32)
    row_live = positions < live_length
    gap = student_out[0].astype(jnp.float32) - teacher_target[0].astype(jnp.float32)
    loss_grad = jnp.where(row_live[:, None], gap, 0.0).astype(jnp.bfloat16)
    order = (seq_pos + jnp.arange(seq_total, dtype=jnp.int32)) % seq_total
    token_order = (order[:, None] * shard_rows + jnp.arange(shard_rows, dtype=jnp.int32)).reshape(-1)
    saved_off = jnp.take(saved_rows, token_order, axis=0)
    live_keys = token_order < live_length
    fwd = attend_forward(saved_off, live_keys, HEAD_DIM)
    attn_mixed = fwd[2].reshape(capacity, local_width)

    def pick_half(value, own):
        split = value.reshape(value.shape[0], blocks_total, block_rows)
        chosen = jnp.where(own, split[:, :, :half_rows], split[:, :, half_rows:])
        return chosen.reshape(value.shape[0], blocks_total * half_rows)

    def section_work(d_output, stage):
        own = section_pos == stage
        (normed, inverse), mods_stage = parts[stage]
        scale_term = mods_stage[0]
        gate_term = mods_stage[1]
        d_branch = (gate_term * d_output.astype(jnp.float32)).astype(jnp.bfloat16)
        branch_full = ring_gather(d_branch, stage, seq_total)
        d_attn = jnp.dot(branch_full, weight_out.T, preferred_element_type=jnp.float32).astype(
            jnp.bfloat16
        )
        own_grads = attend_backward(saved_off, fwd, d_attn, HEAD_DIM)
        handed = lax.ppermute(own_grads, "section", [(stage, 1 - stage)])
        flat_grads = jnp.where(own, own_grads, handed)
        d_mod_part = jnp.dot(flat_grads, weights_of[stage].T, preferred_element_type=jnp.float32)
        d_mod = reduce_seq(d_mod_part, seq_total)
        normed_half = pick_half(normed, own)
        d_norm = d_mod * (1.0 + pick_half(scale_term[None], own))
        sums = jnp.stack([jnp.sum(d_norm, axis=-1), jnp.sum(d_norm * normed_half, axis=-1)])
        sums = (sums + swap(sums)) / model_width
        d_layer = inverse * (d_norm - sums[0][:, None] - normed_half * sums[1][:, None])
        d_half = (pick_half(d_output, own).astype(jnp.float32) + d_layer).astype(
            jnp.bfloat16
        )
        other_half = swap(d_half)
        mine = d_half.reshape(shard_rows, blocks_total, half_rows)
        theirs = other_half.reshape(shard_rows, blocks_total, half_rows)
        joined = jnp.concatenate(
            [jnp.where(own, mine, theirs), jnp.where(own, theirs, mine)], axis=2
        )
        return joined.reshape(shard_rows, model_width), branch_full

    incoming = loss_grad
    grad_input = None
    branch_own = None
    for stage in reversed(range(section_total)):
        d_input, branch_full = section_work(incoming, stage)
        here = section_pos == stage
        grad_input = d_input if grad_input is None else jnp.where(here, d_input, grad_input)
        branch_own = branch_full if branch_own is None else jnp.where(here, branch_full, branch_own)
        incoming = d_input
    out_local = jnp.dot(attn_mixed.T, branch_own, preferred_element_type=jnp.float32)
    out_slice = lax.psum_scatter(
        out_local.astype(jnp.bfloat16), "dp", scatter_dimension=1, tiled=True
    )
    return (grad_input[None, None], out_slice[None])


def solution(mesh):
    in_specs = (
        P("section", "dp", "seq", None),
        P("section", "dp", None, None, "seq"),
        P("section", "dp", None, None),
        P("section", "dp", None, "seq"),
        P("section", "seq", None),
        P("dp"),
        P("dp", "seq", None),
        P("dp", "seq", None),
    )
    out_specs = (P("section", "dp", "seq", None), P("section", "seq", "dp"))
    return jax.shard_map(body, mesh=mesh, in_specs=in_specs, out_specs=out_specs, check_vma=False)
```

```python
import functools
import math

import jax
import jax.numpy as jnp
from jax import lax
from jax.experimental import pallas as pl
from jax.experimental.pallas import tpu as pltpu
from jax.sharding import PartitionSpec as P

HEAD_DIM = 128


def widen(tensor):
    return lax.optimization_barrier(tensor).astype(jnp.float32)


def layer_norm_parts(tokens):
    values = tokens.astype(jnp.float32)
    center = values - jnp.mean(values, axis=-1, keepdims=True)
    variance = jnp.mean(center * center, axis=-1, keepdims=True)
    inverse = lax.rsqrt(variance + 1e-06)
    return (center * inverse, inverse)


def attend_forward(saved_rows, live_keys, head_size):
    row_total = saved_rows.shape[0]
    feature_width = saved_rows.shape[2]
    head_count = feature_width // head_size
    queries = saved_rows[:, 0].reshape(row_total, head_count, head_size).astype(jnp.float32)
    key_rows = saved_rows[:, 1].reshape(row_total, head_count, head_size).astype(jnp.float32)
    value_rows = saved_rows[:, 2].reshape(row_total, head_count, head_size).astype(jnp.float32)
    factor = 1.0 / math.sqrt(head_size)
    scores = jnp.einsum("qhd,khd->hqk", queries, key_rows) * factor
    scores = jnp.where(live_keys[None, None, :], scores, -1e30)
    peak_score = jnp.max(scores, axis=-1, keepdims=True)
    weights = jnp.exp(scores - peak_score)
    weights = weights / jnp.sum(weights, axis=-1, keepdims=True)
    rounded = widen(weights.astype(jnp.bfloat16))
    attn_mixed = jnp.einsum("hqk,khd->qhd", rounded, value_rows).astype(jnp.bfloat16)
    return weights, rounded, attn_mixed


def attend_backward(saved_rows, fwd, d_attn, head_size):
    weights, rounded, attn_mixed = fwd
    row_total = saved_rows.shape[0]
    feature_width = saved_rows.shape[2]
    head_count = feature_width // head_size
    queries = saved_rows[:, 0].reshape(row_total, head_count, head_size).astype(jnp.float32)
    key_rows = saved_rows[:, 1].reshape(row_total, head_count, head_size).astype(jnp.float32)
    value_rows = saved_rows[:, 2].reshape(row_total, head_count, head_size).astype(jnp.float32)
    factor = 1.0 / math.sqrt(head_size)
    upstream = d_attn.reshape(row_total, head_count, head_size).astype(jnp.float32)
    d_weights = jnp.einsum("qhd,khd->hqk", upstream, value_rows)
    delta_rows = jnp.einsum("qhd,qhd->hq", upstream, widen(attn_mixed))
    d_scores = widen((weights * (d_weights - delta_rows[:, :, None]) * factor).astype(jnp.bfloat16))
    grad_q = jnp.einsum("hqk,khd->qhd", d_scores, key_rows).astype(jnp.bfloat16)
    grad_k = jnp.einsum("hqk,qhd->khd", d_scores, queries).astype(jnp.bfloat16)
    grad_v = jnp.einsum("hqk,qhd->khd", rounded, upstream).astype(jnp.bfloat16)
    stacked = jnp.stack([grad_q, grad_k, grad_v], axis=1).reshape(row_total, 3 * feature_width)
    return stacked


RING = ("section", "seq")


def shift_pairs(stage, count, step):
    base = stage * count
    return [(base + pos, base + (pos + step) % count) for pos in range(count)]


def gather_ring(shard, stage, count):
    half = shard.shape[0] // 2
    from_left = lax.ppermute(shard, RING, shift_pairs(stage, count, 1))
    from_right = lax.ppermute(shard, RING, shift_pairs(stage, count, -1))
    far_top = lax.ppermute(from_left[:half], RING, shift_pairs(stage, count, 1))
    far_bottom = lax.ppermute(from_right[half:], RING, shift_pairs(stage, count, -1))
    far = jnp.concatenate([far_top, far_bottom], axis=0)
    return jnp.concatenate([shard, from_right, far, from_left], axis=0)


MESH_ID = pl.DeviceIdType.MESH


def ring_gather_kernel(stage, count, x_ref, o_ref, send_sem, recv_sem, own_sem):
    rows = x_ref.shape[0]
    half = rows // 2
    pos = lax.axis_index("seq")
    dp_pos = lax.axis_index("dp")

    @pl.when(lax.axis_index("section") == stage)
    def _():
        right = lax.rem(pos + 1, count)
        left = lax.rem(pos + count - 1, count)
        barrier = pltpu.get_barrier_semaphore()
        for neighbour in (left, right):
            pl.semaphore_signal(
                barrier, inc=1, device_id=(stage, neighbour, dp_pos), device_id_type=MESH_ID
            )
        pl.semaphore_wait(barrier, 2)
        own = pltpu.make_async_copy(x_ref, o_ref.at[pl.ds(0, rows)], own_sem)
        own.start()

        def remote(src, dst, slot, target):
            return pltpu.make_async_remote_copy(
                src_ref=src,
                dst_ref=dst,
                send_sem=send_sem.at[slot],
                recv_sem=recv_sem.at[slot],
                device_id=(stage, target, dp_pos),
                device_id_type=MESH_ID,
            )

        to_right = remote(x_ref, o_ref.at[pl.ds(3 * rows, rows)], 0, right)
        to_left = remote(x_ref, o_ref.at[pl.ds(rows, rows)], 1, left)
        to_right.start()
        to_left.start()
        to_right.wait()
        to_left.wait()
        relay_right = remote(
            o_ref.at[pl.ds(3 * rows, half)], o_ref.at[pl.ds(2 * rows, half)], 2, right
        )
        relay_left = remote(
            o_ref.at[pl.ds(rows + half, half)], o_ref.at[pl.ds(2 * rows + half, half)], 3, left
        )
        relay_right.start()
        relay_left.start()
        relay_right.wait()
        relay_left.wait()
        own.wait()


def ring_gather(shard, stage, count):
    rows, width = shard.shape
    return pl.pallas_call(
        functools.partial(ring_gather_kernel, stage, count),
        out_shape=jax.ShapeDtypeStruct((count * rows, width), shard.dtype),
        in_specs=[pl.BlockSpec(memory_space=pl.ANY)],
        out_specs=pl.BlockSpec(memory_space=pl.ANY),
        scratch_shapes=[
            pltpu.SemaphoreType.DMA((4,)),
            pltpu.SemaphoreType.DMA((4,)),
            pltpu.SemaphoreType.DMA(()),
        ],
        compiler_params=pltpu.CompilerParams(collective_id=stage, has_side_effects=True),
    )(shard)


def reduce_ring(partial, stage, count):
    rows = partial.shape[0] // count
    half = rows // 2
    blocks = [partial[k * rows : (k + 1) * rows] for k in range(count)]
    low = lambda value: value.astype(jnp.bfloat16)
    first_right = lax.ppermute(low(blocks[2][:half]), RING, shift_pairs(stage, count, 1))
    first_left = lax.ppermute(low(blocks[2][half:]), RING, shift_pairs(stage, count, -1))
    to_right = jnp.concatenate(
        [first_right.astype(jnp.float32) + blocks[1][:half], blocks[1][half:]], axis=0
    )
    to_left = jnp.concatenate(
        [blocks[3][:half], first_left.astype(jnp.float32) + blocks[3][half:]], axis=0
    )
    got_left = lax.ppermute(low(to_right), RING, shift_pairs(stage, count, 1))
    got_right = lax.ppermute(low(to_left), RING, shift_pairs(stage, count, -1))
    return blocks[0] + got_left.astype(jnp.float32) + got_right.astype(jnp.float32)


def swap(value):
    return lax.ppermute(value, "section", [(0, 1), (1, 0)])


def seq_pairs(count, step):
    return [(pos, (pos + step) % count) for pos in range(count)]


def reduce_seq(partial, count):
    rows = partial.shape[0] // count
    half = rows // 2
    blocks = [partial[k * rows : (k + 1) * rows] for k in range(count)]
    low = lambda value: value.astype(jnp.bfloat16)
    first_right = lax.ppermute(low(blocks[2][:half]), "seq", seq_pairs(count, 1))
    first_left = lax.ppermute(low(blocks[2][half:]), "seq", seq_pairs(count, -1))
    to_right = jnp.concatenate(
        [first_right.astype(jnp.float32) + blocks[1][:half], blocks[1][half:]], axis=0
    )
    to_left = jnp.concatenate(
        [blocks[3][:half], first_left.astype(jnp.float32) + blocks[3][half:]], axis=0
    )
    got_left = lax.ppermute(low(to_right), "seq", seq_pairs(count, 1))
    got_right = lax.ppermute(low(to_left), "seq", seq_pairs(count, -1))
    return blocks[0] + got_left.astype(jnp.float32) + got_right.astype(jnp.float32)


def body(section_input, saved_qkv, modulation, w_qkv, w_out, lengths, student_out, teacher_target):
    section_total = lax.axis_size("section")
    section_pos = lax.axis_index("section")
    seq_total = lax.axis_size("seq")
    seq_pos = lax.axis_index("seq")
    inputs = section_input[0, 0]
    saved_rows = saved_qkv[0, 0]
    weight_out = w_out[0]
    shard_rows, model_width = inputs.shape
    capacity = saved_rows.shape[0]
    local_width = saved_rows.shape[2]
    live_length = lengths[0]
    w_local = w_qkv[0]
    block_rows = w_local.shape[0]
    half_rows = block_rows // 2
    blocks_total = model_width // block_rows

    other_inputs = swap(inputs)
    other_mods = swap(modulation[0, 0])
    other_w = swap(w_local)
    parts = {}
    for stage in range(section_total):
        own = section_pos == stage
        x_stage = jnp.where(own, inputs, other_inputs)
        mods_stage = jnp.where(own, modulation[0, 0], other_mods)
        parts[stage] = (layer_norm_parts(x_stage), mods_stage)

    weights_of = {}
    for stage in reversed(range(section_total)):
        own = section_pos == stage
        contribution = jnp.where(own, w_local[:half_rows], other_w[half_rows:])
        weights_of[stage] = lax.all_gather(contribution, "dp", axis=0, tiled=True).reshape(
            blocks_total * half_rows, 3 * local_width
        )

    positions = seq_pos * shard_rows + jnp.arange(shard_rows, dtype=jnp.int32)
    row_live = positions < live_length
    gap = student_out[0].astype(jnp.float32) - teacher_target[0].astype(jnp.float32)
    loss_grad = jnp.where(row_live[:, None], gap, 0.0).astype(jnp.bfloat16)
    order = (seq_pos + jnp.arange(seq_total, dtype=jnp.int32)) % seq_total
    token_order = (order[:, None] * shard_rows + jnp.arange(shard_rows, dtype=jnp.int32)).reshape(-1)
    saved_off = jnp.take(saved_rows, token_order, axis=0)
    live_keys = token_order < live_length
    fwd = attend_forward(saved_off, live_keys, HEAD_DIM)
    attn_mixed = fwd[2].reshape(capacity, local_width)

    def pick_half(value, own):
        split = value.reshape(value.shape[0], blocks_total, block_rows)
        chosen = jnp.where(own, split[:, :, :half_rows], split[:, :, half_rows:])
        return chosen.reshape(value.shape[0], blocks_total * half_rows)

    def section_work(d_output, stage):
        own = section_pos == stage
        (normed, inverse), mods_stage = parts[stage]
        scale_term = mods_stage[0]
        gate_term = mods_stage[1]
        d_branch = (gate_term * d_output.astype(jnp.float32)).astype(jnp.bfloat16)
        if stage == section_total - 1:
            branch_full = gather_ring(d_branch, stage, seq_total)
        else:
            branch_full = ring_gather(d_branch, stage, seq_total)
        d_attn = jnp.dot(branch_full, weight_out.T, preferred_element_type=jnp.float32).astype(
            jnp.bfloat16
        )
        own_grads = attend_backward(saved_off, fwd, d_attn, HEAD_DIM)
        handed = lax.ppermute(own_grads, "section", [(stage, 1 - stage)])
        flat_grads = jnp.where(own, own_grads, handed)
        d_mod_part = jnp.dot(flat_grads, weights_of[stage].T, preferred_element_type=jnp.float32)
        d_mod = reduce_seq(d_mod_part, seq_total)
        normed_half = pick_half(normed, own)
        d_norm = d_mod * (1.0 + pick_half(scale_term[None], own))
        sums = jnp.stack([jnp.sum(d_norm, axis=-1), jnp.sum(d_norm * normed_half, axis=-1)])
        sums = (sums + swap(sums)) / model_width
        d_layer = inverse * (d_norm - sums[0][:, None] - normed_half * sums[1][:, None])
        d_half = (pick_half(d_output, own).astype(jnp.float32) + d_layer).astype(
            jnp.bfloat16
        )
        other_half = swap(d_half)
        mine = d_half.reshape(shard_rows, blocks_total, half_rows)
        theirs = other_half.reshape(shard_rows, blocks_total, half_rows)
        joined = jnp.concatenate(
            [jnp.where(own, mine, theirs), jnp.where(own, theirs, mine)], axis=2
        )
        return joined.reshape(shard_rows, model_width), branch_full

    incoming = loss_grad
    grad_input = None
    branch_own = None
    for stage in reversed(range(section_total)):
        d_input, branch_full = section_work(incoming, stage)
        here = section_pos == stage
        grad_input = d_input if grad_input is None else jnp.where(here, d_input, grad_input)
        branch_own = branch_full if branch_own is None else jnp.where(here, branch_full, branch_own)
        incoming = d_input
    out_local = jnp.dot(attn_mixed.T, branch_own, preferred_element_type=jnp.float32)
    out_slice = lax.psum_scatter(out_local, "dp", scatter_dimension=1, tiled=True)
    return (grad_input[None, None], out_slice.astype(jnp.bfloat16)[None])


def solution(mesh):
    in_specs = (
        P("section", "dp", "seq", None),
        P("section", "dp", None, None, "seq"),
        P("section", "dp", None, None),
        P("section", "dp", None, "seq"),
        P("section", "seq", None),
        P("dp"),
        P("dp", "seq", None),
        P("dp", "seq", None),
    )
    out_specs = (P("section", "dp", "seq", None), P("section", "seq", "dp"))
    return jax.shard_map(body, mesh=mesh, in_specs=in_specs, out_specs=out_specs, check_vma=False)
```

```python
import functools
import math

import jax
import jax.numpy as jnp
from jax import lax
from jax.experimental import pallas as pl
from jax.experimental.pallas import tpu as pltpu
from jax.sharding import PartitionSpec as P

HEAD_DIM = 128


def widen(tensor):
    return lax.optimization_barrier(tensor).astype(jnp.float32)


def layer_norm_parts(tokens):
    values = tokens.astype(jnp.float32)
    center = values - jnp.mean(values, axis=-1, keepdims=True)
    variance = jnp.mean(center * center, axis=-1, keepdims=True)
    inverse = lax.rsqrt(variance + 1e-06)
    return (center * inverse, inverse)


def attend_forward(saved_rows, live_keys, head_size):
    row_total = saved_rows.shape[0]
    feature_width = saved_rows.shape[2]
    head_count = feature_width // head_size
    queries = saved_rows[:, 0].reshape(row_total, head_count, head_size).astype(jnp.float32)
    key_rows = saved_rows[:, 1].reshape(row_total, head_count, head_size).astype(jnp.float32)
    value_rows = saved_rows[:, 2].reshape(row_total, head_count, head_size).astype(jnp.float32)
    factor = 1.0 / math.sqrt(head_size)
    scores = jnp.einsum("qhd,khd->hqk", queries, key_rows) * factor
    scores = jnp.where(live_keys[None, None, :], scores, -1e30)
    peak_score = jnp.max(scores, axis=-1, keepdims=True)
    weights = jnp.exp(scores - peak_score)
    weights = weights / jnp.sum(weights, axis=-1, keepdims=True)
    rounded = widen(weights.astype(jnp.bfloat16))
    attn_mixed = jnp.einsum("hqk,khd->qhd", rounded, value_rows).astype(jnp.bfloat16)
    return weights, rounded, attn_mixed


def attend_backward(saved_rows, fwd, d_attn, head_size):
    weights, rounded, attn_mixed = fwd
    row_total = saved_rows.shape[0]
    feature_width = saved_rows.shape[2]
    head_count = feature_width // head_size
    queries = saved_rows[:, 0].reshape(row_total, head_count, head_size).astype(jnp.float32)
    key_rows = saved_rows[:, 1].reshape(row_total, head_count, head_size).astype(jnp.float32)
    value_rows = saved_rows[:, 2].reshape(row_total, head_count, head_size).astype(jnp.float32)
    factor = 1.0 / math.sqrt(head_size)
    upstream = d_attn.reshape(row_total, head_count, head_size).astype(jnp.float32)
    d_weights = jnp.einsum("qhd,khd->hqk", upstream, value_rows)
    delta_rows = jnp.einsum("qhd,qhd->hq", upstream, widen(attn_mixed))
    d_scores = widen((weights * (d_weights - delta_rows[:, :, None]) * factor).astype(jnp.bfloat16))
    grad_q = jnp.einsum("hqk,khd->qhd", d_scores, key_rows).astype(jnp.bfloat16)
    grad_k = jnp.einsum("hqk,qhd->khd", d_scores, queries).astype(jnp.bfloat16)
    grad_v = jnp.einsum("hqk,qhd->khd", rounded, upstream).astype(jnp.bfloat16)
    stacked = jnp.stack([grad_q, grad_k, grad_v], axis=1).reshape(row_total, 3 * feature_width)
    return stacked


RING = ("section", "seq")


def shift_pairs(stage, count, step):
    base = stage * count
    return [(base + pos, base + (pos + step) % count) for pos in range(count)]


def gather_ring(shard, stage, count):
    half = shard.shape[0] // 2
    from_left = lax.ppermute(shard, RING, shift_pairs(stage, count, 1))
    from_right = lax.ppermute(shard, RING, shift_pairs(stage, count, -1))
    far_top = lax.ppermute(from_left[:half], RING, shift_pairs(stage, count, 1))
    far_bottom = lax.ppermute(from_right[half:], RING, shift_pairs(stage, count, -1))
    far = jnp.concatenate([far_top, far_bottom], axis=0)
    return jnp.concatenate([shard, from_right, far, from_left], axis=0)


MESH_ID = pl.DeviceIdType.MESH


def ring_gather_kernel(stage, count, x_ref, o_ref, send_sem, recv_sem, own_sem):
    rows = x_ref.shape[0]
    half = rows // 2
    pos = lax.axis_index("seq")
    dp_pos = lax.axis_index("dp")

    @pl.when(lax.axis_index("section") == stage)
    def _():
        right = lax.rem(pos + 1, count)
        left = lax.rem(pos + count - 1, count)
        barrier = pltpu.get_barrier_semaphore()
        for neighbour in (left, right):
            pl.semaphore_signal(
                barrier, inc=1, device_id=(stage, neighbour, dp_pos), device_id_type=MESH_ID
            )
        pl.semaphore_wait(barrier, 2)
        own = pltpu.make_async_copy(x_ref, o_ref.at[pl.ds(0, rows)], own_sem)
        own.start()

        def remote(src, dst, slot, target):
            return pltpu.make_async_remote_copy(
                src_ref=src,
                dst_ref=dst,
                send_sem=send_sem.at[slot],
                recv_sem=recv_sem.at[slot],
                device_id=(stage, target, dp_pos),
                device_id_type=MESH_ID,
            )

        to_right = remote(x_ref, o_ref.at[pl.ds(3 * rows, rows)], 0, right)
        to_left = remote(x_ref, o_ref.at[pl.ds(rows, rows)], 1, left)
        to_right.start()
        to_left.start()
        to_right.wait()
        to_left.wait()
        relay_right = remote(
            o_ref.at[pl.ds(3 * rows, half)], o_ref.at[pl.ds(2 * rows, half)], 2, right
        )
        relay_left = remote(
            o_ref.at[pl.ds(rows + half, half)], o_ref.at[pl.ds(2 * rows + half, half)], 3, left
        )
        relay_right.start()
        relay_left.start()
        relay_right.wait()
        relay_left.wait()
        own.wait()


def ring_gather(shard, stage, count):
    rows, width = shard.shape
    return pl.pallas_call(
        functools.partial(ring_gather_kernel, stage, count),
        out_shape=jax.ShapeDtypeStruct((count * rows, width), shard.dtype),
        in_specs=[pl.BlockSpec(memory_space=pl.ANY)],
        out_specs=pl.BlockSpec(memory_space=pl.ANY),
        scratch_shapes=[
            pltpu.SemaphoreType.DMA((4,)),
            pltpu.SemaphoreType.DMA((4,)),
            pltpu.SemaphoreType.DMA(()),
        ],
        compiler_params=pltpu.CompilerParams(collective_id=stage, has_side_effects=True),
    )(shard)


def ring_reduce_kernel(count, p_ref, o_ref, send1, recv1, send2, recv2, send_sem, recv_sem):
    rows = o_ref.shape[0]
    half = rows // 2
    pos = lax.axis_index("seq")
    section = lax.axis_index("section")
    dp_pos = lax.axis_index("dp")
    right = lax.rem(pos + 1, count)
    left = lax.rem(pos + count - 1, count)
    barrier = pltpu.get_barrier_semaphore()
    for neighbour in (left, right):
        pl.semaphore_signal(
            barrier, inc=1, device_id=(section, neighbour, dp_pos), device_id_type=MESH_ID
        )
    pl.semaphore_wait(barrier, 2)

    def remote(src, dst, slot, target):
        return pltpu.make_async_remote_copy(
            src_ref=src,
            dst_ref=dst,
            send_sem=send_sem.at[slot],
            recv_sem=recv_sem.at[slot],
            device_id=(section, target, dp_pos),
            device_id_type=MESH_ID,
        )

    low = jnp.bfloat16
    send1[0] = p_ref[pl.ds(2 * rows, half), :].astype(low)
    send1[1] = p_ref[pl.ds(2 * rows + half, half), :].astype(low)
    first_right = remote(send1.at[0], recv1.at[0], 0, right)
    first_left = remote(send1.at[1], recv1.at[1], 1, left)
    first_right.start()
    first_left.start()
    first_right.wait()
    first_left.wait()
    send2[0, pl.ds(0, half), :] = (
        recv1[0].astype(jnp.float32) + p_ref[pl.ds(rows, half), :]
    ).astype(low)
    send2[0, pl.ds(half, half), :] = p_ref[pl.ds(rows + half, half), :].astype(low)
    send2[1, pl.ds(0, half), :] = p_ref[pl.ds(3 * rows, half), :].astype(low)
    send2[1, pl.ds(half, half), :] = (
        recv1[1].astype(jnp.float32) + p_ref[pl.ds(3 * rows + half, half), :]
    ).astype(low)
    second_right = remote(send2.at[0], recv2.at[0], 2, right)
    second_left = remote(send2.at[1], recv2.at[1], 3, left)
    second_right.start()
    second_left.start()
    second_right.wait()
    second_left.wait()
    o_ref[...] = (
        p_ref[pl.ds(0, rows), :]
        + recv2[0].astype(jnp.float32)
        + recv2[1].astype(jnp.float32)
    )


def ring_reduce(partial, stage, count):
    total_rows, width = partial.shape
    rows = total_rows // count
    half = rows // 2
    vmem = pltpu.MemorySpace.VMEM
    return pl.pallas_call(
        functools.partial(ring_reduce_kernel, count),
        out_shape=jax.ShapeDtypeStruct((rows, width), jnp.float32),
        in_specs=[pl.BlockSpec(memory_space=vmem)],
        out_specs=pl.BlockSpec(memory_space=vmem),
        scratch_shapes=[
            pltpu.VMEM((2, half, width), jnp.bfloat16),
            pltpu.VMEM((2, half, width), jnp.bfloat16),
            pltpu.VMEM((2, rows, width), jnp.bfloat16),
            pltpu.VMEM((2, rows, width), jnp.bfloat16),
            pltpu.SemaphoreType.DMA((4,)),
            pltpu.SemaphoreType.DMA((4,)),
        ],
        compiler_params=pltpu.CompilerParams(collective_id=2 + stage, has_side_effects=True),
    )(partial)


def reduce_ring(partial, stage, count):
    rows = partial.shape[0] // count
    half = rows // 2
    blocks = [partial[k * rows : (k + 1) * rows] for k in range(count)]
    low = lambda value: value.astype(jnp.bfloat16)
    first_right = lax.ppermute(low(blocks[2][:half]), RING, shift_pairs(stage, count, 1))
    first_left = lax.ppermute(low(blocks[2][half:]), RING, shift_pairs(stage, count, -1))
    to_right = jnp.concatenate(
        [first_right.astype(jnp.float32) + blocks[1][:half], blocks[1][half:]], axis=0
    )
    to_left = jnp.concatenate(
        [blocks[3][:half], first_left.astype(jnp.float32) + blocks[3][half:]], axis=0
    )
    got_left = lax.ppermute(low(to_right), RING, shift_pairs(stage, count, 1))
    got_right = lax.ppermute(low(to_left), RING, shift_pairs(stage, count, -1))
    return blocks[0] + got_left.astype(jnp.float32) + got_right.astype(jnp.float32)


def swap(value):
    return lax.ppermute(value, "section", [(0, 1), (1, 0)])


def seq_pairs(count, step):
    return [(pos, (pos + step) % count) for pos in range(count)]


def reduce_seq(partial, count):
    rows = partial.shape[0] // count
    half = rows // 2
    blocks = [partial[k * rows : (k + 1) * rows] for k in range(count)]
    low = lambda value: value.astype(jnp.bfloat16)
    first_right = lax.ppermute(low(blocks[2][:half]), "seq", seq_pairs(count, 1))
    first_left = lax.ppermute(low(blocks[2][half:]), "seq", seq_pairs(count, -1))
    to_right = jnp.concatenate(
        [first_right.astype(jnp.float32) + blocks[1][:half], blocks[1][half:]], axis=0
    )
    to_left = jnp.concatenate(
        [blocks[3][:half], first_left.astype(jnp.float32) + blocks[3][half:]], axis=0
    )
    got_left = lax.ppermute(low(to_right), "seq", seq_pairs(count, 1))
    got_right = lax.ppermute(low(to_left), "seq", seq_pairs(count, -1))
    return blocks[0] + got_left.astype(jnp.float32) + got_right.astype(jnp.float32)


def body(section_input, saved_qkv, modulation, w_qkv, w_out, lengths, student_out, teacher_target):
    section_total = lax.axis_size("section")
    section_pos = lax.axis_index("section")
    seq_total = lax.axis_size("seq")
    seq_pos = lax.axis_index("seq")
    inputs = section_input[0, 0]
    saved_rows = saved_qkv[0, 0]
    weight_out = w_out[0]
    shard_rows, model_width = inputs.shape
    capacity = saved_rows.shape[0]
    local_width = saved_rows.shape[2]
    live_length = lengths[0]
    w_local = w_qkv[0]
    block_rows = w_local.shape[0]
    half_rows = block_rows // 2
    blocks_total = model_width // block_rows

    other_inputs = swap(inputs)
    other_mods = swap(modulation[0, 0])
    other_w = swap(w_local)
    parts = {}
    for stage in range(section_total):
        own = section_pos == stage
        x_stage = jnp.where(own, inputs, other_inputs)
        mods_stage = jnp.where(own, modulation[0, 0], other_mods)
        parts[stage] = (layer_norm_parts(x_stage), mods_stage)

    weights_of = {}
    for stage in reversed(range(section_total)):
        own = section_pos == stage
        contribution = jnp.where(own, w_local[:half_rows], other_w[half_rows:])
        weights_of[stage] = lax.all_gather(contribution, "dp", axis=0, tiled=True).reshape(
            blocks_total * half_rows, 3 * local_width
        )

    positions = seq_pos * shard_rows + jnp.arange(shard_rows, dtype=jnp.int32)
    row_live = positions < live_length
    gap = student_out[0].astype(jnp.float32) - teacher_target[0].astype(jnp.float32)
    loss_grad = jnp.where(row_live[:, None], gap, 0.0).astype(jnp.bfloat16)
    order = (seq_pos + jnp.arange(seq_total, dtype=jnp.int32)) % seq_total
    token_order = (order[:, None] * shard_rows + jnp.arange(shard_rows, dtype=jnp.int32)).reshape(-1)
    saved_off = jnp.take(saved_rows, token_order, axis=0)
    live_keys = token_order < live_length
    fwd = attend_forward(saved_off, live_keys, HEAD_DIM)
    attn_mixed = fwd[2].reshape(capacity, local_width)

    def pick_half(value, own):
        split = value.reshape(value.shape[0], blocks_total, block_rows)
        chosen = jnp.where(own, split[:, :, :half_rows], split[:, :, half_rows:])
        return chosen.reshape(value.shape[0], blocks_total * half_rows)

    def section_work(d_output, stage):
        own = section_pos == stage
        (normed, inverse), mods_stage = parts[stage]
        scale_term = mods_stage[0]
        gate_term = mods_stage[1]
        d_branch = (gate_term * d_output.astype(jnp.float32)).astype(jnp.bfloat16)
        if stage == section_total - 1:
            branch_full = gather_ring(d_branch, stage, seq_total)
        else:
            branch_full = ring_gather(d_branch, stage, seq_total)
        d_attn = jnp.dot(branch_full, weight_out.T, preferred_element_type=jnp.float32).astype(
            jnp.bfloat16
        )
        own_grads = attend_backward(saved_off, fwd, d_attn, HEAD_DIM)
        handed = lax.ppermute(own_grads, "section", [(stage, 1 - stage)])
        flat_grads = jnp.where(own, own_grads, handed)
        d_mod_part = jnp.dot(flat_grads, weights_of[stage].T, preferred_element_type=jnp.float32)
        d_mod = ring_reduce(d_mod_part, stage, seq_total)
        normed_half = pick_half(normed, own)
        d_norm = d_mod * (1.0 + pick_half(scale_term[None], own))
        sums = jnp.stack([jnp.sum(d_norm, axis=-1), jnp.sum(d_norm * normed_half, axis=-1)])
        sums = (sums + swap(sums)) / model_width
        d_layer = inverse * (d_norm - sums[0][:, None] - normed_half * sums[1][:, None])
        d_half = (pick_half(d_output, own).astype(jnp.float32) + d_layer).astype(
            jnp.bfloat16
        )
        other_half = swap(d_half)
        mine = d_half.reshape(shard_rows, blocks_total, half_rows)
        theirs = other_half.reshape(shard_rows, blocks_total, half_rows)
        joined = jnp.concatenate(
            [jnp.where(own, mine, theirs), jnp.where(own, theirs, mine)], axis=2
        )
        return joined.reshape(shard_rows, model_width), branch_full

    incoming = loss_grad
    grad_input = None
    branch_own = None
    for stage in reversed(range(section_total)):
        d_input, branch_full = section_work(incoming, stage)
        here = section_pos == stage
        grad_input = d_input if grad_input is None else jnp.where(here, d_input, grad_input)
        branch_own = branch_full if branch_own is None else jnp.where(here, branch_full, branch_own)
        incoming = d_input
    out_local = jnp.dot(attn_mixed.T, branch_own, preferred_element_type=jnp.float32)
    out_slice = lax.psum_scatter(out_local, "dp", scatter_dimension=1, tiled=True)
    return (grad_input[None, None], out_slice.astype(jnp.bfloat16)[None])


def solution(mesh):
    in_specs = (
        P("section", "dp", "seq", None),
        P("section", "dp", None, None, "seq"),
        P("section", "dp", None, None),
        P("section", "dp", None, "seq"),
        P("section", "seq", None),
        P("dp"),
        P("dp", "seq", None),
        P("dp", "seq", None),
    )
    out_specs = (P("section", "dp", "seq", None), P("section", "seq", "dp"))
    return jax.shard_map(body, mesh=mesh, in_specs=in_specs, out_specs=out_specs, check_vma=False)
```

```python
import functools
import math

import jax
import jax.numpy as jnp
from jax import lax
from jax.experimental import pallas as pl
from jax.experimental.pallas import tpu as pltpu
from jax.sharding import PartitionSpec as P

HEAD_DIM = 128


def widen(tensor):
    return lax.optimization_barrier(tensor).astype(jnp.float32)


def layer_norm_parts(tokens):
    values = tokens.astype(jnp.float32)
    center = values - jnp.mean(values, axis=-1, keepdims=True)
    variance = jnp.mean(center * center, axis=-1, keepdims=True)
    inverse = lax.rsqrt(variance + 1e-06)
    return (center * inverse, inverse)


def attend_forward(saved_rows, live_keys, head_size):
    row_total = saved_rows.shape[0]
    feature_width = saved_rows.shape[2]
    head_count = feature_width // head_size
    queries = saved_rows[:, 0].reshape(row_total, head_count, head_size).astype(jnp.float32)
    key_rows = saved_rows[:, 1].reshape(row_total, head_count, head_size).astype(jnp.float32)
    value_rows = saved_rows[:, 2].reshape(row_total, head_count, head_size).astype(jnp.float32)
    factor = 1.0 / math.sqrt(head_size)
    scores = jnp.einsum("qhd,khd->hqk", queries, key_rows) * factor
    scores = jnp.where(live_keys[None, None, :], scores, -1e30)
    peak_score = jnp.max(scores, axis=-1, keepdims=True)
    weights = jnp.exp(scores - peak_score)
    weights = weights / jnp.sum(weights, axis=-1, keepdims=True)
    rounded = widen(weights.astype(jnp.bfloat16))
    attn_mixed = jnp.einsum("hqk,khd->qhd", rounded, value_rows).astype(jnp.bfloat16)
    return weights, rounded, attn_mixed


def attend_backward(saved_rows, fwd, d_attn, head_size):
    weights, rounded, attn_mixed = fwd
    row_total = saved_rows.shape[0]
    feature_width = saved_rows.shape[2]
    head_count = feature_width // head_size
    queries = saved_rows[:, 0].reshape(row_total, head_count, head_size).astype(jnp.float32)
    key_rows = saved_rows[:, 1].reshape(row_total, head_count, head_size).astype(jnp.float32)
    value_rows = saved_rows[:, 2].reshape(row_total, head_count, head_size).astype(jnp.float32)
    factor = 1.0 / math.sqrt(head_size)
    upstream = d_attn.reshape(row_total, head_count, head_size).astype(jnp.float32)
    d_weights = jnp.einsum("qhd,khd->hqk", upstream, value_rows)
    delta_rows = jnp.einsum("qhd,qhd->hq", upstream, widen(attn_mixed))
    d_scores = widen((weights * (d_weights - delta_rows[:, :, None]) * factor).astype(jnp.bfloat16))
    grad_q = jnp.einsum("hqk,khd->qhd", d_scores, key_rows).astype(jnp.bfloat16)
    grad_k = jnp.einsum("hqk,qhd->khd", d_scores, queries).astype(jnp.bfloat16)
    grad_v = jnp.einsum("hqk,qhd->khd", rounded, upstream).astype(jnp.bfloat16)
    stacked = jnp.stack([grad_q, grad_k, grad_v], axis=1).reshape(row_total, 3 * feature_width)
    return stacked


RING = ("section", "seq")


def shift_pairs(stage, count, step):
    base = stage * count
    return [(base + pos, base + (pos + step) % count) for pos in range(count)]


def gather_ring(shard, stage, count):
    half = shard.shape[0] // 2
    from_left = lax.ppermute(shard, RING, shift_pairs(stage, count, 1))
    from_right = lax.ppermute(shard, RING, shift_pairs(stage, count, -1))
    far_top = lax.ppermute(from_left[:half], RING, shift_pairs(stage, count, 1))
    far_bottom = lax.ppermute(from_right[half:], RING, shift_pairs(stage, count, -1))
    far = jnp.concatenate([far_top, far_bottom], axis=0)
    return jnp.concatenate([shard, from_right, far, from_left], axis=0)


MESH_ID = pl.DeviceIdType.MESH


def ring_gather_kernel(stage, count, x_ref, o_ref, send_sem, recv_sem, own_sem):
    rows = x_ref.shape[0]
    half = rows // 2
    pos = lax.axis_index("seq")
    dp_pos = lax.axis_index("dp")

    @pl.when(lax.axis_index("section") == stage)
    def _():
        right = lax.rem(pos + 1, count)
        left = lax.rem(pos + count - 1, count)
        barrier = pltpu.get_barrier_semaphore()
        for neighbour in (left, right):
            pl.semaphore_signal(
                barrier, inc=1, device_id=(stage, neighbour, dp_pos), device_id_type=MESH_ID
            )
        pl.semaphore_wait(barrier, 2)
        own = pltpu.make_async_copy(x_ref, o_ref.at[pl.ds(0, rows)], own_sem)
        own.start()

        def remote(src, dst, slot, target):
            return pltpu.make_async_remote_copy(
                src_ref=src,
                dst_ref=dst,
                send_sem=send_sem.at[slot],
                recv_sem=recv_sem.at[slot],
                device_id=(stage, target, dp_pos),
                device_id_type=MESH_ID,
            )

        to_right = remote(x_ref, o_ref.at[pl.ds(3 * rows, rows)], 0, right)
        to_left = remote(x_ref, o_ref.at[pl.ds(rows, rows)], 1, left)
        to_right.start()
        to_left.start()
        to_right.wait()
        to_left.wait()
        relay_right = remote(
            o_ref.at[pl.ds(3 * rows, half)], o_ref.at[pl.ds(2 * rows, half)], 2, right
        )
        relay_left = remote(
            o_ref.at[pl.ds(rows + half, half)], o_ref.at[pl.ds(2 * rows + half, half)], 3, left
        )
        relay_right.start()
        relay_left.start()
        relay_right.wait()
        relay_left.wait()
        own.wait()


def ring_gather(shard, stage, count):
    rows, width = shard.shape
    return pl.pallas_call(
        functools.partial(ring_gather_kernel, stage, count),
        out_shape=jax.ShapeDtypeStruct((count * rows, width), shard.dtype),
        in_specs=[pl.BlockSpec(memory_space=pl.ANY)],
        out_specs=pl.BlockSpec(memory_space=pl.ANY),
        scratch_shapes=[
            pltpu.SemaphoreType.DMA((4,)),
            pltpu.SemaphoreType.DMA((4,)),
            pltpu.SemaphoreType.DMA(()),
        ],
        compiler_params=pltpu.CompilerParams(collective_id=stage, has_side_effects=True),
    )(shard)


def reduce_ring(partial, stage, count):
    rows = partial.shape[0] // count
    half = rows // 2
    blocks = [partial[k * rows : (k + 1) * rows] for k in range(count)]
    low = lambda value: value.astype(jnp.bfloat16)
    first_right = lax.ppermute(low(blocks[2][:half]), RING, shift_pairs(stage, count, 1))
    first_left = lax.ppermute(low(blocks[2][half:]), RING, shift_pairs(stage, count, -1))
    to_right = jnp.concatenate(
        [first_right.astype(jnp.float32) + blocks[1][:half], blocks[1][half:]], axis=0
    )
    to_left = jnp.concatenate(
        [blocks[3][:half], first_left.astype(jnp.float32) + blocks[3][half:]], axis=0
    )
    got_left = lax.ppermute(low(to_right), RING, shift_pairs(stage, count, 1))
    got_right = lax.ppermute(low(to_left), RING, shift_pairs(stage, count, -1))
    return blocks[0] + got_left.astype(jnp.float32) + got_right.astype(jnp.float32)


def swap(value):
    return lax.ppermute(value, "section", [(0, 1), (1, 0)])


def seq_pairs(count, step):
    return [(pos, (pos + step) % count) for pos in range(count)]


def reduce_seq(partial, count):
    rows = partial.shape[0] // count
    half = rows // 2
    blocks = [partial[k * rows : (k + 1) * rows] for k in range(count)]
    low = lambda value: value.astype(jnp.bfloat16)
    first_right = lax.ppermute(low(blocks[2][:half]), "seq", seq_pairs(count, 1))
    first_left = lax.ppermute(low(blocks[2][half:]), "seq", seq_pairs(count, -1))
    to_right = jnp.concatenate(
        [first_right.astype(jnp.float32) + blocks[1][:half], blocks[1][half:]], axis=0
    )
    to_left = jnp.concatenate(
        [blocks[3][:half], first_left.astype(jnp.float32) + blocks[3][half:]], axis=0
    )
    got_left = lax.ppermute(low(to_right), "seq", seq_pairs(count, 1))
    got_right = lax.ppermute(low(to_left), "seq", seq_pairs(count, -1))
    return blocks[0] + got_left.astype(jnp.float32) + got_right.astype(jnp.float32)


def body(section_input, saved_qkv, modulation, w_qkv, w_out, lengths, student_out, teacher_target):
    section_total = lax.axis_size("section")
    section_pos = lax.axis_index("section")
    seq_total = lax.axis_size("seq")
    seq_pos = lax.axis_index("seq")
    inputs = section_input[0, 0]
    saved_rows = saved_qkv[0, 0]
    weight_out = w_out[0]
    shard_rows, model_width = inputs.shape
    capacity = saved_rows.shape[0]
    local_width = saved_rows.shape[2]
    live_length = lengths[0]
    w_local = w_qkv[0]
    block_rows = w_local.shape[0]
    half_rows = block_rows // 2
    blocks_total = model_width // block_rows

    other_inputs = swap(inputs)
    other_mods = swap(modulation[0, 0])
    other_w = swap(w_local)
    parts = {}
    for stage in range(section_total):
        own = section_pos == stage
        x_stage = jnp.where(own, inputs, other_inputs)
        mods_stage = jnp.where(own, modulation[0, 0], other_mods)
        parts[stage] = (layer_norm_parts(x_stage), mods_stage)

    weights_of = {}
    for stage in reversed(range(section_total)):
        own = section_pos == stage
        contribution = jnp.where(own, w_local[:half_rows], other_w[half_rows:])
        weights_of[stage] = lax.all_gather(contribution, "dp", axis=0, tiled=True).reshape(
            blocks_total * half_rows, 3 * local_width
        )

    positions = seq_pos * shard_rows + jnp.arange(shard_rows, dtype=jnp.int32)
    row_live = positions < live_length
    gap = student_out[0].astype(jnp.float32) - teacher_target[0].astype(jnp.float32)
    loss_grad = jnp.where(row_live[:, None], gap, 0.0).astype(jnp.bfloat16)
    order = (seq_pos + jnp.arange(seq_total, dtype=jnp.int32)) % seq_total
    token_order = (order[:, None] * shard_rows + jnp.arange(shard_rows, dtype=jnp.int32)).reshape(-1)
    saved_off = jnp.take(saved_rows, token_order, axis=0)
    live_keys = token_order < live_length
    fwd = attend_forward(saved_off, live_keys, HEAD_DIM)
    attn_mixed = fwd[2].reshape(capacity, local_width)
    attn_mixed_t = lax.optimization_barrier(attn_mixed.T)

    def pick_half(value, own):
        split = value.reshape(value.shape[0], blocks_total, block_rows)
        chosen = jnp.where(own, split[:, :, :half_rows], split[:, :, half_rows:])
        return chosen.reshape(value.shape[0], blocks_total * half_rows)

    def section_work(d_output, stage):
        own = section_pos == stage
        (normed, inverse), mods_stage = parts[stage]
        scale_term = mods_stage[0]
        gate_term = mods_stage[1]
        d_branch = (gate_term * d_output.astype(jnp.float32)).astype(jnp.bfloat16)
        if stage == section_total - 1:
            branch_full = gather_ring(d_branch, stage, seq_total)
        else:
            branch_full = ring_gather(d_branch, stage, seq_total)
        d_attn = jnp.dot(branch_full, weight_out.T, preferred_element_type=jnp.float32).astype(
            jnp.bfloat16
        )
        own_grads = attend_backward(saved_off, fwd, d_attn, HEAD_DIM)
        handed = lax.ppermute(own_grads, "section", [(stage, 1 - stage)])
        flat_grads = jnp.where(own, own_grads, handed)
        d_mod_part = jnp.dot(flat_grads, weights_of[stage].T, preferred_element_type=jnp.float32)
        d_mod = reduce_seq(d_mod_part, seq_total)
        normed_half = pick_half(normed, own)
        d_norm = d_mod * (1.0 + pick_half(scale_term[None], own))
        sums = jnp.stack([jnp.sum(d_norm, axis=-1), jnp.sum(d_norm * normed_half, axis=-1)])
        sums = (sums + swap(sums)) / model_width
        d_layer = inverse * (d_norm - sums[0][:, None] - normed_half * sums[1][:, None])
        d_half = (pick_half(d_output, own).astype(jnp.float32) + d_layer).astype(
            jnp.bfloat16
        )
        other_half = swap(d_half)
        mine = d_half.reshape(shard_rows, blocks_total, half_rows)
        theirs = other_half.reshape(shard_rows, blocks_total, half_rows)
        joined = jnp.concatenate(
            [jnp.where(own, mine, theirs), jnp.where(own, theirs, mine)], axis=2
        )
        return joined.reshape(shard_rows, model_width), branch_full

    incoming = loss_grad
    grad_input = None
    branch_own = None
    for stage in reversed(range(section_total)):
        d_input, branch_full = section_work(incoming, stage)
        here = section_pos == stage
        grad_input = d_input if grad_input is None else jnp.where(here, d_input, grad_input)
        branch_own = branch_full if branch_own is None else jnp.where(here, branch_full, branch_own)
        incoming = d_input
    out_local = jnp.dot(attn_mixed_t, branch_own, preferred_element_type=jnp.float32)
    out_slice = lax.psum_scatter(out_local, "dp", scatter_dimension=1, tiled=True)
    return (grad_input[None, None], out_slice.astype(jnp.bfloat16)[None])


def solution(mesh):
    in_specs = (
        P("section", "dp", "seq", None),
        P("section", "dp", None, None, "seq"),
        P("section", "dp", None, None),
        P("section", "dp", None, "seq"),
        P("section", "seq", None),
        P("dp"),
        P("dp", "seq", None),
        P("dp", "seq", None),
    )
    out_specs = (P("section", "dp", "seq", None), P("section", "seq", "dp"))
    return jax.shard_map(body, mesh=mesh, in_specs=in_specs, out_specs=out_specs, check_vma=False)
```

```python
import functools
import math

import jax
import jax.numpy as jnp
from jax import lax
from jax.experimental import pallas as pl
from jax.experimental.pallas import tpu as pltpu
from jax.sharding import PartitionSpec as P

HEAD_DIM = 128


def widen(tensor):
    return lax.optimization_barrier(tensor).astype(jnp.float32)


def layer_norm_parts(tokens):
    values = tokens.astype(jnp.float32)
    center = values - jnp.mean(values, axis=-1, keepdims=True)
    variance = jnp.mean(center * center, axis=-1, keepdims=True)
    inverse = lax.rsqrt(variance + 1e-06)
    return (center * inverse, inverse)


def attend_forward(saved_rows, live_keys, head_size):
    row_total = saved_rows.shape[0]
    feature_width = saved_rows.shape[2]
    head_count = feature_width // head_size
    queries = saved_rows[:, 0].reshape(row_total, head_count, head_size).astype(jnp.float32)
    key_rows = saved_rows[:, 1].reshape(row_total, head_count, head_size).astype(jnp.float32)
    value_rows = saved_rows[:, 2].reshape(row_total, head_count, head_size).astype(jnp.float32)
    factor = 1.0 / math.sqrt(head_size)
    scores = jnp.einsum("qhd,khd->hqk", queries, key_rows) * factor
    scores = jnp.where(live_keys[None, None, :], scores, -1e30)
    peak_score = jnp.max(scores, axis=-1, keepdims=True)
    weights = jnp.exp(scores - peak_score)
    weights = weights / jnp.sum(weights, axis=-1, keepdims=True)
    rounded = widen(weights.astype(jnp.bfloat16))
    attn_mixed = jnp.einsum("hqk,khd->qhd", rounded, value_rows).astype(jnp.bfloat16)
    return weights, rounded, attn_mixed


def attend_backward(saved_rows, fwd, d_attn, head_size):
    weights, rounded, attn_mixed = fwd
    row_total = saved_rows.shape[0]
    feature_width = saved_rows.shape[2]
    head_count = feature_width // head_size
    queries = saved_rows[:, 0].reshape(row_total, head_count, head_size).astype(jnp.float32)
    key_rows = saved_rows[:, 1].reshape(row_total, head_count, head_size).astype(jnp.float32)
    value_rows = saved_rows[:, 2].reshape(row_total, head_count, head_size).astype(jnp.float32)
    factor = 1.0 / math.sqrt(head_size)
    upstream = d_attn.reshape(row_total, head_count, head_size).astype(jnp.float32)
    d_weights = jnp.einsum("qhd,khd->hqk", upstream, value_rows)
    delta_rows = jnp.einsum("qhd,qhd->hq", upstream, widen(attn_mixed))
    d_scores = widen((weights * (d_weights - delta_rows[:, :, None]) * factor).astype(jnp.bfloat16))
    grad_q = jnp.einsum("hqk,khd->qhd", d_scores, key_rows).astype(jnp.bfloat16)
    grad_k = jnp.einsum("hqk,qhd->khd", d_scores, queries).astype(jnp.bfloat16)
    grad_v = jnp.einsum("hqk,qhd->khd", rounded, upstream).astype(jnp.bfloat16)
    stacked = jnp.stack([grad_q, grad_k, grad_v], axis=1).reshape(row_total, 3 * feature_width)
    return stacked


RING = ("section", "seq")


def shift_pairs(stage, count, step):
    base = stage * count
    return [(base + pos, base + (pos + step) % count) for pos in range(count)]


def gather_ring(shard, stage, count):
    half = shard.shape[0] // 2
    from_left = lax.ppermute(shard, RING, shift_pairs(stage, count, 1))
    from_right = lax.ppermute(shard, RING, shift_pairs(stage, count, -1))
    far_top = lax.ppermute(from_left[:half], RING, shift_pairs(stage, count, 1))
    far_bottom = lax.ppermute(from_right[half:], RING, shift_pairs(stage, count, -1))
    far = jnp.concatenate([far_top, far_bottom], axis=0)
    return jnp.concatenate([shard, from_right, far, from_left], axis=0)


MESH_ID = pl.DeviceIdType.MESH


def ring_gather_kernel(stage, count, x_ref, o_ref, send_sem, recv_sem, own_sem):
    rows = x_ref.shape[0]
    half = rows // 2
    pos = lax.axis_index("seq")
    dp_pos = lax.axis_index("dp")

    @pl.when(lax.axis_index("section") == stage)
    def _():
        right = lax.rem(pos + 1, count)
        left = lax.rem(pos + count - 1, count)
        barrier = pltpu.get_barrier_semaphore()
        for neighbour in (left, right):
            pl.semaphore_signal(
                barrier, inc=1, device_id=(stage, neighbour, dp_pos), device_id_type=MESH_ID
            )
        pl.semaphore_wait(barrier, 2)
        own = pltpu.make_async_copy(x_ref, o_ref.at[pl.ds(0, rows)], own_sem)
        own.start()

        def remote(src, dst, slot, target):
            return pltpu.make_async_remote_copy(
                src_ref=src,
                dst_ref=dst,
                send_sem=send_sem.at[slot],
                recv_sem=recv_sem.at[slot],
                device_id=(stage, target, dp_pos),
                device_id_type=MESH_ID,
            )

        to_right = remote(x_ref, o_ref.at[pl.ds(3 * rows, rows)], 0, right)
        to_left = remote(x_ref, o_ref.at[pl.ds(rows, rows)], 1, left)
        to_right.start()
        to_left.start()
        to_right.wait()
        to_left.wait()
        relay_right = remote(
            o_ref.at[pl.ds(3 * rows, half)], o_ref.at[pl.ds(2 * rows, half)], 2, right
        )
        relay_left = remote(
            o_ref.at[pl.ds(rows + half, half)], o_ref.at[pl.ds(2 * rows + half, half)], 3, left
        )
        relay_right.start()
        relay_left.start()
        relay_right.wait()
        relay_left.wait()
        own.wait()


def ring_gather(shard, stage, count):
    rows, width = shard.shape
    return pl.pallas_call(
        functools.partial(ring_gather_kernel, stage, count),
        out_shape=jax.ShapeDtypeStruct((count * rows, width), shard.dtype),
        in_specs=[pl.BlockSpec(memory_space=pl.ANY)],
        out_specs=pl.BlockSpec(memory_space=pl.ANY),
        scratch_shapes=[
            pltpu.SemaphoreType.DMA((4,)),
            pltpu.SemaphoreType.DMA((4,)),
            pltpu.SemaphoreType.DMA(()),
        ],
        compiler_params=pltpu.CompilerParams(collective_id=stage, has_side_effects=True),
    )(shard)


def reduce_ring(partial, stage, count):
    rows = partial.shape[0] // count
    half = rows // 2
    blocks = [partial[k * rows : (k + 1) * rows] for k in range(count)]
    low = lambda value: value.astype(jnp.bfloat16)
    first_right = lax.ppermute(low(blocks[2][:half]), RING, shift_pairs(stage, count, 1))
    first_left = lax.ppermute(low(blocks[2][half:]), RING, shift_pairs(stage, count, -1))
    to_right = jnp.concatenate(
        [first_right.astype(jnp.float32) + blocks[1][:half], blocks[1][half:]], axis=0
    )
    to_left = jnp.concatenate(
        [blocks[3][:half], first_left.astype(jnp.float32) + blocks[3][half:]], axis=0
    )
    got_left = lax.ppermute(low(to_right), RING, shift_pairs(stage, count, 1))
    got_right = lax.ppermute(low(to_left), RING, shift_pairs(stage, count, -1))
    return blocks[0] + got_left.astype(jnp.float32) + got_right.astype(jnp.float32)


def swap(value):
    return lax.ppermute(value, "section", [(0, 1), (1, 0)])


def seq_pairs(count, step):
    return [(pos, (pos + step) % count) for pos in range(count)]


def reduce_seq(partial, count):
    rows = partial.shape[0] // count
    half = rows // 2
    blocks = [partial[k * rows : (k + 1) * rows] for k in range(count)]
    low = lambda value: value.astype(jnp.bfloat16)
    first_right = lax.ppermute(low(blocks[2][:half]), "seq", seq_pairs(count, 1))
    first_left = lax.ppermute(low(blocks[2][half:]), "seq", seq_pairs(count, -1))
    to_right = jnp.concatenate(
        [first_right.astype(jnp.float32) + blocks[1][:half], blocks[1][half:]], axis=0
    )
    to_left = jnp.concatenate(
        [blocks[3][:half], first_left.astype(jnp.float32) + blocks[3][half:]], axis=0
    )
    got_left = lax.ppermute(low(to_right), "seq", seq_pairs(count, 1))
    got_right = lax.ppermute(low(to_left), "seq", seq_pairs(count, -1))
    return blocks[0] + got_left.astype(jnp.float32) + got_right.astype(jnp.float32)


def body(section_input, saved_qkv, modulation, w_qkv, w_out, lengths, student_out, teacher_target):
    section_total = lax.axis_size("section")
    section_pos = lax.axis_index("section")
    seq_total = lax.axis_size("seq")
    seq_pos = lax.axis_index("seq")
    inputs = section_input[0, 0]
    saved_rows = saved_qkv[0, 0]
    weight_out = w_out[0]
    shard_rows, model_width = inputs.shape
    capacity = saved_rows.shape[0]
    local_width = saved_rows.shape[2]
    live_length = lengths[0]
    w_local = w_qkv[0]
    block_rows = w_local.shape[0]
    half_rows = block_rows // 2
    blocks_total = model_width // block_rows

    other_inputs = swap(inputs)
    other_mods = swap(modulation[0, 0])
    other_w = swap(w_local)
    parts = {}
    for stage in range(section_total):
        own = section_pos == stage
        x_stage = jnp.where(own, inputs, other_inputs)
        mods_stage = jnp.where(own, modulation[0, 0], other_mods)
        parts[stage] = (layer_norm_parts(x_stage), mods_stage)

    weights_of = {}
    for stage in reversed(range(section_total)):
        own = section_pos == stage
        contribution = jnp.where(own, w_local[:half_rows], other_w[half_rows:])
        weights_of[stage] = lax.all_gather(contribution, "dp", axis=0, tiled=True).reshape(
            blocks_total * half_rows, 3 * local_width
        )

    positions = seq_pos * shard_rows + jnp.arange(shard_rows, dtype=jnp.int32)
    row_live = positions < live_length
    gap = student_out[0].astype(jnp.float32) - teacher_target[0].astype(jnp.float32)
    loss_grad = jnp.where(row_live[:, None], gap, 0.0).astype(jnp.bfloat16)
    order = (seq_pos + jnp.arange(seq_total, dtype=jnp.int32)) % seq_total
    token_order = (order[:, None] * shard_rows + jnp.arange(shard_rows, dtype=jnp.int32)).reshape(-1)
    saved_off = jnp.take(saved_rows, token_order, axis=0)
    live_keys = token_order < live_length
    fwd = attend_forward(saved_off, live_keys, HEAD_DIM)
    attn_mixed = fwd[2].reshape(capacity, local_width)
    attn_mixed_t = lax.optimization_barrier(attn_mixed.T)

    def pick_half(value, own):
        split = value.reshape(value.shape[0], blocks_total, block_rows)
        chosen = jnp.where(own, split[:, :, :half_rows], split[:, :, half_rows:])
        return chosen.reshape(value.shape[0], blocks_total * half_rows)

    def section_work(d_output, stage):
        own = section_pos == stage
        (normed, inverse), mods_stage = parts[stage]
        scale_term = mods_stage[0]
        gate_term = mods_stage[1]
        d_branch = (gate_term * d_output.astype(jnp.float32)).astype(jnp.bfloat16)
        if stage == section_total - 1:
            branch_full = gather_ring(d_branch, stage, seq_total)
        else:
            branch_full = ring_gather(d_branch, stage, seq_total)
        d_attn = jnp.dot(branch_full, weight_out.T, preferred_element_type=jnp.float32).astype(
            jnp.bfloat16
        )
        own_grads = attend_backward(saved_off, fwd, d_attn, HEAD_DIM)
        handed = lax.ppermute(own_grads, "section", [(stage, 1 - stage)])
        flat_grads = jnp.where(own, own_grads, handed)
        d_mod_part = jnp.dot(flat_grads, weights_of[stage].T, preferred_element_type=jnp.float32)
        d_mod = reduce_seq(d_mod_part, seq_total)
        normed_half = pick_half(normed, own)
        d_norm = d_mod * (1.0 + pick_half(scale_term[None], own))
        sums = jnp.stack([jnp.sum(d_norm, axis=-1), jnp.sum(d_norm * normed_half, axis=-1)])
        sums = (sums + swap(sums)) / model_width
        d_layer = inverse * (d_norm - sums[0][:, None] - normed_half * sums[1][:, None])
        d_half = (pick_half(d_output, own).astype(jnp.float32) + d_layer).astype(
            jnp.bfloat16
        )
        other_half = swap(d_half)
        mine = d_half.reshape(shard_rows, blocks_total, half_rows)
        theirs = other_half.reshape(shard_rows, blocks_total, half_rows)
        joined = jnp.concatenate(
            [jnp.where(own, mine, theirs), jnp.where(own, theirs, mine)], axis=2
        )
        return joined.reshape(shard_rows, model_width), branch_full

    incoming = loss_grad
    grad_input = None
    branch_own = None
    for stage in reversed(range(section_total)):
        d_input, branch_full = section_work(incoming, stage)
        here = section_pos == stage
        grad_input = d_input if grad_input is None else jnp.where(here, d_input, grad_input)
        branch_own = branch_full if branch_own is None else jnp.where(here, branch_full, branch_own)
        incoming = d_input
    out_local = jnp.dot(attn_mixed_t, branch_own, preferred_element_type=jnp.float32)
    out_slice = lax.psum_scatter(
        out_local.astype(jnp.bfloat16), "dp", scatter_dimension=1, tiled=True
    )
    return (grad_input[None, None], out_slice[None])


def solution(mesh):
    in_specs = (
        P("section", "dp", "seq", None),
        P("section", "dp", None, None, "seq"),
        P("section", "dp", None, None),
        P("section", "dp", None, "seq"),
        P("section", "seq", None),
        P("dp"),
        P("dp", "seq", None),
        P("dp", "seq", None),
    )
    out_specs = (P("section", "dp", "seq", None), P("section", "seq", "dp"))
    return jax.shard_map(body, mesh=mesh, in_specs=in_specs, out_specs=out_specs, check_vma=False)
```

```python
import functools
import math

import jax
import jax.numpy as jnp
from jax import lax
from jax.experimental import pallas as pl
from jax.experimental.pallas import tpu as pltpu
from jax.sharding import PartitionSpec as P

HEAD_DIM = 128


def widen(tensor):
    return lax.optimization_barrier(tensor).astype(jnp.float32)


def layer_norm_parts(tokens):
    values = tokens.astype(jnp.float32)
    center = values - jnp.mean(values, axis=-1, keepdims=True)
    variance = jnp.mean(center * center, axis=-1, keepdims=True)
    inverse = lax.rsqrt(variance + 1e-06)
    return (center * inverse, inverse)


def attend_forward(saved_rows, live_keys, head_size):
    row_total = saved_rows.shape[0]
    feature_width = saved_rows.shape[2]
    head_count = feature_width // head_size
    queries = saved_rows[:, 0].reshape(row_total, head_count, head_size).astype(jnp.float32)
    key_rows = saved_rows[:, 1].reshape(row_total, head_count, head_size).astype(jnp.float32)
    value_rows = saved_rows[:, 2].reshape(row_total, head_count, head_size).astype(jnp.float32)
    factor = 1.0 / math.sqrt(head_size)
    scores = jnp.einsum("qhd,khd->hqk", queries, key_rows) * factor
    scores = jnp.where(live_keys[None, None, :], scores, -1e30)
    peak_score = jnp.max(scores, axis=-1, keepdims=True)
    weights = jnp.exp(scores - peak_score)
    weights = weights / jnp.sum(weights, axis=-1, keepdims=True)
    rounded = widen(weights.astype(jnp.bfloat16))
    attn_mixed = jnp.einsum("hqk,khd->qhd", rounded, value_rows).astype(jnp.bfloat16)
    return weights, rounded, attn_mixed


def attend_backward(saved_rows, fwd, d_attn, head_size):
    weights, rounded, attn_mixed = fwd
    row_total = saved_rows.shape[0]
    feature_width = saved_rows.shape[2]
    head_count = feature_width // head_size
    queries = saved_rows[:, 0].reshape(row_total, head_count, head_size).astype(jnp.float32)
    key_rows = saved_rows[:, 1].reshape(row_total, head_count, head_size).astype(jnp.float32)
    value_rows = saved_rows[:, 2].reshape(row_total, head_count, head_size).astype(jnp.float32)
    factor = 1.0 / math.sqrt(head_size)
    upstream = d_attn.reshape(row_total, head_count, head_size).astype(jnp.float32)
    d_weights = jnp.einsum("qhd,khd->hqk", upstream, value_rows)
    delta_rows = jnp.einsum("qhd,qhd->hq", upstream, widen(attn_mixed))
    d_scores = widen((weights * (d_weights - delta_rows[:, :, None]) * factor).astype(jnp.bfloat16))
    grad_q = jnp.einsum("hqk,khd->qhd", d_scores, key_rows).astype(jnp.bfloat16)
    grad_k = jnp.einsum("hqk,qhd->khd", d_scores, queries).astype(jnp.bfloat16)
    grad_v = jnp.einsum("hqk,qhd->khd", rounded, upstream).astype(jnp.bfloat16)
    stacked = jnp.stack([grad_q, grad_k, grad_v], axis=1).reshape(row_total, 3 * feature_width)
    return stacked


RING = ("section", "seq")


def shift_pairs(stage, count, step):
    base = stage * count
    return [(base + pos, base + (pos + step) % count) for pos in range(count)]


def gather_ring(shard, stage, count):
    half = shard.shape[0] // 2
    from_left = lax.ppermute(shard, RING, shift_pairs(stage, count, 1))
    from_right = lax.ppermute(shard, RING, shift_pairs(stage, count, -1))
    far_top = lax.ppermute(from_left[:half], RING, shift_pairs(stage, count, 1))
    far_bottom = lax.ppermute(from_right[half:], RING, shift_pairs(stage, count, -1))
    far = jnp.concatenate([far_top, far_bottom], axis=0)
    return jnp.concatenate([shard, from_right, far, from_left], axis=0)


MESH_ID = pl.DeviceIdType.MESH


def ring_gather_kernel(stage, count, x_ref, o_ref, send_sem, recv_sem, own_sem):
    rows = x_ref.shape[0]
    half = rows // 2
    pos = lax.axis_index("seq")
    dp_pos = lax.axis_index("dp")

    @pl.when(lax.axis_index("section") == stage)
    def _():
        right = lax.rem(pos + 1, count)
        left = lax.rem(pos + count - 1, count)
        barrier = pltpu.get_barrier_semaphore()
        for neighbour in (left, right):
            pl.semaphore_signal(
                barrier, inc=1, device_id=(stage, neighbour, dp_pos), device_id_type=MESH_ID
            )
        pl.semaphore_wait(barrier, 2)
        own = pltpu.make_async_copy(x_ref, o_ref.at[pl.ds(0, rows)], own_sem)
        own.start()

        def remote(src, dst, slot, target):
            return pltpu.make_async_remote_copy(
                src_ref=src,
                dst_ref=dst,
                send_sem=send_sem.at[slot],
                recv_sem=recv_sem.at[slot],
                device_id=(stage, target, dp_pos),
                device_id_type=MESH_ID,
            )

        to_right = remote(x_ref, o_ref.at[pl.ds(3 * rows, rows)], 0, right)
        to_left = remote(x_ref, o_ref.at[pl.ds(rows, rows)], 1, left)
        to_right.start()
        to_left.start()
        to_right.wait()
        to_left.wait()
        relay_right = remote(
            o_ref.at[pl.ds(3 * rows, half)], o_ref.at[pl.ds(2 * rows, half)], 2, right
        )
        relay_left = remote(
            o_ref.at[pl.ds(rows + half, half)], o_ref.at[pl.ds(2 * rows + half, half)], 3, left
        )
        relay_right.start()
        relay_left.start()
        relay_right.wait()
        relay_left.wait()
        own.wait()


def ring_gather(shard, stage, count):
    rows, width = shard.shape
    return pl.pallas_call(
        functools.partial(ring_gather_kernel, stage, count),
        out_shape=jax.ShapeDtypeStruct((count * rows, width), shard.dtype),
        in_specs=[pl.BlockSpec(memory_space=pl.ANY)],
        out_specs=pl.BlockSpec(memory_space=pl.ANY),
        scratch_shapes=[
            pltpu.SemaphoreType.DMA((4,)),
            pltpu.SemaphoreType.DMA((4,)),
            pltpu.SemaphoreType.DMA(()),
        ],
        compiler_params=pltpu.CompilerParams(collective_id=stage, has_side_effects=True),
    )(shard)


def reduce_ring(partial, stage, count):
    rows = partial.shape[0] // count
    half = rows // 2
    blocks = [partial[k * rows : (k + 1) * rows] for k in range(count)]
    low = lambda value: value.astype(jnp.bfloat16)
    first_right = lax.ppermute(low(blocks[2][:half]), RING, shift_pairs(stage, count, 1))
    first_left = lax.ppermute(low(blocks[2][half:]), RING, shift_pairs(stage, count, -1))
    to_right = jnp.concatenate(
        [first_right.astype(jnp.float32) + blocks[1][:half], blocks[1][half:]], axis=0
    )
    to_left = jnp.concatenate(
        [blocks[3][:half], first_left.astype(jnp.float32) + blocks[3][half:]], axis=0
    )
    got_left = lax.ppermute(low(to_right), RING, shift_pairs(stage, count, 1))
    got_right = lax.ppermute(low(to_left), RING, shift_pairs(stage, count, -1))
    return blocks[0] + got_left.astype(jnp.float32) + got_right.astype(jnp.float32)


def swap(value):
    return lax.ppermute(value, "section", [(0, 1), (1, 0)])


def seq_pairs(count, step):
    return [(pos, (pos + step) % count) for pos in range(count)]


def reduce_seq(partial, count):
    rows = partial.shape[0] // count
    half = rows // 2
    blocks = [partial[k * rows : (k + 1) * rows] for k in range(count)]
    low = lambda value: value.astype(jnp.bfloat16)
    first_right = lax.ppermute(low(blocks[2][:half]), "seq", seq_pairs(count, 1))
    first_left = lax.ppermute(low(blocks[2][half:]), "seq", seq_pairs(count, -1))
    to_right = jnp.concatenate(
        [first_right.astype(jnp.float32) + blocks[1][:half], blocks[1][half:]], axis=0
    )
    to_left = jnp.concatenate(
        [blocks[3][:half], first_left.astype(jnp.float32) + blocks[3][half:]], axis=0
    )
    got_left = lax.ppermute(low(to_right), "seq", seq_pairs(count, 1))
    got_right = lax.ppermute(low(to_left), "seq", seq_pairs(count, -1))
    return blocks[0] + got_left.astype(jnp.float32) + got_right.astype(jnp.float32)


def body(section_input, saved_qkv, modulation, w_qkv, w_out, lengths, student_out, teacher_target):
    section_total = lax.axis_size("section")
    section_pos = lax.axis_index("section")
    seq_total = lax.axis_size("seq")
    seq_pos = lax.axis_index("seq")
    inputs = section_input[0, 0]
    saved_rows = saved_qkv[0, 0]
    weight_out = w_out[0]
    shard_rows, model_width = inputs.shape
    capacity = saved_rows.shape[0]
    local_width = saved_rows.shape[2]
    live_length = lengths[0]
    w_local = w_qkv[0]
    block_rows = w_local.shape[0]
    half_rows = block_rows // 2
    blocks_total = model_width // block_rows

    other_inputs = swap(inputs)
    other_mods = swap(modulation[0, 0])
    other_w = swap(w_local)
    parts = {}
    for stage in range(section_total):
        own = section_pos == stage
        x_stage = jnp.where(own, inputs, other_inputs)
        mods_stage = jnp.where(own, modulation[0, 0], other_mods)
        parts[stage] = (layer_norm_parts(x_stage), mods_stage)

    weights_of = {}
    for stage in reversed(range(section_total)):
        own = section_pos == stage
        contribution = jnp.where(own, w_local[:half_rows], other_w[half_rows:])
        weights_of[stage] = lax.all_gather(contribution, "dp", axis=0, tiled=True).reshape(
            blocks_total * half_rows, 3 * local_width
        )

    positions = seq_pos * shard_rows + jnp.arange(shard_rows, dtype=jnp.int32)
    row_live = positions < live_length
    gap = student_out[0].astype(jnp.float32) - teacher_target[0].astype(jnp.float32)
    loss_grad = jnp.where(row_live[:, None], gap, 0.0).astype(jnp.bfloat16)
    order = (seq_pos + jnp.arange(seq_total, dtype=jnp.int32)) % seq_total
    token_order = (order[:, None] * shard_rows + jnp.arange(shard_rows, dtype=jnp.int32)).reshape(-1)
    saved_off = jnp.take(saved_rows, token_order, axis=0)
    live_keys = token_order < live_length
    fwd = attend_forward(saved_off, live_keys, HEAD_DIM)
    attn_mixed = fwd[2].reshape(capacity, local_width)
    attn_mixed_t = lax.optimization_barrier(attn_mixed.T)

    def pick_half(value, own):
        split = value.reshape(value.shape[0], blocks_total, block_rows)
        chosen = jnp.where(own, split[:, :, :half_rows], split[:, :, half_rows:])
        return chosen.reshape(value.shape[0], blocks_total * half_rows)

    def section_work(d_output, stage):
        own = section_pos == stage
        (normed, inverse), mods_stage = parts[stage]
        scale_term = mods_stage[0]
        gate_term = mods_stage[1]
        d_branch = (gate_term * d_output.astype(jnp.float32)).astype(jnp.bfloat16)
        if stage == section_total - 1:
            branch_full = gather_ring(d_branch, stage, seq_total)
        else:
            branch_full = ring_gather(d_branch, stage, seq_total)
        d_attn = jnp.dot(branch_full, weight_out.T, preferred_element_type=jnp.float32).astype(
            jnp.bfloat16
        )
        own_grads = attend_backward(saved_off, fwd, d_attn, HEAD_DIM)
        handed = lax.ppermute(own_grads, "section", [(stage, 1 - stage)])
        flat_grads = jnp.where(own, own_grads, handed)
        d_mod_part = jnp.dot(flat_grads, weights_of[stage].T, preferred_element_type=jnp.float32)
        d_mod = reduce_seq(d_mod_part, seq_total)
        normed_half = pick_half(normed, own)
        d_norm = d_mod * (1.0 + pick_half(scale_term[None], own))
        sums = jnp.stack([jnp.sum(d_norm, axis=-1), jnp.sum(d_norm * normed_half, axis=-1)])
        sums = (sums + swap(sums)) / model_width
        d_layer = inverse * (d_norm - sums[0][:, None] - normed_half * sums[1][:, None])
        d_half = (pick_half(d_output, own).astype(jnp.float32) + d_layer).astype(
            jnp.bfloat16
        )
        other_half = swap(d_half)
        mine = d_half.reshape(shard_rows, blocks_total, half_rows)
        theirs = other_half.reshape(shard_rows, blocks_total, half_rows)
        joined = jnp.concatenate(
            [jnp.where(own, mine, theirs), jnp.where(own, theirs, mine)], axis=2
        )
        return joined.reshape(shard_rows, model_width), branch_full

    incoming = loss_grad
    grad_input = None
    branch_own = None
    for stage in reversed(range(section_total)):
        d_input, branch_full = section_work(incoming, stage)
        here = section_pos == stage
        grad_input = d_input if grad_input is None else jnp.where(here, d_input, grad_input)
        branch_own = branch_full if branch_own is None else jnp.where(here, branch_full, branch_own)
        incoming = d_input
    out_local = lax.dot_general(
        branch_own, attn_mixed_t, (((0,), (1,)), ((), ())), preferred_element_type=jnp.float32
    )
    out_slice = lax.psum_scatter(out_local, "dp", scatter_dimension=0, tiled=True)
    return (grad_input[None, None], out_slice.astype(jnp.bfloat16).T[None])


def solution(mesh):
    in_specs = (
        P("section", "dp", "seq", None),
        P("section", "dp", None, None, "seq"),
        P("section", "dp", None, None),
        P("section", "dp", None, "seq"),
        P("section", "seq", None),
        P("dp"),
        P("dp", "seq", None),
        P("dp", "seq", None),
    )
    out_specs = (P("section", "dp", "seq", None), P("section", "seq", "dp"))
    return jax.shard_map(body, mesh=mesh, in_specs=in_specs, out_specs=out_specs, check_vma=False)
```

```python
import functools
import math

import jax
import jax.numpy as jnp
from jax import lax
from jax.experimental import pallas as pl
from jax.experimental.pallas import tpu as pltpu
from jax.sharding import PartitionSpec as P

HEAD_DIM = 128


def widen(tensor):
    return lax.optimization_barrier(tensor).astype(jnp.float32)


def layer_norm_parts(tokens):
    values = tokens.astype(jnp.float32)
    center = values - jnp.mean(values, axis=-1, keepdims=True)
    variance = jnp.mean(center * center, axis=-1, keepdims=True)
    inverse = lax.rsqrt(variance + 1e-06)
    return (center * inverse, inverse)


def attend_forward(saved_rows, live_keys, head_size):
    row_total = saved_rows.shape[0]
    feature_width = saved_rows.shape[2]
    head_count = feature_width // head_size
    queries = saved_rows[:, 0].reshape(row_total, head_count, head_size).astype(jnp.float32)
    key_rows = saved_rows[:, 1].reshape(row_total, head_count, head_size).astype(jnp.float32)
    value_rows = saved_rows[:, 2].reshape(row_total, head_count, head_size).astype(jnp.float32)
    factor = 1.0 / math.sqrt(head_size)
    scores = jnp.einsum("qhd,khd->hqk", queries, key_rows) * factor
    scores = jnp.where(live_keys[None, None, :], scores, -1e30)
    peak_score = jnp.max(scores, axis=-1, keepdims=True)
    weights = jnp.exp(scores - peak_score)
    weights = weights / jnp.sum(weights, axis=-1, keepdims=True)
    rounded = widen(weights.astype(jnp.bfloat16))
    attn_mixed = jnp.einsum("hqk,khd->qhd", rounded, value_rows).astype(jnp.bfloat16)
    return weights, rounded, attn_mixed


def attend_backward(saved_rows, fwd, d_attn, head_size):
    weights, rounded, attn_mixed = fwd
    row_total = saved_rows.shape[0]
    feature_width = saved_rows.shape[2]
    head_count = feature_width // head_size
    queries = saved_rows[:, 0].reshape(row_total, head_count, head_size).astype(jnp.float32)
    key_rows = saved_rows[:, 1].reshape(row_total, head_count, head_size).astype(jnp.float32)
    value_rows = saved_rows[:, 2].reshape(row_total, head_count, head_size).astype(jnp.float32)
    factor = 1.0 / math.sqrt(head_size)
    upstream = d_attn.reshape(row_total, head_count, head_size).astype(jnp.float32)
    d_weights = jnp.einsum("qhd,khd->hqk", upstream, value_rows)
    delta_rows = jnp.einsum("qhd,qhd->hq", upstream, widen(attn_mixed))
    d_scores = widen((weights * (d_weights - delta_rows[:, :, None]) * factor).astype(jnp.bfloat16))
    grad_q = jnp.einsum("hqk,khd->qhd", d_scores, key_rows).astype(jnp.bfloat16)
    grad_k = jnp.einsum("hqk,qhd->khd", d_scores, queries).astype(jnp.bfloat16)
    grad_v = jnp.einsum("hqk,qhd->khd", rounded, upstream).astype(jnp.bfloat16)
    stacked = jnp.stack([grad_q, grad_k, grad_v], axis=1).reshape(row_total, 3 * feature_width)
    return stacked


RING = ("section", "seq")


def shift_pairs(stage, count, step):
    base = stage * count
    return [(base + pos, base + (pos + step) % count) for pos in range(count)]


def gather_ring(shard, stage, count):
    half = shard.shape[0] // 2
    from_left = lax.ppermute(shard, RING, shift_pairs(stage, count, 1))
    from_right = lax.ppermute(shard, RING, shift_pairs(stage, count, -1))
    far_top = lax.ppermute(from_left[:half], RING, shift_pairs(stage, count, 1))
    far_bottom = lax.ppermute(from_right[half:], RING, shift_pairs(stage, count, -1))
    far = jnp.concatenate([far_top, far_bottom], axis=0)
    return jnp.concatenate([shard, from_right, far, from_left], axis=0)


MESH_ID = pl.DeviceIdType.MESH


def ring_gather_kernel(stage, count, x_ref, o_ref, send_sem, recv_sem, own_sem):
    rows = x_ref.shape[0]
    half = rows // 2
    pos = lax.axis_index("seq")
    dp_pos = lax.axis_index("dp")

    @pl.when(lax.axis_index("section") == stage)
    def _():
        right = lax.rem(pos + 1, count)
        left = lax.rem(pos + count - 1, count)
        barrier = pltpu.get_barrier_semaphore()
        for neighbour in (left, right):
            pl.semaphore_signal(
                barrier, inc=1, device_id=(stage, neighbour, dp_pos), device_id_type=MESH_ID
            )
        pl.semaphore_wait(barrier, 2)
        own = pltpu.make_async_copy(x_ref, o_ref.at[pl.ds(0, rows)], own_sem)
        own.start()

        def remote(src, dst, slot, target):
            return pltpu.make_async_remote_copy(
                src_ref=src,
                dst_ref=dst,
                send_sem=send_sem.at[slot],
                recv_sem=recv_sem.at[slot],
                device_id=(stage, target, dp_pos),
                device_id_type=MESH_ID,
            )

        to_right = remote(x_ref, o_ref.at[pl.ds(3 * rows, rows)], 0, right)
        to_left = remote(x_ref, o_ref.at[pl.ds(rows, rows)], 1, left)
        to_right.start()
        to_left.start()
        to_right.wait()
        to_left.wait()
        relay_right = remote(
            o_ref.at[pl.ds(3 * rows, half)], o_ref.at[pl.ds(2 * rows, half)], 2, right
        )
        relay_left = remote(
            o_ref.at[pl.ds(rows + half, half)], o_ref.at[pl.ds(2 * rows + half, half)], 3, left
        )
        relay_right.start()
        relay_left.start()
        relay_right.wait()
        relay_left.wait()
        own.wait()


def ring_gather(shard, stage, count):
    rows, width = shard.shape
    return pl.pallas_call(
        functools.partial(ring_gather_kernel, stage, count),
        out_shape=jax.ShapeDtypeStruct((count * rows, width), shard.dtype),
        in_specs=[pl.BlockSpec(memory_space=pl.ANY)],
        out_specs=pl.BlockSpec(memory_space=pl.ANY),
        scratch_shapes=[
            pltpu.SemaphoreType.DMA((4,)),
            pltpu.SemaphoreType.DMA((4,)),
            pltpu.SemaphoreType.DMA(()),
        ],
        compiler_params=pltpu.CompilerParams(collective_id=stage, has_side_effects=True),
    )(shard)


def pair_gather_kernel(stage, count, x_ref, o_ref, send_sem, recv_sem, own_sem):
    rows = x_ref.shape[0]
    half = rows // 2
    pos = lax.axis_index("seq")
    dp_pos = lax.axis_index("dp")
    right = lax.rem(pos + 1, count)
    left = lax.rem(pos + count - 1, count)
    helper = 1 - stage
    barrier = pltpu.get_barrier_semaphore()

    def remote(src, dst, slot, target):
        return pltpu.make_async_remote_copy(
            src_ref=src,
            dst_ref=dst,
            send_sem=send_sem.at[slot],
            recv_sem=recv_sem.at[slot],
            device_id=target,
            device_id_type=MESH_ID,
        )

    @pl.when(lax.axis_index("section") == stage)
    def _():
        pl.semaphore_signal(barrier, inc=1, device_id=(stage, left, dp_pos), device_id_type=MESH_ID)
        pl.semaphore_signal(barrier, inc=1, device_id=(helper, pos, dp_pos), device_id_type=MESH_ID)
        pl.semaphore_wait(barrier, 1)
        own = pltpu.make_async_copy(x_ref, o_ref.at[pl.ds(0, rows)], own_sem)
        own.start()
        near = remote(x_ref, o_ref.at[pl.ds(3 * rows, rows)], 0, (stage, right, dp_pos))
        near.start()
        near.wait()
        far = remote(
            o_ref.at[pl.ds(3 * rows, half)], o_ref.at[pl.ds(2 * rows, half)], 1, (stage, right, dp_pos)
        )
        far.start()
        far.wait()
        for slot, start, size in ((4, rows, rows), (5, 2 * rows + half, half)):
            remote(
                o_ref.at[pl.ds(start, size)], o_ref.at[pl.ds(start, size)], slot, (helper, pos, dp_pos)
            ).wait_recv()
        own.wait()

    @pl.when(lax.axis_index("section") == helper)
    def _():
        pl.semaphore_signal(barrier, inc=1, device_id=(helper, right, dp_pos), device_id_type=MESH_ID)
        pl.semaphore_wait(barrier, 2)
        near = remote(x_ref, o_ref.at[pl.ds(rows, rows)], 2, (helper, left, dp_pos))
        near.start()
        near.wait()
        far = remote(
            o_ref.at[pl.ds(rows + half, half)],
            o_ref.at[pl.ds(2 * rows + half, half)],
            3,
            (helper, left, dp_pos),
        )
        far.start()
        far.wait()
        handoff = [
            remote(o_ref.at[pl.ds(start, size)], o_ref.at[pl.ds(start, size)], slot, (stage, pos, dp_pos))
            for slot, start, size in ((4, rows, rows), (5, 2 * rows + half, half))
        ]
        for copy in handoff:
            copy.start()
        for copy in handoff:
            copy.wait_send()


def pair_gather(shard, stage, count):
    rows, width = shard.shape
    return pl.pallas_call(
        functools.partial(pair_gather_kernel, stage, count),
        out_shape=jax.ShapeDtypeStruct((count * rows, width), shard.dtype),
        in_specs=[pl.BlockSpec(memory_space=pl.ANY)],
        out_specs=pl.BlockSpec(memory_space=pl.ANY),
        scratch_shapes=[
            pltpu.SemaphoreType.DMA((6,)),
            pltpu.SemaphoreType.DMA((6,)),
            pltpu.SemaphoreType.DMA(()),
        ],
        compiler_params=pltpu.CompilerParams(collective_id=4 + stage, has_side_effects=True),
    )(shard)


def reduce_ring(partial, stage, count):
    rows = partial.shape[0] // count
    half = rows // 2
    blocks = [partial[k * rows : (k + 1) * rows] for k in range(count)]
    low = lambda value: value.astype(jnp.bfloat16)
    first_right = lax.ppermute(low(blocks[2][:half]), RING, shift_pairs(stage, count, 1))
    first_left = lax.ppermute(low(blocks[2][half:]), RING, shift_pairs(stage, count, -1))
    to_right = jnp.concatenate(
        [first_right.astype(jnp.float32) + blocks[1][:half], blocks[1][half:]], axis=0
    )
    to_left = jnp.concatenate(
        [blocks[3][:half], first_left.astype(jnp.float32) + blocks[3][half:]], axis=0
    )
    got_left = lax.ppermute(low(to_right), RING, shift_pairs(stage, count, 1))
    got_right = lax.ppermute(low(to_left), RING, shift_pairs(stage, count, -1))
    return blocks[0] + got_left.astype(jnp.float32) + got_right.astype(jnp.float32)


def swap(value):
    return lax.ppermute(value, "section", [(0, 1), (1, 0)])


def seq_pairs(count, step):
    return [(pos, (pos + step) % count) for pos in range(count)]


def reduce_seq(partial, count):
    rows = partial.shape[0] // count
    half = rows // 2
    blocks = [partial[k * rows : (k + 1) * rows] for k in range(count)]
    low = lambda value: value.astype(jnp.bfloat16)
    first_right = lax.ppermute(low(blocks[2][:half]), "seq", seq_pairs(count, 1))
    first_left = lax.ppermute(low(blocks[2][half:]), "seq", seq_pairs(count, -1))
    to_right = jnp.concatenate(
        [first_right.astype(jnp.float32) + blocks[1][:half], blocks[1][half:]], axis=0
    )
    to_left = jnp.concatenate(
        [blocks[3][:half], first_left.astype(jnp.float32) + blocks[3][half:]], axis=0
    )
    got_left = lax.ppermute(low(to_right), "seq", seq_pairs(count, 1))
    got_right = lax.ppermute(low(to_left), "seq", seq_pairs(count, -1))
    return blocks[0] + got_left.astype(jnp.float32) + got_right.astype(jnp.float32)


def body(section_input, saved_qkv, modulation, w_qkv, w_out, lengths, student_out, teacher_target):
    section_total = lax.axis_size("section")
    section_pos = lax.axis_index("section")
    seq_total = lax.axis_size("seq")
    seq_pos = lax.axis_index("seq")
    inputs = section_input[0, 0]
    saved_rows = saved_qkv[0, 0]
    weight_out = w_out[0]
    shard_rows, model_width = inputs.shape
    capacity = saved_rows.shape[0]
    local_width = saved_rows.shape[2]
    live_length = lengths[0]
    w_local = w_qkv[0]
    block_rows = w_local.shape[0]
    half_rows = block_rows // 2
    blocks_total = model_width // block_rows

    other_inputs = swap(inputs)
    other_mods = swap(modulation[0, 0])
    other_w = swap(w_local)
    parts = {}
    for stage in range(section_total):
        own = section_pos == stage
        x_stage = jnp.where(own, inputs, other_inputs)
        mods_stage = jnp.where(own, modulation[0, 0], other_mods)
        parts[stage] = (layer_norm_parts(x_stage), mods_stage)

    weights_of = {}
    for stage in reversed(range(section_total)):
        own = section_pos == stage
        contribution = jnp.where(own, w_local[:half_rows], other_w[half_rows:])
        weights_of[stage] = lax.all_gather(contribution, "dp", axis=0, tiled=True).reshape(
            blocks_total * half_rows, 3 * local_width
        )

    positions = seq_pos * shard_rows + jnp.arange(shard_rows, dtype=jnp.int32)
    row_live = positions < live_length
    gap = student_out[0].astype(jnp.float32) - teacher_target[0].astype(jnp.float32)
    loss_grad = jnp.where(row_live[:, None], gap, 0.0).astype(jnp.bfloat16)
    order = (seq_pos + jnp.arange(seq_total, dtype=jnp.int32)) % seq_total
    token_order = (order[:, None] * shard_rows + jnp.arange(shard_rows, dtype=jnp.int32)).reshape(-1)
    saved_off = jnp.take(saved_rows, token_order, axis=0)
    live_keys = token_order < live_length
    fwd = attend_forward(saved_off, live_keys, HEAD_DIM)
    attn_mixed = fwd[2].reshape(capacity, local_width)
    attn_mixed_t = lax.optimization_barrier(attn_mixed.T)

    def pick_half(value, own):
        split = value.reshape(value.shape[0], blocks_total, block_rows)
        chosen = jnp.where(own, split[:, :, :half_rows], split[:, :, half_rows:])
        return chosen.reshape(value.shape[0], blocks_total * half_rows)

    def section_work(d_output, stage):
        own = section_pos == stage
        (normed, inverse), mods_stage = parts[stage]
        scale_term = mods_stage[0]
        gate_term = mods_stage[1]
        d_branch = (gate_term * d_output.astype(jnp.float32)).astype(jnp.bfloat16)
        if stage == section_total - 1:
            branch_full = gather_ring(d_branch, stage, seq_total)
        else:
            branch_full = pair_gather(d_branch, stage, seq_total)
        d_attn = jnp.dot(branch_full, weight_out.T, preferred_element_type=jnp.float32).astype(
            jnp.bfloat16
        )
        own_grads = attend_backward(saved_off, fwd, d_attn, HEAD_DIM)
        handed = lax.ppermute(own_grads, "section", [(stage, 1 - stage)])
        flat_grads = jnp.where(own, own_grads, handed)
        d_mod_part = jnp.dot(flat_grads, weights_of[stage].T, preferred_element_type=jnp.float32)
        d_mod = reduce_seq(d_mod_part, seq_total)
        normed_half = pick_half(normed, own)
        d_norm = d_mod * (1.0 + pick_half(scale_term[None], own))
        sums = jnp.stack([jnp.sum(d_norm, axis=-1), jnp.sum(d_norm * normed_half, axis=-1)])
        sums = (sums + swap(sums)) / model_width
        d_layer = inverse * (d_norm - sums[0][:, None] - normed_half * sums[1][:, None])
        d_half = (pick_half(d_output, own).astype(jnp.float32) + d_layer).astype(
            jnp.bfloat16
        )
        other_half = swap(d_half)
        mine = d_half.reshape(shard_rows, blocks_total, half_rows)
        theirs = other_half.reshape(shard_rows, blocks_total, half_rows)
        joined = jnp.concatenate(
            [jnp.where(own, mine, theirs), jnp.where(own, theirs, mine)], axis=2
        )
        return joined.reshape(shard_rows, model_width), branch_full

    incoming = loss_grad
    grad_input = None
    branch_own = None
    for stage in reversed(range(section_total)):
        d_input, branch_full = section_work(incoming, stage)
        here = section_pos == stage
        grad_input = d_input if grad_input is None else jnp.where(here, d_input, grad_input)
        branch_own = branch_full if branch_own is None else jnp.where(here, branch_full, branch_own)
        incoming = d_input
    out_local = jnp.dot(attn_mixed_t, branch_own, preferred_element_type=jnp.float32)
    out_slice = lax.psum_scatter(out_local, "dp", scatter_dimension=1, tiled=True)
    return (grad_input[None, None], out_slice.astype(jnp.bfloat16)[None])


def solution(mesh):
    in_specs = (
        P("section", "dp", "seq", None),
        P("section", "dp", None, None, "seq"),
        P("section", "dp", None, None),
        P("section", "dp", None, "seq"),
        P("section", "seq", None),
        P("dp"),
        P("dp", "seq", None),
        P("dp", "seq", None),
    )
    out_specs = (P("section", "dp", "seq", None), P("section", "seq", "dp"))
    return jax.shard_map(body, mesh=mesh, in_specs=in_specs, out_specs=out_specs, check_vma=False)
```

```python
import functools
import math

import jax
import jax.numpy as jnp
from jax import lax
from jax.experimental import pallas as pl
from jax.experimental.pallas import tpu as pltpu
from jax.sharding import PartitionSpec as P

HEAD_DIM = 128


def widen(tensor):
    return lax.optimization_barrier(tensor).astype(jnp.float32)


def layer_norm_parts(tokens):
    values = tokens.astype(jnp.float32)
    center = values - jnp.mean(values, axis=-1, keepdims=True)
    variance = jnp.mean(center * center, axis=-1, keepdims=True)
    inverse = lax.rsqrt(variance + 1e-06)
    return (center * inverse, inverse)


def attend_forward(saved_rows, live_keys, head_size):
    row_total = saved_rows.shape[0]
    feature_width = saved_rows.shape[2]
    head_count = feature_width // head_size
    queries = saved_rows[:, 0].reshape(row_total, head_count, head_size).astype(jnp.float32)
    key_rows = saved_rows[:, 1].reshape(row_total, head_count, head_size).astype(jnp.float32)
    value_rows = saved_rows[:, 2].reshape(row_total, head_count, head_size).astype(jnp.float32)
    factor = 1.0 / math.sqrt(head_size)
    scores = jnp.einsum("qhd,khd->hqk", queries, key_rows) * factor
    scores = jnp.where(live_keys[None, None, :], scores, -1e30)
    peak_score = jnp.max(scores, axis=-1, keepdims=True)
    weights = jnp.exp(scores - peak_score)
    weights = weights / jnp.sum(weights, axis=-1, keepdims=True)
    rounded = widen(weights.astype(jnp.bfloat16))
    attn_mixed = jnp.einsum("hqk,khd->qhd", rounded, value_rows).astype(jnp.bfloat16)
    return weights, rounded, attn_mixed


def attend_backward(saved_rows, fwd, d_attn, head_size):
    weights, rounded, attn_mixed = fwd
    row_total = saved_rows.shape[0]
    feature_width = saved_rows.shape[2]
    head_count = feature_width // head_size
    queries = saved_rows[:, 0].reshape(row_total, head_count, head_size).astype(jnp.float32)
    key_rows = saved_rows[:, 1].reshape(row_total, head_count, head_size).astype(jnp.float32)
    value_rows = saved_rows[:, 2].reshape(row_total, head_count, head_size).astype(jnp.float32)
    factor = 1.0 / math.sqrt(head_size)
    upstream = d_attn.reshape(row_total, head_count, head_size).astype(jnp.float32)
    d_weights = jnp.einsum("qhd,khd->hqk", upstream, value_rows)
    delta_rows = jnp.einsum("qhd,qhd->hq", upstream, widen(attn_mixed))
    d_scores = widen((weights * (d_weights - delta_rows[:, :, None]) * factor).astype(jnp.bfloat16))
    grad_q = jnp.einsum("hqk,khd->qhd", d_scores, key_rows).astype(jnp.bfloat16)
    grad_k = jnp.einsum("hqk,qhd->khd", d_scores, queries).astype(jnp.bfloat16)
    grad_v = jnp.einsum("hqk,qhd->khd", rounded, upstream).astype(jnp.bfloat16)
    stacked = jnp.stack([grad_q, grad_k, grad_v], axis=1).reshape(row_total, 3 * feature_width)
    return stacked


RING = ("section", "seq")


def shift_pairs(stage, count, step):
    base = stage * count
    return [(base + pos, base + (pos + step) % count) for pos in range(count)]


def gather_ring(shard, stage, count):
    half = shard.shape[0] // 2
    from_left = lax.ppermute(shard, RING, shift_pairs(stage, count, 1))
    from_right = lax.ppermute(shard, RING, shift_pairs(stage, count, -1))
    far_top = lax.ppermute(from_left[:half], RING, shift_pairs(stage, count, 1))
    far_bottom = lax.ppermute(from_right[half:], RING, shift_pairs(stage, count, -1))
    far = jnp.concatenate([far_top, far_bottom], axis=0)
    return jnp.concatenate([shard, from_right, far, from_left], axis=0)


MESH_ID = pl.DeviceIdType.MESH


def ring_gather_kernel(stage, count, x_ref, o_ref, send_sem, recv_sem, own_sem):
    rows = x_ref.shape[0]
    half = rows // 2
    pos = lax.axis_index("seq")
    dp_pos = lax.axis_index("dp")

    @pl.when(lax.axis_index("section") == stage)
    def _():
        right = lax.rem(pos + 1, count)
        left = lax.rem(pos + count - 1, count)
        barrier = pltpu.get_barrier_semaphore()
        for neighbour in (left, right):
            pl.semaphore_signal(
                barrier, inc=1, device_id=(stage, neighbour, dp_pos), device_id_type=MESH_ID
            )
        pl.semaphore_wait(barrier, 2)
        own = pltpu.make_async_copy(x_ref, o_ref.at[pl.ds(0, rows)], own_sem)
        own.start()

        def remote(src, dst, slot, target):
            return pltpu.make_async_remote_copy(
                src_ref=src,
                dst_ref=dst,
                send_sem=send_sem.at[slot],
                recv_sem=recv_sem.at[slot],
                device_id=(stage, target, dp_pos),
                device_id_type=MESH_ID,
            )

        to_right = remote(x_ref, o_ref.at[pl.ds(3 * rows, rows)], 0, right)
        to_left = remote(x_ref, o_ref.at[pl.ds(rows, rows)], 1, left)
        to_right.start()
        to_left.start()
        to_right.wait()
        to_left.wait()
        relay_right = remote(
            o_ref.at[pl.ds(3 * rows, half)], o_ref.at[pl.ds(2 * rows, half)], 2, right
        )
        relay_left = remote(
            o_ref.at[pl.ds(rows + half, half)], o_ref.at[pl.ds(2 * rows + half, half)], 3, left
        )
        relay_right.start()
        relay_left.start()
        relay_right.wait()
        relay_left.wait()
        own.wait()


def ring_gather(shard, stage, count):
    rows, width = shard.shape
    return pl.pallas_call(
        functools.partial(ring_gather_kernel, stage, count),
        out_shape=jax.ShapeDtypeStruct((count * rows, width), shard.dtype),
        in_specs=[pl.BlockSpec(memory_space=pl.ANY)],
        out_specs=pl.BlockSpec(memory_space=pl.ANY),
        scratch_shapes=[
            pltpu.SemaphoreType.DMA((4,)),
            pltpu.SemaphoreType.DMA((4,)),
            pltpu.SemaphoreType.DMA(()),
        ],
        compiler_params=pltpu.CompilerParams(collective_id=stage, has_side_effects=True),
    )(shard)


def reduce_ring(partial, stage, count):
    rows = partial.shape[0] // count
    half = rows // 2
    blocks = [partial[k * rows : (k + 1) * rows] for k in range(count)]
    low = lambda value: value.astype(jnp.bfloat16)
    first_right = lax.ppermute(low(blocks[2][:half]), RING, shift_pairs(stage, count, 1))
    first_left = lax.ppermute(low(blocks[2][half:]), RING, shift_pairs(stage, count, -1))
    to_right = jnp.concatenate(
        [first_right.astype(jnp.float32) + blocks[1][:half], blocks[1][half:]], axis=0
    )
    to_left = jnp.concatenate(
        [blocks[3][:half], first_left.astype(jnp.float32) + blocks[3][half:]], axis=0
    )
    got_left = lax.ppermute(low(to_right), RING, shift_pairs(stage, count, 1))
    got_right = lax.ppermute(low(to_left), RING, shift_pairs(stage, count, -1))
    return blocks[0] + got_left.astype(jnp.float32) + got_right.astype(jnp.float32)


def swap(value):
    return lax.ppermute(value, "section", [(0, 1), (1, 0)])


def seq_pairs(count, step):
    return [(pos, (pos + step) % count) for pos in range(count)]


def reduce_seq(partial, count):
    blocks = partial
    half = blocks[0].shape[0] // 2
    low = lambda value: value.astype(jnp.bfloat16)
    first_right = lax.ppermute(low(blocks[2][:half]), "seq", seq_pairs(count, 1))
    first_left = lax.ppermute(low(blocks[2][half:]), "seq", seq_pairs(count, -1))
    to_right = jnp.concatenate(
        [first_right.astype(jnp.float32) + blocks[1][:half], blocks[1][half:]], axis=0
    )
    to_left = jnp.concatenate(
        [blocks[3][:half], first_left.astype(jnp.float32) + blocks[3][half:]], axis=0
    )
    got_left = lax.ppermute(low(to_right), "seq", seq_pairs(count, 1))
    got_right = lax.ppermute(low(to_left), "seq", seq_pairs(count, -1))
    return blocks[0] + got_left.astype(jnp.float32) + got_right.astype(jnp.float32)


def body(section_input, saved_qkv, modulation, w_qkv, w_out, lengths, student_out, teacher_target):
    section_total = lax.axis_size("section")
    section_pos = lax.axis_index("section")
    seq_total = lax.axis_size("seq")
    seq_pos = lax.axis_index("seq")
    inputs = section_input[0, 0]
    saved_rows = saved_qkv[0, 0]
    weight_out = w_out[0]
    shard_rows, model_width = inputs.shape
    capacity = saved_rows.shape[0]
    local_width = saved_rows.shape[2]
    live_length = lengths[0]
    w_local = w_qkv[0]
    block_rows = w_local.shape[0]
    half_rows = block_rows // 2
    blocks_total = model_width // block_rows

    other_inputs = swap(inputs)
    other_mods = swap(modulation[0, 0])
    other_w = swap(w_local)
    parts = {}
    for stage in range(section_total):
        own = section_pos == stage
        x_stage = jnp.where(own, inputs, other_inputs)
        mods_stage = jnp.where(own, modulation[0, 0], other_mods)
        parts[stage] = (layer_norm_parts(x_stage), mods_stage)

    weights_of = {}
    for stage in reversed(range(section_total)):
        own = section_pos == stage
        contribution = jnp.where(own, w_local[:half_rows], other_w[half_rows:])
        weights_of[stage] = lax.all_gather(contribution, "dp", axis=0, tiled=True).reshape(
            blocks_total * half_rows, 3 * local_width
        )

    positions = seq_pos * shard_rows + jnp.arange(shard_rows, dtype=jnp.int32)
    row_live = positions < live_length
    gap = student_out[0].astype(jnp.float32) - teacher_target[0].astype(jnp.float32)
    loss_grad = jnp.where(row_live[:, None], gap, 0.0).astype(jnp.bfloat16)
    order = (seq_pos + jnp.arange(seq_total, dtype=jnp.int32)) % seq_total
    token_order = (order[:, None] * shard_rows + jnp.arange(shard_rows, dtype=jnp.int32)).reshape(-1)
    saved_off = jnp.take(saved_rows, token_order, axis=0)
    live_keys = token_order < live_length
    fwd = attend_forward(saved_off, live_keys, HEAD_DIM)
    attn_mixed = fwd[2].reshape(capacity, local_width)
    attn_mixed_t = lax.optimization_barrier(attn_mixed.T)

    def pick_half(value, own):
        split = value.reshape(value.shape[0], blocks_total, block_rows)
        chosen = jnp.where(own, split[:, :, :half_rows], split[:, :, half_rows:])
        return chosen.reshape(value.shape[0], blocks_total * half_rows)

    def section_work(d_output, stage):
        own = section_pos == stage
        (normed, inverse), mods_stage = parts[stage]
        scale_term = mods_stage[0]
        gate_term = mods_stage[1]
        d_branch = (gate_term * d_output.astype(jnp.float32)).astype(jnp.bfloat16)
        if stage == section_total - 1:
            branch_full = gather_ring(d_branch, stage, seq_total)
        else:
            branch_full = ring_gather(d_branch, stage, seq_total)
        d_attn = jnp.dot(branch_full, weight_out.T, preferred_element_type=jnp.float32).astype(
            jnp.bfloat16
        )
        own_grads = attend_backward(saved_off, fwd, d_attn, HEAD_DIM)
        handed = lax.ppermute(own_grads, "section", [(stage, 1 - stage)])
        flat_grads = jnp.where(own, own_grads, handed)
        d_mod_blocks = [
            jnp.dot(
                flat_grads[k * shard_rows : (k + 1) * shard_rows],
                weights_of[stage].T,
                preferred_element_type=jnp.float32,
            )
            for k in range(seq_total)
        ]
        d_mod = reduce_seq(d_mod_blocks, seq_total)
        normed_half = pick_half(normed, own)
        d_norm = d_mod * (1.0 + pick_half(scale_term[None], own))
        sums = jnp.stack([jnp.sum(d_norm, axis=-1), jnp.sum(d_norm * normed_half, axis=-1)])
        sums = (sums + swap(sums)) / model_width
        d_layer = inverse * (d_norm - sums[0][:, None] - normed_half * sums[1][:, None])
        d_half = (pick_half(d_output, own).astype(jnp.float32) + d_layer).astype(
            jnp.bfloat16
        )
        other_half = swap(d_half)
        mine = d_half.reshape(shard_rows, blocks_total, half_rows)
        theirs = other_half.reshape(shard_rows, blocks_total, half_rows)
        joined = jnp.concatenate(
            [jnp.where(own, mine, theirs), jnp.where(own, theirs, mine)], axis=2
        )
        return joined.reshape(shard_rows, model_width), branch_full

    incoming = loss_grad
    grad_input = None
    branch_own = None
    for stage in reversed(range(section_total)):
        d_input, branch_full = section_work(incoming, stage)
        here = section_pos == stage
        grad_input = d_input if grad_input is None else jnp.where(here, d_input, grad_input)
        branch_own = branch_full if branch_own is None else jnp.where(here, branch_full, branch_own)
        incoming = d_input
    out_local = jnp.dot(attn_mixed_t, branch_own, preferred_element_type=jnp.float32)
    out_slice = lax.psum_scatter(out_local, "dp", scatter_dimension=1, tiled=True)
    return (grad_input[None, None], out_slice.astype(jnp.bfloat16)[None])


def solution(mesh):
    in_specs = (
        P("section", "dp", "seq", None),
        P("section", "dp", None, None, "seq"),
        P("section", "dp", None, None),
        P("section", "dp", None, "seq"),
        P("section", "seq", None),
        P("dp"),
        P("dp", "seq", None),
        P("dp", "seq", None),
    )
    out_specs = (P("section", "dp", "seq", None), P("section", "seq", "dp"))
    return jax.shard_map(body, mesh=mesh, in_specs=in_specs, out_specs=out_specs, check_vma=False)
```

```python
import functools
import math

import jax
import jax.numpy as jnp
from jax import lax
from jax.experimental import pallas as pl
from jax.experimental.pallas import tpu as pltpu
from jax.sharding import PartitionSpec as P

HEAD_DIM = 128


def widen(tensor):
    return lax.optimization_barrier(tensor).astype(jnp.float32)


def layer_norm_parts(tokens):
    values = tokens.astype(jnp.float32)
    center = values - jnp.mean(values, axis=-1, keepdims=True)
    variance = jnp.mean(center * center, axis=-1, keepdims=True)
    inverse = lax.rsqrt(variance + 1e-06)
    return (center * inverse, inverse)


def attend_forward(saved_rows, live_keys, head_size):
    row_total = saved_rows.shape[0]
    feature_width = saved_rows.shape[2]
    head_count = feature_width // head_size
    queries = saved_rows[:, 0].reshape(row_total, head_count, head_size).astype(jnp.float32)
    key_rows = saved_rows[:, 1].reshape(row_total, head_count, head_size).astype(jnp.float32)
    value_rows = saved_rows[:, 2].reshape(row_total, head_count, head_size).astype(jnp.float32)
    factor = 1.0 / math.sqrt(head_size)
    scores = jnp.einsum("qhd,khd->hqk", queries, key_rows) * factor
    scores = jnp.where(live_keys[None, None, :], scores, -1e30)
    peak_score = jnp.max(scores, axis=-1, keepdims=True)
    weights = jnp.exp(scores - peak_score)
    weights = weights / jnp.sum(weights, axis=-1, keepdims=True)
    rounded = widen(weights.astype(jnp.bfloat16))
    attn_mixed = jnp.einsum("hqk,khd->qhd", rounded, value_rows).astype(jnp.bfloat16)
    return weights, rounded, attn_mixed


def attend_backward(saved_rows, fwd, d_attn, head_size):
    weights, rounded, attn_mixed = fwd
    row_total = saved_rows.shape[0]
    feature_width = saved_rows.shape[2]
    head_count = feature_width // head_size
    queries = saved_rows[:, 0].reshape(row_total, head_count, head_size).astype(jnp.float32)
    key_rows = saved_rows[:, 1].reshape(row_total, head_count, head_size).astype(jnp.float32)
    value_rows = saved_rows[:, 2].reshape(row_total, head_count, head_size).astype(jnp.float32)
    factor = 1.0 / math.sqrt(head_size)
    upstream = d_attn.reshape(row_total, head_count, head_size).astype(jnp.float32)
    d_weights = jnp.einsum("qhd,khd->hqk", upstream, value_rows)
    delta_rows = jnp.einsum("qhd,qhd->hq", upstream, widen(attn_mixed))
    d_scores = widen((weights * (d_weights - delta_rows[:, :, None]) * factor).astype(jnp.bfloat16))
    grad_q = jnp.einsum("hqk,khd->qhd", d_scores, key_rows).astype(jnp.bfloat16)
    grad_k = jnp.einsum("hqk,qhd->khd", d_scores, queries).astype(jnp.bfloat16)
    grad_v = jnp.einsum("hqk,qhd->khd", rounded, upstream).astype(jnp.bfloat16)
    stacked = jnp.stack([grad_q, grad_k, grad_v], axis=1).reshape(row_total, 3 * feature_width)
    return stacked


RING = ("section", "seq")


def shift_pairs(stage, count, step):
    base = stage * count
    return [(base + pos, base + (pos + step) % count) for pos in range(count)]


def gather_ring(shard, stage, count):
    half = shard.shape[0] // 2
    from_left = lax.ppermute(shard, RING, shift_pairs(stage, count, 1))
    from_right = lax.ppermute(shard, RING, shift_pairs(stage, count, -1))
    far_top = lax.ppermute(from_left[:half], RING, shift_pairs(stage, count, 1))
    far_bottom = lax.ppermute(from_right[half:], RING, shift_pairs(stage, count, -1))
    far = jnp.concatenate([far_top, far_bottom], axis=0)
    return jnp.concatenate([shard, from_right, far, from_left], axis=0)


MESH_ID = pl.DeviceIdType.MESH


def ring_gather_kernel(stage, count, x_ref, o_ref, send_sem, recv_sem, own_sem):
    rows = x_ref.shape[0]
    half = rows // 2
    pos = lax.axis_index("seq")
    dp_pos = lax.axis_index("dp")

    @pl.when(lax.axis_index("section") == stage)
    def _():
        right = lax.rem(pos + 1, count)
        left = lax.rem(pos + count - 1, count)
        barrier = pltpu.get_barrier_semaphore()
        for neighbour in (left, right):
            pl.semaphore_signal(
                barrier, inc=1, device_id=(stage, neighbour, dp_pos), device_id_type=MESH_ID
            )
        pl.semaphore_wait(barrier, 2)
        own = pltpu.make_async_copy(x_ref, o_ref.at[pl.ds(0, rows)], own_sem)
        own.start()

        def remote(src, dst, slot, target):
            return pltpu.make_async_remote_copy(
                src_ref=src,
                dst_ref=dst,
                send_sem=send_sem.at[slot],
                recv_sem=recv_sem.at[slot],
                device_id=(stage, target, dp_pos),
                device_id_type=MESH_ID,
            )

        to_right = remote(x_ref, o_ref.at[pl.ds(3 * rows, rows)], 0, right)
        to_left = remote(x_ref, o_ref.at[pl.ds(rows, rows)], 1, left)
        to_right.start()
        to_left.start()
        to_right.wait()
        to_left.wait()
        relay_right = remote(
            o_ref.at[pl.ds(3 * rows, half)], o_ref.at[pl.ds(2 * rows, half)], 2, right
        )
        relay_left = remote(
            o_ref.at[pl.ds(rows + half, half)], o_ref.at[pl.ds(2 * rows + half, half)], 3, left
        )
        relay_right.start()
        relay_left.start()
        relay_right.wait()
        relay_left.wait()
        own.wait()


def ring_gather(shard, stage, count):
    rows, width = shard.shape
    return pl.pallas_call(
        functools.partial(ring_gather_kernel, stage, count),
        out_shape=jax.ShapeDtypeStruct((count * rows, width), shard.dtype),
        in_specs=[pl.BlockSpec(memory_space=pl.ANY)],
        out_specs=pl.BlockSpec(memory_space=pl.ANY),
        scratch_shapes=[
            pltpu.SemaphoreType.DMA((4,)),
            pltpu.SemaphoreType.DMA((4,)),
            pltpu.SemaphoreType.DMA(()),
        ],
        compiler_params=pltpu.CompilerParams(collective_id=stage, has_side_effects=True),
    )(shard)


def reduce_ring(partial, stage, count):
    rows = partial.shape[0] // count
    half = rows // 2
    blocks = [partial[k * rows : (k + 1) * rows] for k in range(count)]
    low = lambda value: value.astype(jnp.bfloat16)
    first_right = lax.ppermute(low(blocks[2][:half]), RING, shift_pairs(stage, count, 1))
    first_left = lax.ppermute(low(blocks[2][half:]), RING, shift_pairs(stage, count, -1))
    to_right = jnp.concatenate(
        [first_right.astype(jnp.float32) + blocks[1][:half], blocks[1][half:]], axis=0
    )
    to_left = jnp.concatenate(
        [blocks[3][:half], first_left.astype(jnp.float32) + blocks[3][half:]], axis=0
    )
    got_left = lax.ppermute(low(to_right), RING, shift_pairs(stage, count, 1))
    got_right = lax.ppermute(low(to_left), RING, shift_pairs(stage, count, -1))
    return blocks[0] + got_left.astype(jnp.float32) + got_right.astype(jnp.float32)


def swap(value):
    return lax.ppermute(value, "section", [(0, 1), (1, 0)])


def seq_pairs(count, step):
    return [(pos, (pos + step) % count) for pos in range(count)]


def reduce_seq(partial, count):
    rows = partial.shape[0] // count
    half = rows // 2
    blocks = [partial[k * rows : (k + 1) * rows] for k in range(count)]
    low = lambda value: value.astype(jnp.bfloat16)
    first_right = lax.ppermute(low(blocks[2][:half]), "seq", seq_pairs(count, 1))
    first_left = lax.ppermute(low(blocks[2][half:]), "seq", seq_pairs(count, -1))
    to_right = jnp.concatenate(
        [first_right.astype(jnp.float32) + blocks[1][:half], blocks[1][half:]], axis=0
    )
    to_left = jnp.concatenate(
        [blocks[3][:half], first_left.astype(jnp.float32) + blocks[3][half:]], axis=0
    )
    got_left = lax.ppermute(low(to_right), "seq", seq_pairs(count, 1))
    got_right = lax.ppermute(low(to_left), "seq", seq_pairs(count, -1))
    return blocks[0] + got_left.astype(jnp.float32) + got_right.astype(jnp.float32)


def body(section_input, saved_qkv, modulation, w_qkv, w_out, lengths, student_out, teacher_target):
    section_total = lax.axis_size("section")
    section_pos = lax.axis_index("section")
    seq_total = lax.axis_size("seq")
    seq_pos = lax.axis_index("seq")
    inputs = section_input[0, 0]
    saved_rows = saved_qkv[0, 0]
    weight_out = w_out[0]
    shard_rows, model_width = inputs.shape
    capacity = saved_rows.shape[0]
    local_width = saved_rows.shape[2]
    live_length = lengths[0]
    w_local = w_qkv[0]
    block_rows = w_local.shape[0]
    half_rows = block_rows // 2
    blocks_total = model_width // block_rows

    other_inputs = swap(inputs)
    other_mods = swap(modulation[0, 0])
    other_w = swap(w_local[half_rows:])
    parts = {}
    for stage in range(section_total):
        own = section_pos == stage
        x_stage = jnp.where(own, inputs, other_inputs)
        mods_stage = jnp.where(own, modulation[0, 0], other_mods)
        parts[stage] = (layer_norm_parts(x_stage), mods_stage)

    weights_of = {}
    for stage in reversed(range(section_total)):
        own = section_pos == stage
        contribution = jnp.where(own, w_local[:half_rows], other_w)
        weights_of[stage] = lax.all_gather(contribution, "dp", axis=0, tiled=True).reshape(
            blocks_total * half_rows, 3 * local_width
        )

    positions = seq_pos * shard_rows + jnp.arange(shard_rows, dtype=jnp.int32)
    row_live = positions < live_length
    gap = student_out[0].astype(jnp.float32) - teacher_target[0].astype(jnp.float32)
    loss_grad = jnp.where(row_live[:, None], gap, 0.0).astype(jnp.bfloat16)
    order = (seq_pos + jnp.arange(seq_total, dtype=jnp.int32)) % seq_total
    token_order = (order[:, None] * shard_rows + jnp.arange(shard_rows, dtype=jnp.int32)).reshape(-1)
    saved_off = jnp.take(saved_rows, token_order, axis=0)
    live_keys = token_order < live_length
    fwd = attend_forward(saved_off, live_keys, HEAD_DIM)
    attn_mixed = fwd[2].reshape(capacity, local_width)
    attn_mixed_t = lax.optimization_barrier(attn_mixed.T)

    def pick_half(value, own):
        split = value.reshape(value.shape[0], blocks_total, block_rows)
        chosen = jnp.where(own, split[:, :, :half_rows], split[:, :, half_rows:])
        return chosen.reshape(value.shape[0], blocks_total * half_rows)

    def section_work(d_output, stage):
        own = section_pos == stage
        (normed, inverse), mods_stage = parts[stage]
        scale_term = mods_stage[0]
        gate_term = mods_stage[1]
        d_branch = (gate_term * d_output.astype(jnp.float32)).astype(jnp.bfloat16)
        if stage == section_total - 1:
            branch_full = gather_ring(d_branch, stage, seq_total)
        else:
            branch_full = ring_gather(d_branch, stage, seq_total)
        d_attn = jnp.dot(branch_full, weight_out.T, preferred_element_type=jnp.float32).astype(
            jnp.bfloat16
        )
        own_grads = attend_backward(saved_off, fwd, d_attn, HEAD_DIM)
        handed = lax.ppermute(own_grads, "section", [(stage, 1 - stage)])
        flat_grads = jnp.where(own, own_grads, handed)
        d_mod_part = jnp.dot(flat_grads, weights_of[stage].T, preferred_element_type=jnp.float32)
        d_mod = reduce_seq(d_mod_part, seq_total)
        normed_half = pick_half(normed, own)
        d_norm = d_mod * (1.0 + pick_half(scale_term[None], own))
        sums = jnp.stack([jnp.sum(d_norm, axis=-1), jnp.sum(d_norm * normed_half, axis=-1)])
        sums = (sums + swap(sums)) / model_width
        d_layer = inverse * (d_norm - sums[0][:, None] - normed_half * sums[1][:, None])
        d_half = (pick_half(d_output, own).astype(jnp.float32) + d_layer).astype(
            jnp.bfloat16
        )
        other_half = swap(d_half)
        mine = d_half.reshape(shard_rows, blocks_total, half_rows)
        theirs = other_half.reshape(shard_rows, blocks_total, half_rows)
        joined = jnp.concatenate(
            [jnp.where(own, mine, theirs), jnp.where(own, theirs, mine)], axis=2
        )
        return joined.reshape(shard_rows, model_width), branch_full

    incoming = loss_grad
    grad_input = None
    branch_own = None
    for stage in reversed(range(section_total)):
        d_input, branch_full = section_work(incoming, stage)
        here = section_pos == stage
        grad_input = d_input if grad_input is None else jnp.where(here, d_input, grad_input)
        branch_own = branch_full if branch_own is None else jnp.where(here, branch_full, branch_own)
        incoming = d_input
    out_local = jnp.dot(attn_mixed_t, branch_own, preferred_element_type=jnp.float32)
    out_slice = lax.psum_scatter(out_local, "dp", scatter_dimension=1, tiled=True)
    return (grad_input[None, None], out_slice.astype(jnp.bfloat16)[None])


def solution(mesh):
    in_specs = (
        P("section", "dp", "seq", None),
        P("section", "dp", None, None, "seq"),
        P("section", "dp", None, None),
        P("section", "dp", None, "seq"),
        P("section", "seq", None),
        P("dp"),
        P("dp", "seq", None),
        P("dp", "seq", None),
    )
    out_specs = (P("section", "dp", "seq", None), P("section", "seq", "dp"))
    return jax.shard_map(body, mesh=mesh, in_specs=in_specs, out_specs=out_specs, check_vma=False)
```

```python
import functools
import math

import jax
import jax.numpy as jnp
from jax import lax
from jax.experimental import pallas as pl
from jax.experimental.pallas import tpu as pltpu
from jax.sharding import PartitionSpec as P

HEAD_DIM = 128


def widen(tensor):
    return lax.optimization_barrier(tensor).astype(jnp.float32)


def layer_norm_parts(tokens):
    values = tokens.astype(jnp.float32)
    center = values - jnp.mean(values, axis=-1, keepdims=True)
    variance = jnp.mean(center * center, axis=-1, keepdims=True)
    inverse = lax.rsqrt(variance + 1e-06)
    return (center * inverse, inverse)


def attend_forward(saved_rows, live_keys, head_size):
    row_total = saved_rows.shape[0]
    feature_width = saved_rows.shape[2]
    head_count = feature_width // head_size
    queries = saved_rows[:, 0].reshape(row_total, head_count, head_size).astype(jnp.float32)
    key_rows = saved_rows[:, 1].reshape(row_total, head_count, head_size).astype(jnp.float32)
    value_rows = saved_rows[:, 2].reshape(row_total, head_count, head_size).astype(jnp.float32)
    factor = 1.0 / math.sqrt(head_size)
    scores = jnp.einsum("qhd,khd->hqk", queries, key_rows) * factor
    scores = jnp.where(live_keys[None, None, :], scores, -1e30)
    peak_score = jnp.max(scores, axis=-1, keepdims=True)
    weights = jnp.exp(scores - peak_score)
    weights = weights / jnp.sum(weights, axis=-1, keepdims=True)
    rounded = widen(weights.astype(jnp.bfloat16))
    attn_mixed = jnp.einsum("hqk,khd->qhd", rounded, value_rows).astype(jnp.bfloat16)
    return weights, rounded, attn_mixed


def attend_backward(saved_rows, fwd, d_attn, head_size):
    weights, rounded, attn_mixed = fwd
    row_total = saved_rows.shape[0]
    feature_width = saved_rows.shape[2]
    head_count = feature_width // head_size
    queries = saved_rows[:, 0].reshape(row_total, head_count, head_size).astype(jnp.float32)
    key_rows = saved_rows[:, 1].reshape(row_total, head_count, head_size).astype(jnp.float32)
    value_rows = saved_rows[:, 2].reshape(row_total, head_count, head_size).astype(jnp.float32)
    factor = 1.0 / math.sqrt(head_size)
    upstream = d_attn.reshape(row_total, head_count, head_size).astype(jnp.float32)
    d_weights = jnp.einsum("qhd,khd->hqk", upstream, value_rows)
    delta_rows = jnp.einsum("qhd,qhd->hq", upstream, widen(attn_mixed))
    d_scores = widen((weights * (d_weights - delta_rows[:, :, None]) * factor).astype(jnp.bfloat16))
    grad_q = jnp.einsum("hqk,khd->qhd", d_scores, key_rows).astype(jnp.bfloat16)
    grad_k = jnp.einsum("hqk,qhd->khd", d_scores, queries).astype(jnp.bfloat16)
    grad_v = jnp.einsum("hqk,qhd->khd", rounded, upstream).astype(jnp.bfloat16)
    stacked = jnp.stack([grad_q, grad_k, grad_v], axis=1).reshape(row_total, 3 * feature_width)
    return stacked


RING = ("section", "seq")


def shift_pairs(stage, count, step):
    base = stage * count
    return [(base + pos, base + (pos + step) % count) for pos in range(count)]


def gather_ring(shard, stage, count):
    half = shard.shape[0] // 2
    from_left = lax.ppermute(shard, RING, shift_pairs(stage, count, 1))
    from_right = lax.ppermute(shard, RING, shift_pairs(stage, count, -1))
    far_top = lax.ppermute(from_left[:half], RING, shift_pairs(stage, count, 1))
    far_bottom = lax.ppermute(from_right[half:], RING, shift_pairs(stage, count, -1))
    far = jnp.concatenate([far_top, far_bottom], axis=0)
    return jnp.concatenate([shard, from_right, far, from_left], axis=0)


MESH_ID = pl.DeviceIdType.MESH


def ring_gather_kernel(stage, count, x_ref, keep_ref, o_ref, send_sem, recv_sem, own_sem):
    rows = x_ref.shape[0]
    half = rows // 2
    pos = lax.axis_index("seq")
    dp_pos = lax.axis_index("dp")

    @pl.when(lax.axis_index("section") == stage)
    def _():
        right = lax.rem(pos + 1, count)
        left = lax.rem(pos + count - 1, count)
        barrier = pltpu.get_barrier_semaphore()
        for neighbour in (left, right):
            pl.semaphore_signal(
                barrier, inc=1, device_id=(stage, neighbour, dp_pos), device_id_type=MESH_ID
            )
        pl.semaphore_wait(barrier, 2)
        own = pltpu.make_async_copy(x_ref, o_ref.at[pl.ds(0, rows)], own_sem)
        own.start()

        def remote(src, dst, slot, target):
            return pltpu.make_async_remote_copy(
                src_ref=src,
                dst_ref=dst,
                send_sem=send_sem.at[slot],
                recv_sem=recv_sem.at[slot],
                device_id=(stage, target, dp_pos),
                device_id_type=MESH_ID,
            )

        to_right = remote(x_ref, o_ref.at[pl.ds(3 * rows, rows)], 0, right)
        to_left = remote(x_ref, o_ref.at[pl.ds(rows, rows)], 1, left)
        to_right.start()
        to_left.start()
        to_right.wait()
        to_left.wait()
        relay_right = remote(
            o_ref.at[pl.ds(3 * rows, half)], o_ref.at[pl.ds(2 * rows, half)], 2, right
        )
        relay_left = remote(
            o_ref.at[pl.ds(rows + half, half)], o_ref.at[pl.ds(2 * rows + half, half)], 3, left
        )
        relay_right.start()
        relay_left.start()
        relay_right.wait()
        relay_left.wait()
        own.wait()


def ring_gather(shard, stage, count, keep):
    rows, width = shard.shape
    return pl.pallas_call(
        functools.partial(ring_gather_kernel, stage, count),
        out_shape=jax.ShapeDtypeStruct((count * rows, width), shard.dtype),
        in_specs=[pl.BlockSpec(memory_space=pl.ANY), pl.BlockSpec(memory_space=pl.ANY)],
        out_specs=pl.BlockSpec(memory_space=pl.ANY),
        scratch_shapes=[
            pltpu.SemaphoreType.DMA((4,)),
            pltpu.SemaphoreType.DMA((4,)),
            pltpu.SemaphoreType.DMA(()),
        ],
        input_output_aliases={1: 0},
        compiler_params=pltpu.CompilerParams(collective_id=stage, has_side_effects=True),
    )(shard, keep)


def reduce_ring(partial, stage, count):
    rows = partial.shape[0] // count
    half = rows // 2
    blocks = [partial[k * rows : (k + 1) * rows] for k in range(count)]
    low = lambda value: value.astype(jnp.bfloat16)
    first_right = lax.ppermute(low(blocks[2][:half]), RING, shift_pairs(stage, count, 1))
    first_left = lax.ppermute(low(blocks[2][half:]), RING, shift_pairs(stage, count, -1))
    to_right = jnp.concatenate(
        [first_right.astype(jnp.float32) + blocks[1][:half], blocks[1][half:]], axis=0
    )
    to_left = jnp.concatenate(
        [blocks[3][:half], first_left.astype(jnp.float32) + blocks[3][half:]], axis=0
    )
    got_left = lax.ppermute(low(to_right), RING, shift_pairs(stage, count, 1))
    got_right = lax.ppermute(low(to_left), RING, shift_pairs(stage, count, -1))
    return blocks[0] + got_left.astype(jnp.float32) + got_right.astype(jnp.float32)


def swap(value):
    return lax.ppermute(value, "section", [(0, 1), (1, 0)])


def seq_pairs(count, step):
    return [(pos, (pos + step) % count) for pos in range(count)]


def reduce_seq(partial, count):
    rows = partial.shape[0] // count
    half = rows // 2
    blocks = [partial[k * rows : (k + 1) * rows] for k in range(count)]
    low = lambda value: value.astype(jnp.bfloat16)
    first_right = lax.ppermute(low(blocks[2][:half]), "seq", seq_pairs(count, 1))
    first_left = lax.ppermute(low(blocks[2][half:]), "seq", seq_pairs(count, -1))
    to_right = jnp.concatenate(
        [first_right.astype(jnp.float32) + blocks[1][:half], blocks[1][half:]], axis=0
    )
    to_left = jnp.concatenate(
        [blocks[3][:half], first_left.astype(jnp.float32) + blocks[3][half:]], axis=0
    )
    got_left = lax.ppermute(low(to_right), "seq", seq_pairs(count, 1))
    got_right = lax.ppermute(low(to_left), "seq", seq_pairs(count, -1))
    return blocks[0] + got_left.astype(jnp.float32) + got_right.astype(jnp.float32)


def body(section_input, saved_qkv, modulation, w_qkv, w_out, lengths, student_out, teacher_target):
    section_total = lax.axis_size("section")
    section_pos = lax.axis_index("section")
    seq_total = lax.axis_size("seq")
    seq_pos = lax.axis_index("seq")
    inputs = section_input[0, 0]
    saved_rows = saved_qkv[0, 0]
    weight_out = w_out[0]
    shard_rows, model_width = inputs.shape
    capacity = saved_rows.shape[0]
    local_width = saved_rows.shape[2]
    live_length = lengths[0]
    w_local = w_qkv[0]
    block_rows = w_local.shape[0]
    half_rows = block_rows // 2
    blocks_total = model_width // block_rows

    other_inputs = swap(inputs)
    other_mods = swap(modulation[0, 0])
    other_w = swap(w_local[half_rows:])
    parts = {}
    for stage in range(section_total):
        own = section_pos == stage
        x_stage = jnp.where(own, inputs, other_inputs)
        mods_stage = jnp.where(own, modulation[0, 0], other_mods)
        parts[stage] = (layer_norm_parts(x_stage), mods_stage)

    weights_of = {}
    for stage in reversed(range(section_total)):
        own = section_pos == stage
        contribution = jnp.where(own, w_local[:half_rows], other_w)
        weights_of[stage] = lax.all_gather(contribution, "dp", axis=0, tiled=True).reshape(
            blocks_total * half_rows, 3 * local_width
        )

    positions = seq_pos * shard_rows + jnp.arange(shard_rows, dtype=jnp.int32)
    row_live = positions < live_length
    gap = student_out[0].astype(jnp.float32) - teacher_target[0].astype(jnp.float32)
    loss_grad = jnp.where(row_live[:, None], gap, 0.0).astype(jnp.bfloat16)
    order = (seq_pos + jnp.arange(seq_total, dtype=jnp.int32)) % seq_total
    token_order = (order[:, None] * shard_rows + jnp.arange(shard_rows, dtype=jnp.int32)).reshape(-1)
    saved_off = jnp.take(saved_rows, token_order, axis=0)
    live_keys = token_order < live_length
    fwd = attend_forward(saved_off, live_keys, HEAD_DIM)
    attn_mixed = fwd[2].reshape(capacity, local_width)
    attn_mixed_t = lax.optimization_barrier(attn_mixed.T)

    def pick_half(value, own):
        split = value.reshape(value.shape[0], blocks_total, block_rows)
        chosen = jnp.where(own, split[:, :, :half_rows], split[:, :, half_rows:])
        return chosen.reshape(value.shape[0], blocks_total * half_rows)

    def section_work(d_output, stage, keep):
        own = section_pos == stage
        (normed, inverse), mods_stage = parts[stage]
        scale_term = mods_stage[0]
        gate_term = mods_stage[1]
        d_branch = (gate_term * d_output.astype(jnp.float32)).astype(jnp.bfloat16)
        if stage == section_total - 1:
            branch_full = gather_ring(d_branch, stage, seq_total)
        else:
            branch_full = ring_gather(d_branch, stage, seq_total, keep)
        d_attn = jnp.dot(branch_full, weight_out.T, preferred_element_type=jnp.float32).astype(
            jnp.bfloat16
        )
        own_grads = attend_backward(saved_off, fwd, d_attn, HEAD_DIM)
        handed = lax.ppermute(own_grads, "section", [(stage, 1 - stage)])
        flat_grads = jnp.where(own, own_grads, handed)
        d_mod_part = jnp.dot(flat_grads, weights_of[stage].T, preferred_element_type=jnp.float32)
        d_mod = reduce_seq(d_mod_part, seq_total)
        normed_half = pick_half(normed, own)
        d_norm = d_mod * (1.0 + pick_half(scale_term[None], own))
        sums = jnp.stack([jnp.sum(d_norm, axis=-1), jnp.sum(d_norm * normed_half, axis=-1)])
        sums = (sums + swap(sums)) / model_width
        d_layer = inverse * (d_norm - sums[0][:, None] - normed_half * sums[1][:, None])
        d_half = (pick_half(d_output, own).astype(jnp.float32) + d_layer).astype(
            jnp.bfloat16
        )
        other_half = swap(d_half)
        mine = d_half.reshape(shard_rows, blocks_total, half_rows)
        theirs = other_half.reshape(shard_rows, blocks_total, half_rows)
        joined = jnp.concatenate(
            [jnp.where(own, mine, theirs), jnp.where(own, theirs, mine)], axis=2
        )
        return joined.reshape(shard_rows, model_width), branch_full

    incoming = loss_grad
    grad_input = None
    branch_own = None
    for stage in reversed(range(section_total)):
        d_input, branch_full = section_work(incoming, stage, branch_own)
        here = section_pos == stage
        grad_input = d_input if grad_input is None else jnp.where(here, d_input, grad_input)
        branch_own = branch_full
        incoming = d_input
    out_local = jnp.dot(attn_mixed_t, branch_own, preferred_element_type=jnp.float32)
    out_slice = lax.psum_scatter(out_local, "dp", scatter_dimension=1, tiled=True)
    return (grad_input[None, None], out_slice.astype(jnp.bfloat16)[None])


def solution(mesh):
    in_specs = (
        P("section", "dp", "seq", None),
        P("section", "dp", None, None, "seq"),
        P("section", "dp", None, None),
        P("section", "dp", None, "seq"),
        P("section", "seq", None),
        P("dp"),
        P("dp", "seq", None),
        P("dp", "seq", None),
    )
    out_specs = (P("section", "dp", "seq", None), P("section", "seq", "dp"))
    return jax.shard_map(body, mesh=mesh, in_specs=in_specs, out_specs=out_specs, check_vma=False)
```

```python
import functools
import math

import jax
import jax.numpy as jnp
from jax import lax
from jax.experimental import pallas as pl
from jax.experimental.pallas import tpu as pltpu
from jax.sharding import PartitionSpec as P

HEAD_DIM = 128


def widen(tensor):
    return lax.optimization_barrier(tensor).astype(jnp.float32)


def layer_norm_parts(tokens):
    values = tokens.astype(jnp.float32)
    center = values - jnp.mean(values, axis=-1, keepdims=True)
    variance = jnp.mean(center * center, axis=-1, keepdims=True)
    inverse = lax.rsqrt(variance + 1e-06)
    return (center * inverse, inverse)


def attend_forward(saved_rows, live_keys, head_size):
    row_total = saved_rows.shape[0]
    feature_width = saved_rows.shape[2]
    head_count = feature_width // head_size
    queries = saved_rows[:, 0].reshape(row_total, head_count, head_size)
    key_rows = saved_rows[:, 1].reshape(row_total, head_count, head_size)
    value_rows = saved_rows[:, 2].reshape(row_total, head_count, head_size)
    factor = 1.0 / math.sqrt(head_size)
    scores = jnp.einsum("qhd,khd->hqk", queries, key_rows, preferred_element_type=jnp.float32)
    scores = scores * factor
    scores = jnp.where(live_keys[None, None, :], scores, -1e30)
    peak_score = jnp.max(scores, axis=-1, keepdims=True)
    weights = jnp.exp(scores - peak_score)
    weights = weights / jnp.sum(weights, axis=-1, keepdims=True)
    rounded = lax.optimization_barrier(weights.astype(jnp.bfloat16))
    attn_mixed = jnp.einsum(
        "hqk,khd->qhd", rounded, value_rows, preferred_element_type=jnp.float32
    ).astype(jnp.bfloat16)
    return weights, rounded, attn_mixed


def attend_backward(saved_rows, fwd, d_attn, head_size):
    weights, rounded, attn_mixed = fwd
    row_total = saved_rows.shape[0]
    feature_width = saved_rows.shape[2]
    head_count = feature_width // head_size
    queries = saved_rows[:, 0].reshape(row_total, head_count, head_size)
    key_rows = saved_rows[:, 1].reshape(row_total, head_count, head_size)
    value_rows = saved_rows[:, 2].reshape(row_total, head_count, head_size)
    factor = 1.0 / math.sqrt(head_size)
    upstream = d_attn.reshape(row_total, head_count, head_size)
    f32 = jnp.float32
    d_weights = jnp.einsum("qhd,khd->hqk", upstream, value_rows, preferred_element_type=f32)
    delta_rows = jnp.einsum("qhd,qhd->hq", upstream.astype(f32), widen(attn_mixed))
    d_scores = lax.optimization_barrier(
        (weights * (d_weights - delta_rows[:, :, None]) * factor).astype(jnp.bfloat16)
    )
    grad_q = jnp.einsum("hqk,khd->qhd", d_scores, key_rows, preferred_element_type=f32)
    grad_k = jnp.einsum("hqk,qhd->khd", d_scores, queries, preferred_element_type=f32)
    grad_v = jnp.einsum("hqk,qhd->khd", rounded, upstream, preferred_element_type=f32)
    stacked = jnp.stack(
        [grad_q.astype(jnp.bfloat16), grad_k.astype(jnp.bfloat16), grad_v.astype(jnp.bfloat16)],
        axis=1,
    ).reshape(row_total, 3 * feature_width)
    return stacked


RING = ("section", "seq")


def shift_pairs(stage, count, step):
    base = stage * count
    return [(base + pos, base + (pos + step) % count) for pos in range(count)]


def gather_ring(shard, stage, count):
    half = shard.shape[0] // 2
    from_left = lax.ppermute(shard, RING, shift_pairs(stage, count, 1))
    from_right = lax.ppermute(shard, RING, shift_pairs(stage, count, -1))
    far_top = lax.ppermute(from_left[:half], RING, shift_pairs(stage, count, 1))
    far_bottom = lax.ppermute(from_right[half:], RING, shift_pairs(stage, count, -1))
    far = jnp.concatenate([far_top, far_bottom], axis=0)
    return jnp.concatenate([shard, from_right, far, from_left], axis=0)


MESH_ID = pl.DeviceIdType.MESH


def ring_gather_kernel(stage, count, x_ref, keep_ref, o_ref, send_sem, recv_sem, own_sem):
    rows = x_ref.shape[0]
    half = rows // 2
    pos = lax.axis_index("seq")
    dp_pos = lax.axis_index("dp")

    @pl.when(lax.axis_index("section") == stage)
    def _():
        right = lax.rem(pos + 1, count)
        left = lax.rem(pos + count - 1, count)
        barrier = pltpu.get_barrier_semaphore()
        for neighbour in (left, right):
            pl.semaphore_signal(
                barrier, inc=1, device_id=(stage, neighbour, dp_pos), device_id_type=MESH_ID
            )
        pl.semaphore_wait(barrier, 2)
        own = pltpu.make_async_copy(x_ref, o_ref.at[pl.ds(0, rows)], own_sem)
        own.start()

        def remote(src, dst, slot, target):
            return pltpu.make_async_remote_copy(
                src_ref=src,
                dst_ref=dst,
                send_sem=send_sem.at[slot],
                recv_sem=recv_sem.at[slot],
                device_id=(stage, target, dp_pos),
                device_id_type=MESH_ID,
            )

        to_right = remote(x_ref, o_ref.at[pl.ds(3 * rows, rows)], 0, right)
        to_left = remote(x_ref, o_ref.at[pl.ds(rows, rows)], 1, left)
        to_right.start()
        to_left.start()
        to_right.wait()
        to_left.wait()
        relay_right = remote(
            o_ref.at[pl.ds(3 * rows, half)], o_ref.at[pl.ds(2 * rows, half)], 2, right
        )
        relay_left = remote(
            o_ref.at[pl.ds(rows + half, half)], o_ref.at[pl.ds(2 * rows + half, half)], 3, left
        )
        relay_right.start()
        relay_left.start()
        relay_right.wait()
        relay_left.wait()
        own.wait()


def ring_gather(shard, stage, count, keep):
    rows, width = shard.shape
    return pl.pallas_call(
        functools.partial(ring_gather_kernel, stage, count),
        out_shape=jax.ShapeDtypeStruct((count * rows, width), shard.dtype),
        in_specs=[pl.BlockSpec(memory_space=pl.ANY), pl.BlockSpec(memory_space=pl.ANY)],
        out_specs=pl.BlockSpec(memory_space=pl.ANY),
        scratch_shapes=[
            pltpu.SemaphoreType.DMA((4,)),
            pltpu.SemaphoreType.DMA((4,)),
            pltpu.SemaphoreType.DMA(()),
        ],
        input_output_aliases={1: 0},
        compiler_params=pltpu.CompilerParams(collective_id=stage, has_side_effects=True),
    )(shard, keep)


def reduce_ring(partial, stage, count):
    rows = partial.shape[0] // count
    half = rows // 2
    blocks = [partial[k * rows : (k + 1) * rows] for k in range(count)]
    low = lambda value: value.astype(jnp.bfloat16)
    first_right = lax.ppermute(low(blocks[2][:half]), RING, shift_pairs(stage, count, 1))
    first_left = lax.ppermute(low(blocks[2][half:]), RING, shift_pairs(stage, count, -1))
    to_right = jnp.concatenate(
        [first_right.astype(jnp.float32) + blocks[1][:half], blocks[1][half:]], axis=0
    )
    to_left = jnp.concatenate(
        [blocks[3][:half], first_left.astype(jnp.float32) + blocks[3][half:]], axis=0
    )
    got_left = lax.ppermute(low(to_right), RING, shift_pairs(stage, count, 1))
    got_right = lax.ppermute(low(to_left), RING, shift_pairs(stage, count, -1))
    return blocks[0] + got_left.astype(jnp.float32) + got_right.astype(jnp.float32)


def swap(value):
    return lax.ppermute(value, "section", [(0, 1), (1, 0)])


def seq_pairs(count, step):
    return [(pos, (pos + step) % count) for pos in range(count)]


def reduce_seq(partial, count):
    rows = partial.shape[0] // count
    half = rows // 2
    blocks = [partial[k * rows : (k + 1) * rows] for k in range(count)]
    low = lambda value: value.astype(jnp.bfloat16)
    first_right = lax.ppermute(low(blocks[2][:half]), "seq", seq_pairs(count, 1))
    first_left = lax.ppermute(low(blocks[2][half:]), "seq", seq_pairs(count, -1))
    to_right = jnp.concatenate(
        [first_right.astype(jnp.float32) + blocks[1][:half], blocks[1][half:]], axis=0
    )
    to_left = jnp.concatenate(
        [blocks[3][:half], first_left.astype(jnp.float32) + blocks[3][half:]], axis=0
    )
    got_left = lax.ppermute(low(to_right), "seq", seq_pairs(count, 1))
    got_right = lax.ppermute(low(to_left), "seq", seq_pairs(count, -1))
    return blocks[0] + got_left.astype(jnp.float32) + got_right.astype(jnp.float32)


def body(section_input, saved_qkv, modulation, w_qkv, w_out, lengths, student_out, teacher_target):
    section_total = lax.axis_size("section")
    section_pos = lax.axis_index("section")
    seq_total = lax.axis_size("seq")
    seq_pos = lax.axis_index("seq")
    inputs = section_input[0, 0]
    saved_rows = saved_qkv[0, 0]
    weight_out = w_out[0]
    shard_rows, model_width = inputs.shape
    capacity = saved_rows.shape[0]
    local_width = saved_rows.shape[2]
    live_length = lengths[0]
    w_local = w_qkv[0]
    block_rows = w_local.shape[0]
    half_rows = block_rows // 2
    blocks_total = model_width // block_rows

    other_inputs = swap(inputs)
    other_mods = swap(modulation[0, 0])
    other_w = swap(w_local[half_rows:])
    parts = {}
    for stage in range(section_total):
        own = section_pos == stage
        x_stage = jnp.where(own, inputs, other_inputs)
        mods_stage = jnp.where(own, modulation[0, 0], other_mods)
        parts[stage] = (layer_norm_parts(x_stage), mods_stage)

    weights_of = {}
    for stage in reversed(range(section_total)):
        own = section_pos == stage
        contribution = jnp.where(own, w_local[:half_rows], other_w)
        weights_of[stage] = lax.all_gather(contribution, "dp", axis=0, tiled=True).reshape(
            blocks_total * half_rows, 3 * local_width
        )

    positions = seq_pos * shard_rows + jnp.arange(shard_rows, dtype=jnp.int32)
    row_live = positions < live_length
    gap = student_out[0].astype(jnp.float32) - teacher_target[0].astype(jnp.float32)
    loss_grad = jnp.where(row_live[:, None], gap, 0.0).astype(jnp.bfloat16)
    order = (seq_pos + jnp.arange(seq_total, dtype=jnp.int32)) % seq_total
    token_order = (order[:, None] * shard_rows + jnp.arange(shard_rows, dtype=jnp.int32)).reshape(-1)
    saved_off = jnp.take(saved_rows, token_order, axis=0)
    live_keys = token_order < live_length
    fwd = attend_forward(saved_off, live_keys, HEAD_DIM)
    attn_mixed = fwd[2].reshape(capacity, local_width)
    attn_mixed_t = lax.optimization_barrier(attn_mixed.T)

    def pick_half(value, own):
        split = value.reshape(value.shape[0], blocks_total, block_rows)
        chosen = jnp.where(own, split[:, :, :half_rows], split[:, :, half_rows:])
        return chosen.reshape(value.shape[0], blocks_total * half_rows)

    def section_work(d_output, stage, keep):
        own = section_pos == stage
        (normed, inverse), mods_stage = parts[stage]
        scale_term = mods_stage[0]
        gate_term = mods_stage[1]
        d_branch = (gate_term * d_output.astype(jnp.float32)).astype(jnp.bfloat16)
        if stage == section_total - 1:
            branch_full = gather_ring(d_branch, stage, seq_total)
        else:
            branch_full = ring_gather(d_branch, stage, seq_total, keep)
        d_attn = jnp.dot(branch_full, weight_out.T, preferred_element_type=jnp.float32).astype(
            jnp.bfloat16
        )
        own_grads = attend_backward(saved_off, fwd, d_attn, HEAD_DIM)
        handed = lax.ppermute(own_grads, "section", [(stage, 1 - stage)])
        flat_grads = jnp.where(own, own_grads, handed)
        d_mod_part = jnp.dot(flat_grads, weights_of[stage].T, preferred_element_type=jnp.float32)
        d_mod = reduce_seq(d_mod_part, seq_total)
        normed_half = pick_half(normed, own)
        d_norm = d_mod * (1.0 + pick_half(scale_term[None], own))
        sums = jnp.stack([jnp.sum(d_norm, axis=-1), jnp.sum(d_norm * normed_half, axis=-1)])
        sums = (sums + swap(sums)) / model_width
        d_layer = inverse * (d_norm - sums[0][:, None] - normed_half * sums[1][:, None])
        d_half = (pick_half(d_output, own).astype(jnp.float32) + d_layer).astype(
            jnp.bfloat16
        )
        other_half = swap(d_half)
        mine = d_half.reshape(shard_rows, blocks_total, half_rows)
        theirs = other_half.reshape(shard_rows, blocks_total, half_rows)
        joined = jnp.concatenate(
            [jnp.where(own, mine, theirs), jnp.where(own, theirs, mine)], axis=2
        )
        return joined.reshape(shard_rows, model_width), branch_full

    incoming = loss_grad
    grad_input = None
    branch_own = None
    for stage in reversed(range(section_total)):
        d_input, branch_full = section_work(incoming, stage, branch_own)
        here = section_pos == stage
        grad_input = d_input if grad_input is None else jnp.where(here, d_input, grad_input)
        branch_own = branch_full
        incoming = d_input
    out_local = jnp.dot(attn_mixed_t, branch_own, preferred_element_type=jnp.float32)
    out_slice = lax.psum_scatter(out_local, "dp", scatter_dimension=1, tiled=True)
    return (grad_input[None, None], out_slice.astype(jnp.bfloat16)[None])


def solution(mesh):
    in_specs = (
        P("section", "dp", "seq", None),
        P("section", "dp", None, None, "seq"),
        P("section", "dp", None, None),
        P("section", "dp", None, "seq"),
        P("section", "seq", None),
        P("dp"),
        P("dp", "seq", None),
        P("dp", "seq", None),
    )
    out_specs = (P("section", "dp", "seq", None), P("section", "seq", "dp"))
    return jax.shard_map(body, mesh=mesh, in_specs=in_specs, out_specs=out_specs, check_vma=False)
```

```python
import functools
import math

import jax
import jax.numpy as jnp
from jax import lax
from jax.experimental import pallas as pl
from jax.experimental.pallas import tpu as pltpu
from jax.sharding import PartitionSpec as P

HEAD_DIM = 128


def widen(tensor):
    return lax.optimization_barrier(tensor).astype(jnp.float32)


def layer_norm_parts(tokens):
    values = tokens.astype(jnp.float32)
    center = values - jnp.mean(values, axis=-1, keepdims=True)
    variance = jnp.mean(center * center, axis=-1, keepdims=True)
    inverse = lax.rsqrt(variance + 1e-06)
    return (center * inverse, inverse)


def attend_forward(saved_rows, live_keys, head_size):
    row_total = saved_rows.shape[0]
    feature_width = saved_rows.shape[2]
    head_count = feature_width // head_size
    queries = saved_rows[:, 0].reshape(row_total, head_count, head_size).astype(jnp.float32)
    key_rows = saved_rows[:, 1].reshape(row_total, head_count, head_size).astype(jnp.float32)
    value_rows = saved_rows[:, 2].reshape(row_total, head_count, head_size).astype(jnp.float32)
    factor = 1.0 / math.sqrt(head_size)
    scores = jnp.einsum("qhd,khd->hqk", queries, key_rows) * factor
    scores = jnp.where(live_keys[None, None, :], scores, -1e30)
    peak_score = jnp.max(scores, axis=-1, keepdims=True)
    weights = jnp.exp(scores - peak_score)
    weights = weights / jnp.sum(weights, axis=-1, keepdims=True)
    rounded = widen(weights.astype(jnp.bfloat16))
    attn_mixed = jnp.einsum("hqk,khd->qhd", rounded, value_rows).astype(jnp.bfloat16)
    return weights, rounded, attn_mixed


def attend_backward(saved_rows, fwd, d_attn, head_size):
    weights, rounded, attn_mixed = fwd
    row_total = saved_rows.shape[0]
    feature_width = saved_rows.shape[2]
    head_count = feature_width // head_size
    queries = saved_rows[:, 0].reshape(row_total, head_count, head_size).astype(jnp.float32)
    key_rows = saved_rows[:, 1].reshape(row_total, head_count, head_size).astype(jnp.float32)
    value_rows = saved_rows[:, 2].reshape(row_total, head_count, head_size).astype(jnp.float32)
    factor = 1.0 / math.sqrt(head_size)
    upstream = d_attn.reshape(row_total, head_count, head_size).astype(jnp.float32)
    d_weights = jnp.einsum("qhd,khd->hqk", upstream, value_rows)
    delta_rows = jnp.einsum("qhd,qhd->hq", upstream, widen(attn_mixed))
    d_scores = widen((weights * (d_weights - delta_rows[:, :, None]) * factor).astype(jnp.bfloat16))
    grad_q = jnp.einsum("hqk,khd->qhd", d_scores, key_rows).astype(jnp.bfloat16)
    grad_k = jnp.einsum("hqk,qhd->khd", d_scores, queries).astype(jnp.bfloat16)
    grad_v = jnp.einsum("hqk,qhd->khd", rounded, upstream).astype(jnp.bfloat16)
    stacked = jnp.stack([grad_q, grad_k, grad_v], axis=1).reshape(row_total, 3 * feature_width)
    return stacked


RING = ("section", "seq")


def shift_pairs(stage, count, step):
    base = stage * count
    return [(base + pos, base + (pos + step) % count) for pos in range(count)]


def gather_ring(shard, stage, count):
    half = shard.shape[0] // 2
    from_left = lax.ppermute(shard, RING, shift_pairs(stage, count, 1))
    from_right = lax.ppermute(shard, RING, shift_pairs(stage, count, -1))
    far_top = lax.ppermute(from_left[:half], RING, shift_pairs(stage, count, 1))
    far_bottom = lax.ppermute(from_right[half:], RING, shift_pairs(stage, count, -1))
    far = jnp.concatenate([far_top, far_bottom], axis=0)
    return jnp.concatenate([shard, from_right, far, from_left], axis=0)


MESH_ID = pl.DeviceIdType.MESH


def ring_gather_kernel(stage, count, x_ref, keep_ref, o_ref, send_sem, recv_sem, own_sem):
    rows = x_ref.shape[0]
    half = rows // 2
    pos = lax.axis_index("seq")
    dp_pos = lax.axis_index("dp")

    @pl.when(lax.axis_index("section") == stage)
    def _():
        right = lax.rem(pos + 1, count)
        left = lax.rem(pos + count - 1, count)
        barrier = pltpu.get_barrier_semaphore()
        for neighbour in (left, right):
            pl.semaphore_signal(
                barrier, inc=1, device_id=(stage, neighbour, dp_pos), device_id_type=MESH_ID
            )
        pl.semaphore_wait(barrier, 2)
        own = pltpu.make_async_copy(x_ref, o_ref.at[pl.ds(0, rows)], own_sem)
        own.start()

        def remote(src, dst, slot, target):
            return pltpu.make_async_remote_copy(
                src_ref=src,
                dst_ref=dst,
                send_sem=send_sem.at[slot],
                recv_sem=recv_sem.at[slot],
                device_id=(stage, target, dp_pos),
                device_id_type=MESH_ID,
            )

        to_right = remote(x_ref, o_ref.at[pl.ds(3 * rows, rows)], 0, right)
        to_left = remote(x_ref, o_ref.at[pl.ds(rows, rows)], 1, left)
        to_right.start()
        to_left.start()
        to_right.wait()
        to_left.wait()
        relay_right = remote(
            o_ref.at[pl.ds(3 * rows, half)], o_ref.at[pl.ds(2 * rows, half)], 2, right
        )
        relay_left = remote(
            o_ref.at[pl.ds(rows + half, half)], o_ref.at[pl.ds(2 * rows + half, half)], 3, left
        )
        relay_right.start()
        relay_left.start()
        relay_right.wait()
        relay_left.wait()
        own.wait()


def ring_gather(shard, stage, count, keep):
    rows, width = shard.shape
    return pl.pallas_call(
        functools.partial(ring_gather_kernel, stage, count),
        out_shape=jax.ShapeDtypeStruct((count * rows, width), shard.dtype),
        in_specs=[pl.BlockSpec(memory_space=pl.ANY), pl.BlockSpec(memory_space=pl.ANY)],
        out_specs=pl.BlockSpec(memory_space=pl.ANY),
        scratch_shapes=[
            pltpu.SemaphoreType.DMA((4,)),
            pltpu.SemaphoreType.DMA((4,)),
            pltpu.SemaphoreType.DMA(()),
        ],
        input_output_aliases={1: 0},
        compiler_params=pltpu.CompilerParams(collective_id=stage, has_side_effects=True),
    )(shard, keep)


def reduce_ring(partial, stage, count):
    rows = partial.shape[0] // count
    half = rows // 2
    blocks = [partial[k * rows : (k + 1) * rows] for k in range(count)]
    low = lambda value: value.astype(jnp.bfloat16)
    first_right = lax.ppermute(low(blocks[2][:half]), RING, shift_pairs(stage, count, 1))
    first_left = lax.ppermute(low(blocks[2][half:]), RING, shift_pairs(stage, count, -1))
    to_right = jnp.concatenate(
        [first_right.astype(jnp.float32) + blocks[1][:half], blocks[1][half:]], axis=0
    )
    to_left = jnp.concatenate(
        [blocks[3][:half], first_left.astype(jnp.float32) + blocks[3][half:]], axis=0
    )
    got_left = lax.ppermute(low(to_right), RING, shift_pairs(stage, count, 1))
    got_right = lax.ppermute(low(to_left), RING, shift_pairs(stage, count, -1))
    return blocks[0] + got_left.astype(jnp.float32) + got_right.astype(jnp.float32)


def swap(value):
    return lax.ppermute(value, "section", [(0, 1), (1, 0)])


def seq_pairs(count, step):
    return [(pos, (pos + step) % count) for pos in range(count)]


def reduce_seq(partial, count):
    rows = partial.shape[0] // count
    half = rows // 2
    blocks = [partial[k * rows : (k + 1) * rows] for k in range(count)]
    low = lambda value: value.astype(jnp.bfloat16)
    first_right = lax.ppermute(low(blocks[2][:half]), "seq", seq_pairs(count, 1))
    first_left = lax.ppermute(low(blocks[2][half:]), "seq", seq_pairs(count, -1))
    to_right = jnp.concatenate(
        [first_right.astype(jnp.float32) + blocks[1][:half], blocks[1][half:]], axis=0
    )
    to_left = jnp.concatenate(
        [blocks[3][:half], first_left.astype(jnp.float32) + blocks[3][half:]], axis=0
    )
    got_left = lax.ppermute(low(to_right), "seq", seq_pairs(count, 1))
    got_right = lax.ppermute(low(to_left), "seq", seq_pairs(count, -1))
    return blocks[0] + got_left.astype(jnp.float32) + got_right.astype(jnp.float32)


def body(section_input, saved_qkv, modulation, w_qkv, w_out, lengths, student_out, teacher_target):
    section_total = lax.axis_size("section")
    section_pos = lax.axis_index("section")
    seq_total = lax.axis_size("seq")
    seq_pos = lax.axis_index("seq")
    inputs = section_input[0, 0]
    saved_rows = saved_qkv[0, 0]
    weight_out = w_out[0]
    shard_rows, model_width = inputs.shape
    capacity = saved_rows.shape[0]
    local_width = saved_rows.shape[2]
    live_length = lengths[0]
    w_local = w_qkv[0]
    block_rows = w_local.shape[0]
    half_rows = block_rows // 2
    blocks_total = model_width // block_rows

    other_inputs = swap(inputs)
    other_mods = swap(modulation[0, 0])
    other_w = swap(w_local[half_rows:])
    parts = {}
    for stage in range(section_total):
        own = section_pos == stage
        x_stage = jnp.where(own, inputs, other_inputs)
        mods_stage = jnp.where(own, modulation[0, 0], other_mods)
        parts[stage] = (layer_norm_parts(x_stage), mods_stage)

    weights_of = {}
    for stage in reversed(range(section_total)):
        own = section_pos == stage
        contribution = jnp.where(own, w_local[:half_rows], other_w)
        weights_of[stage] = lax.all_gather(contribution, "dp", axis=0, tiled=True).reshape(
            blocks_total * half_rows, 3 * local_width
        )

    positions = seq_pos * shard_rows + jnp.arange(shard_rows, dtype=jnp.int32)
    row_live = positions < live_length
    gap = student_out[0].astype(jnp.float32) - teacher_target[0].astype(jnp.float32)
    loss_grad = jnp.where(row_live[:, None], gap, 0.0).astype(jnp.bfloat16)
    order = (seq_pos + jnp.arange(seq_total, dtype=jnp.int32)) % seq_total
    token_order = (order[:, None] * shard_rows + jnp.arange(shard_rows, dtype=jnp.int32)).reshape(-1)
    saved_off = jnp.take(saved_rows, token_order, axis=0)
    live_keys = token_order < live_length
    last = section_total - 1
    first_branch = (parts[last][1][1] * loss_grad.astype(jnp.float32)).astype(jnp.bfloat16)
    first_left = lax.ppermute(first_branch, RING, shift_pairs(last, seq_total, 1))
    first_right = lax.ppermute(first_branch, RING, shift_pairs(last, seq_total, -1))
    saved_off, first_left, first_right = lax.optimization_barrier(
        (saved_off, first_left, first_right)
    )
    fwd = attend_forward(saved_off, live_keys, HEAD_DIM)
    attn_mixed = fwd[2].reshape(capacity, local_width)
    attn_mixed_t = lax.optimization_barrier(attn_mixed.T)

    def pick_half(value, own):
        split = value.reshape(value.shape[0], blocks_total, block_rows)
        chosen = jnp.where(own, split[:, :, :half_rows], split[:, :, half_rows:])
        return chosen.reshape(value.shape[0], blocks_total * half_rows)

    def section_work(d_output, stage, keep):
        own = section_pos == stage
        (normed, inverse), mods_stage = parts[stage]
        scale_term = mods_stage[0]
        gate_term = mods_stage[1]
        d_branch = (gate_term * d_output.astype(jnp.float32)).astype(jnp.bfloat16)
        if stage == section_total - 1:
            half_block = shard_rows // 2
            far_top = lax.ppermute(first_left[:half_block], RING, shift_pairs(stage, seq_total, 1))
            far_bottom = lax.ppermute(
                first_right[half_block:], RING, shift_pairs(stage, seq_total, -1)
            )
            far = jnp.concatenate([far_top, far_bottom], axis=0)
            branch_full = jnp.concatenate([first_branch, first_right, far, first_left], axis=0)
        else:
            branch_full = ring_gather(d_branch, stage, seq_total, keep)
        d_attn = jnp.dot(branch_full, weight_out.T, preferred_element_type=jnp.float32).astype(
            jnp.bfloat16
        )
        own_grads = attend_backward(saved_off, fwd, d_attn, HEAD_DIM)
        handed = lax.ppermute(own_grads, "section", [(stage, 1 - stage)])
        flat_grads = jnp.where(own, own_grads, handed)
        d_mod_part = jnp.dot(flat_grads, weights_of[stage].T, preferred_element_type=jnp.float32)
        d_mod = reduce_seq(d_mod_part, seq_total)
        normed_half = pick_half(normed, own)
        d_norm = d_mod * (1.0 + pick_half(scale_term[None], own))
        sums = jnp.stack([jnp.sum(d_norm, axis=-1), jnp.sum(d_norm * normed_half, axis=-1)])
        sums = (sums + swap(sums)) / model_width
        d_layer = inverse * (d_norm - sums[0][:, None] - normed_half * sums[1][:, None])
        d_half = (pick_half(d_output, own).astype(jnp.float32) + d_layer).astype(
            jnp.bfloat16
        )
        other_half = swap(d_half)
        mine = d_half.reshape(shard_rows, blocks_total, half_rows)
        theirs = other_half.reshape(shard_rows, blocks_total, half_rows)
        joined = jnp.concatenate(
            [jnp.where(own, mine, theirs), jnp.where(own, theirs, mine)], axis=2
        )
        return joined.reshape(shard_rows, model_width), branch_full

    incoming = loss_grad
    grad_input = None
    branch_own = None
    for stage in reversed(range(section_total)):
        d_input, branch_full = section_work(incoming, stage, branch_own)
        here = section_pos == stage
        grad_input = d_input if grad_input is None else jnp.where(here, d_input, grad_input)
        branch_own = branch_full
        incoming = d_input
    out_local = jnp.dot(attn_mixed_t, branch_own, preferred_element_type=jnp.float32)
    out_slice = lax.psum_scatter(out_local, "dp", scatter_dimension=1, tiled=True)
    return (grad_input[None, None], out_slice.astype(jnp.bfloat16)[None])


def solution(mesh):
    in_specs = (
        P("section", "dp", "seq", None),
        P("section", "dp", None, None, "seq"),
        P("section", "dp", None, None),
        P("section", "dp", None, "seq"),
        P("section", "seq", None),
        P("dp"),
        P("dp", "seq", None),
        P("dp", "seq", None),
    )
    out_specs = (P("section", "dp", "seq", None), P("section", "seq", "dp"))
    return jax.shard_map(body, mesh=mesh, in_specs=in_specs, out_specs=out_specs, check_vma=False)
```

```python
import functools
import math

import jax
import jax.numpy as jnp
from jax import lax
from jax.experimental import pallas as pl
from jax.experimental.pallas import tpu as pltpu
from jax.sharding import PartitionSpec as P

HEAD_DIM = 128


def widen(tensor):
    return lax.optimization_barrier(tensor).astype(jnp.float32)


def layer_norm_parts(tokens):
    values = tokens.astype(jnp.float32)
    center = values - jnp.mean(values, axis=-1, keepdims=True)
    variance = jnp.mean(center * center, axis=-1, keepdims=True)
    inverse = lax.rsqrt(variance + 1e-06)
    return (center * inverse, inverse)


def attend_forward(saved_rows, live_keys, head_size):
    row_total = saved_rows.shape[0]
    feature_width = saved_rows.shape[2]
    head_count = feature_width // head_size
    queries = saved_rows[:, 0].reshape(row_total, head_count, head_size).astype(jnp.float32)
    key_rows = saved_rows[:, 1].reshape(row_total, head_count, head_size).astype(jnp.float32)
    value_rows = saved_rows[:, 2].reshape(row_total, head_count, head_size).astype(jnp.float32)
    factor = 1.0 / math.sqrt(head_size)
    scores = jnp.einsum("qhd,khd->hqk", queries, key_rows) * factor
    scores = jnp.where(live_keys[None, None, :], scores, -1e30)
    peak_score = jnp.max(scores, axis=-1, keepdims=True)
    weights = jnp.exp(scores - peak_score)
    weights = weights / jnp.sum(weights, axis=-1, keepdims=True)
    rounded = widen(weights.astype(jnp.bfloat16))
    attn_mixed = jnp.einsum("hqk,khd->qhd", rounded, value_rows).astype(jnp.bfloat16)
    return weights, rounded, attn_mixed


def attend_backward(saved_rows, fwd, d_attn, head_size):
    weights, rounded, attn_mixed = fwd
    row_total = saved_rows.shape[0]
    feature_width = saved_rows.shape[2]
    head_count = feature_width // head_size
    queries = saved_rows[:, 0].reshape(row_total, head_count, head_size).astype(jnp.float32)
    key_rows = saved_rows[:, 1].reshape(row_total, head_count, head_size).astype(jnp.float32)
    value_rows = saved_rows[:, 2].reshape(row_total, head_count, head_size).astype(jnp.float32)
    factor = 1.0 / math.sqrt(head_size)
    upstream = d_attn.reshape(row_total, head_count, head_size).astype(jnp.float32)
    d_weights = jnp.einsum("qhd,khd->hqk", upstream, value_rows)
    delta_rows = jnp.einsum("qhd,qhd->hq", upstream, widen(attn_mixed))
    d_scores = widen((weights * (d_weights - delta_rows[:, :, None]) * factor).astype(jnp.bfloat16))
    grad_q = jnp.einsum("hqk,khd->qhd", d_scores, key_rows).astype(jnp.bfloat16)
    grad_k = jnp.einsum("hqk,qhd->khd", d_scores, queries).astype(jnp.bfloat16)
    grad_v = jnp.einsum("hqk,qhd->khd", rounded, upstream).astype(jnp.bfloat16)
    stacked = jnp.stack([grad_q, grad_k, grad_v], axis=1).reshape(row_total, 3 * feature_width)
    return stacked


RING = ("section", "seq")


def shift_pairs(stage, count, step):
    base = stage * count
    return [(base + pos, base + (pos + step) % count) for pos in range(count)]


def gather_ring(shard, stage, count):
    half = shard.shape[0] // 2
    from_left = lax.ppermute(shard, RING, shift_pairs(stage, count, 1))
    from_right = lax.ppermute(shard, RING, shift_pairs(stage, count, -1))
    far_top = lax.ppermute(from_left[:half], RING, shift_pairs(stage, count, 1))
    far_bottom = lax.ppermute(from_right[half:], RING, shift_pairs(stage, count, -1))
    far = jnp.concatenate([far_top, far_bottom], axis=0)
    return jnp.concatenate([shard, from_right, far, from_left], axis=0)


MESH_ID = pl.DeviceIdType.MESH


def ring_gather_kernel(stage, count, x_ref, keep_ref, o_ref, send_sem, recv_sem, own_sem):
    rows = x_ref.shape[0]
    half = rows // 2
    pos = lax.axis_index("seq")
    dp_pos = lax.axis_index("dp")

    @pl.when(lax.axis_index("section") == stage)
    def _():
        right = lax.rem(pos + 1, count)
        left = lax.rem(pos + count - 1, count)
        barrier = pltpu.get_barrier_semaphore()
        for neighbour in (left, right):
            pl.semaphore_signal(
                barrier, inc=1, device_id=(stage, neighbour, dp_pos), device_id_type=MESH_ID
            )
        pl.semaphore_wait(barrier, 2)
        own = pltpu.make_async_copy(x_ref, o_ref.at[pl.ds(0, rows)], own_sem)
        own.start()

        def remote(src, dst, slot, target):
            return pltpu.make_async_remote_copy(
                src_ref=src,
                dst_ref=dst,
                send_sem=send_sem.at[slot],
                recv_sem=recv_sem.at[slot],
                device_id=(stage, target, dp_pos),
                device_id_type=MESH_ID,
            )

        to_right = remote(x_ref, o_ref.at[pl.ds(3 * rows, rows)], 0, right)
        to_left = remote(x_ref, o_ref.at[pl.ds(rows, rows)], 1, left)
        to_right.start()
        to_left.start()
        to_right.wait()
        to_left.wait()
        relay_right = remote(
            o_ref.at[pl.ds(3 * rows, half)], o_ref.at[pl.ds(2 * rows, half)], 2, right
        )
        relay_left = remote(
            o_ref.at[pl.ds(rows + half, half)], o_ref.at[pl.ds(2 * rows + half, half)], 3, left
        )
        relay_right.start()
        relay_left.start()
        relay_right.wait()
        relay_left.wait()
        own.wait()


def ring_gather(shard, stage, count, keep):
    rows, width = shard.shape
    return pl.pallas_call(
        functools.partial(ring_gather_kernel, stage, count),
        out_shape=jax.ShapeDtypeStruct((count * rows, width), shard.dtype),
        in_specs=[pl.BlockSpec(memory_space=pl.ANY), pl.BlockSpec(memory_space=pl.ANY)],
        out_specs=pl.BlockSpec(memory_space=pl.ANY),
        scratch_shapes=[
            pltpu.SemaphoreType.DMA((4,)),
            pltpu.SemaphoreType.DMA((4,)),
            pltpu.SemaphoreType.DMA(()),
        ],
        input_output_aliases={1: 0},
        compiler_params=pltpu.CompilerParams(collective_id=stage, has_side_effects=True),
    )(shard, keep)


def reduce_ring(partial, stage, count):
    rows = partial.shape[0] // count
    half = rows // 2
    blocks = [partial[k * rows : (k + 1) * rows] for k in range(count)]
    low = lambda value: value.astype(jnp.bfloat16)
    first_right = lax.ppermute(low(blocks[2][:half]), RING, shift_pairs(stage, count, 1))
    first_left = lax.ppermute(low(blocks[2][half:]), RING, shift_pairs(stage, count, -1))
    to_right = jnp.concatenate(
        [first_right.astype(jnp.float32) + blocks[1][:half], blocks[1][half:]], axis=0
    )
    to_left = jnp.concatenate(
        [blocks[3][:half], first_left.astype(jnp.float32) + blocks[3][half:]], axis=0
    )
    got_left = lax.ppermute(low(to_right), RING, shift_pairs(stage, count, 1))
    got_right = lax.ppermute(low(to_left), RING, shift_pairs(stage, count, -1))
    return blocks[0] + got_left.astype(jnp.float32) + got_right.astype(jnp.float32)


def swap(value):
    return lax.ppermute(value, "section", [(0, 1), (1, 0)])


def seq_pairs(count, step):
    return [(pos, (pos + step) % count) for pos in range(count)]


def reduce_seq(partial, count):
    rows = partial.shape[0] // count
    half = rows // 2
    blocks = [partial[k * rows : (k + 1) * rows] for k in range(count)]
    low = lambda value: value.astype(jnp.bfloat16)
    first_right = lax.ppermute(low(blocks[2][:half]), "seq", seq_pairs(count, 1))
    first_left = lax.ppermute(low(blocks[2][half:]), "seq", seq_pairs(count, -1))
    to_right = jnp.concatenate(
        [first_right.astype(jnp.float32) + blocks[1][:half], blocks[1][half:]], axis=0
    )
    to_left = jnp.concatenate(
        [blocks[3][:half], first_left.astype(jnp.float32) + blocks[3][half:]], axis=0
    )
    got_left = lax.ppermute(low(to_right), "seq", seq_pairs(count, 1))
    got_right = lax.ppermute(low(to_left), "seq", seq_pairs(count, -1))
    return blocks[0] + got_left.astype(jnp.float32) + got_right.astype(jnp.float32)


def body(section_input, saved_qkv, modulation, w_qkv, w_out, lengths, student_out, teacher_target):
    section_total = lax.axis_size("section")
    section_pos = lax.axis_index("section")
    seq_total = lax.axis_size("seq")
    seq_pos = lax.axis_index("seq")
    inputs = section_input[0, 0]
    saved_rows = saved_qkv[0, 0]
    weight_out = w_out[0]
    shard_rows, model_width = inputs.shape
    capacity = saved_rows.shape[0]
    local_width = saved_rows.shape[2]
    live_length = lengths[0]
    w_local = w_qkv[0]
    block_rows = w_local.shape[0]
    half_rows = block_rows // 2
    blocks_total = model_width // block_rows

    other_inputs = swap(inputs)
    other_mods = swap(modulation[0, 0])
    other_w = swap(w_local[half_rows:])
    parts = {}
    for stage in range(section_total):
        own = section_pos == stage
        x_stage = jnp.where(own, inputs, other_inputs)
        mods_stage = jnp.where(own, modulation[0, 0], other_mods)
        parts[stage] = (layer_norm_parts(x_stage), mods_stage)

    weights_of = {}
    for stage in reversed(range(section_total)):
        own = section_pos == stage
        contribution = jnp.where(own, w_local[:half_rows], other_w)
        weights_of[stage] = lax.all_gather(contribution, "dp", axis=0, tiled=True).reshape(
            blocks_total * half_rows, 3 * local_width
        )

    positions = seq_pos * shard_rows + jnp.arange(shard_rows, dtype=jnp.int32)
    row_live = positions < live_length
    gap = student_out[0].astype(jnp.float32) - teacher_target[0].astype(jnp.float32)
    loss_grad = jnp.where(row_live[:, None], gap, 0.0).astype(jnp.bfloat16)
    order = (seq_pos + jnp.arange(seq_total, dtype=jnp.int32)) % seq_total
    token_order = (order[:, None] * shard_rows + jnp.arange(shard_rows, dtype=jnp.int32)).reshape(-1)
    doubled = jnp.concatenate([saved_rows, saved_rows], axis=0)
    saved_off = lax.dynamic_slice_in_dim(doubled, seq_pos * shard_rows, capacity, axis=0)
    live_keys = token_order < live_length
    last = section_total - 1
    first_branch = (parts[last][1][1] * loss_grad.astype(jnp.float32)).astype(jnp.bfloat16)
    first_left = lax.ppermute(first_branch, RING, shift_pairs(last, seq_total, 1))
    first_right = lax.ppermute(first_branch, RING, shift_pairs(last, seq_total, -1))
    saved_off, first_left, first_right = lax.optimization_barrier(
        (saved_off, first_left, first_right)
    )
    fwd = attend_forward(saved_off, live_keys, HEAD_DIM)
    attn_mixed = fwd[2].reshape(capacity, local_width)
    attn_mixed_t = lax.optimization_barrier(attn_mixed.T)

    def pick_half(value, own):
        split = value.reshape(value.shape[0], blocks_total, block_rows)
        chosen = jnp.where(own, split[:, :, :half_rows], split[:, :, half_rows:])
        return chosen.reshape(value.shape[0], blocks_total * half_rows)

    def section_work(d_output, stage, keep):
        own = section_pos == stage
        (normed, inverse), mods_stage = parts[stage]
        scale_term = mods_stage[0]
        gate_term = mods_stage[1]
        d_branch = (gate_term * d_output.astype(jnp.float32)).astype(jnp.bfloat16)
        if stage == section_total - 1:
            half_block = shard_rows // 2
            far_top = lax.ppermute(first_left[:half_block], RING, shift_pairs(stage, seq_total, 1))
            far_bottom = lax.ppermute(
                first_right[half_block:], RING, shift_pairs(stage, seq_total, -1)
            )
            far = jnp.concatenate([far_top, far_bottom], axis=0)
            branch_full = jnp.concatenate([first_branch, first_right, far, first_left], axis=0)
        else:
            branch_full = ring_gather(d_branch, stage, seq_total, keep)
        d_attn = jnp.dot(branch_full, weight_out.T, preferred_element_type=jnp.float32).astype(
            jnp.bfloat16
        )
        own_grads = attend_backward(saved_off, fwd, d_attn, HEAD_DIM)
        handed = lax.ppermute(own_grads, "section", [(stage, 1 - stage)])
        flat_grads = jnp.where(own, own_grads, handed)
        d_mod_part = jnp.dot(flat_grads, weights_of[stage].T, preferred_element_type=jnp.float32)
        d_mod = reduce_seq(d_mod_part, seq_total)
        normed_half = pick_half(normed, own)
        d_norm = d_mod * (1.0 + pick_half(scale_term[None], own))
        sums = jnp.stack([jnp.sum(d_norm, axis=-1), jnp.sum(d_norm * normed_half, axis=-1)])
        sums = (sums + swap(sums)) / model_width
        d_layer = inverse * (d_norm - sums[0][:, None] - normed_half * sums[1][:, None])
        d_half = (pick_half(d_output, own).astype(jnp.float32) + d_layer).astype(
            jnp.bfloat16
        )
        other_half = swap(d_half)
        mine = d_half.reshape(shard_rows, blocks_total, half_rows)
        theirs = other_half.reshape(shard_rows, blocks_total, half_rows)
        joined = jnp.concatenate(
            [jnp.where(own, mine, theirs), jnp.where(own, theirs, mine)], axis=2
        )
        return joined.reshape(shard_rows, model_width), branch_full

    incoming = loss_grad
    grad_input = None
    branch_own = None
    for stage in reversed(range(section_total)):
        d_input, branch_full = section_work(incoming, stage, branch_own)
        here = section_pos == stage
        grad_input = d_input if grad_input is None else jnp.where(here, d_input, grad_input)
        branch_own = branch_full
        incoming = d_input
    out_local = jnp.dot(attn_mixed_t, branch_own, preferred_element_type=jnp.float32)
    out_slice = lax.psum_scatter(out_local, "dp", scatter_dimension=1, tiled=True)
    return (grad_input[None, None], out_slice.astype(jnp.bfloat16)[None])


def solution(mesh):
    in_specs = (
        P("section", "dp", "seq", None),
        P("section", "dp", None, None, "seq"),
        P("section", "dp", None, None),
        P("section", "dp", None, "seq"),
        P("section", "seq", None),
        P("dp"),
        P("dp", "seq", None),
        P("dp", "seq", None),
    )
    out_specs = (P("section", "dp", "seq", None), P("section", "seq", "dp"))
    return jax.shard_map(body, mesh=mesh, in_specs=in_specs, out_specs=out_specs, check_vma=False)
```
